32 devices in a mesh: ax: 8 (over z, x), rad: 4 (over y, core).
Axes of the slice: x: 2, y: 2, z: 4, core: 2. Of those that a mesh axis runs over, the one named last changes fastest.
Arguments:
- velocity: float32 [3, 12, 24, 768], P(None, 'rad', 'ax'), may hold values from -50 to 50
- cycle_map: int32 [3, 768], replicated, may hold values from 0 to 95, never falling along the last dimension, each value on 1 to 16 neighbouring positions
Outputs:
- new_velocity: float32 [3, 12, 24, 768], P(None, 'rad', 'ax')
The draws below stay inside these ranges and needn't reach their ends.
Inputs may be any that keep to these rules, and one draw needn't show every extreme that they name: `cycle_map`: in each row the numbers never fall along the azimuth, and each of 0 to 95 is taken by 1 to 16 consecutive points, one by exactly 16.
All inputs are finite; a program needn't handle non-finite values.
Results may differ from the reference program's by a relative error of at most 0.0003.
Values sent between devices are 32-bit elements; how exact they have to be, the bound alone decides.
A program may use at most 64 MiB of HBM per device.

```python
import math
import jax
import jax.numpy as jnp
import numpy as np
from jax import lax

TH = 768
Z_DEV = 3
NRING = 3
NC = 96
MOSTSEG = 16
NZ = 24
NR = 12
N_AX = 8


def box_along(values, axis, width):
    total = values
    for offset in range(1, width // 2 + 1):
        total = total + jnp.roll(values, offset, axis) + jnp.roll(values, -offset, axis)
    return total


def draw_velocity(key, part):
    subkeys = jax.random.split(key, 8)
    white_noise = jnp.clip(jax.random.normal(subkeys[0], (3, NR, NZ, TH), jnp.float32), -4.0, 4.0)
    other_noise = jnp.clip(jax.random.normal(subkeys[7], (3, NR, NZ, TH), jnp.float32), -4.0, 4.0)
    box_width = 5
    smooth_noise = box_along(box_along(other_noise, 2, box_width), 3, box_width) * (1.0 / box_width)
    block_of_row = jnp.arange(NZ, dtype=jnp.int32) * 8 // NZ
    block_order = jax.random.permutation(subkeys[4], 8).astype(jnp.float32)
    jitter = jax.random.uniform(subkeys[5], (8,), jnp.float32, 0.0, 1.0)
    white_share = 0.1 + 0.85 * (block_order + jitter) / 8.0
    block_gain = jnp.exp(jax.random.uniform(subkeys[6], (8,), jnp.float32, -1.0, 1.0) * 0.2)
    share_rows = white_share[block_of_row][None, None, :, None]
    rough_part = jnp.clip(jnp.sqrt(share_rows) * white_noise + jnp.sqrt(1.0 - share_rows) * smooth_noise, -3.0, 3.0)
    axial_pos = jnp.arange(NZ, dtype=jnp.float32) / NZ
    azimuth = jnp.arange(TH, dtype=jnp.float32) * (2.0 * math.pi / TH)
    radius = (jnp.arange(NR, dtype=jnp.float32) + 0.5) / NR
    phases = jax.random.uniform(subkeys[1], (3, 3), jnp.float32, 0.0, 2.0 * math.pi)
    smooth_part = 0.0
    for wave_number in range(3):
        smooth_part = smooth_part + jnp.sin(2.0 * math.pi * (wave_number + 1) * axial_pos[None, None, :, None] + (wave_number + 1) * azimuth[None, None, None, :] + 3.0 * radius[None, :, None, None] + phases[:, wave_number][:, None, None, None])
    row_scale = jnp.exp(jax.random.uniform(subkeys[2], (NZ,), jnp.float32, -1.0, 1.0) * (math.log(10.0) / 4.0))
    column_scale = jnp.exp(jax.random.uniform(subkeys[3], (TH,), jnp.float32, -1.0, 1.0) * (math.log(10.0) / 4.0))
    envelope = (1.0 + 2.0 * axial_pos) ** 0.25
    amplitude = (envelope * row_scale * block_gain[block_of_row])[None, None, :, None] * column_scale[None, None, None, :]
    mean_flow = 1.0 - radius * radius
    axial_mask = jnp.array([1.0, 0.0, 0.0], jnp.float32)
    mixed = rough_part + 2.0 * axial_pos[None, None, :, None] * smooth_part
    return amplitude * mixed + axial_mask[:, None, None, None] * mean_flow[None, :, None, None]


def profile(amount, total, limit, slope):
    loads = [(1 << 20) // math.isqrt(rank ** slope) + 1 for rank in range(2, amount + 1)]
    spare, given = total - limit - (amount - 1), [1] * (amount - 1)
    while spare > 0:
        free = [i for i in range(amount - 1) if given[i] < limit]
        pool, remaining = sum([loads[i] for i in free]), spare
        for i in free:
            more = min(limit - given[i], max(1, remaining * loads[i] // pool), spare)
            given[i] = given[i] + more
            spare = spare - more
    return np.array([limit] + given)


def uneven_parts(stream_key, number_of, total, most, lean):
    if number_of == 2:
        one = jax.random.randint(stream_key, (), max(1, total - most), min(most, total - 1) + 1)
        return jnp.stack([one, total - one])
    sizes = jnp.asarray(profile(number_of, total, most, lean), jnp.int32)
    twos = (number_of - 1) // 2
    donor, taker = sizes[1:1 + 2 * twos:2], sizes[2:2 + 2 * twos:2]
    slack = jnp.minimum(donor - 1, most - taker)
    moved = jax.random.randint(jax.random.fold_in(stream_key, 1), (twos,), 0, 1 << 20) % (slack + 1)
    sizes = sizes.at[1:1 + 2 * twos:2].set(donor - moved).at[2:2 + 2 * twos:2].set(taker + moved)
    return sizes[jax.random.permutation(jax.random.fold_in(stream_key, 2), number_of)]


def setup_inputs(seed: int = 0) -> dict:
    arg_keys = jax.random.split(jax.random.key(seed), 3)
    velocity = draw_velocity(jax.random.fold_in(arg_keys[2], 71), 0)
    cycle_map = jax.vmap(lambda own: jnp.searchsorted(jnp.cumsum(uneven_parts(own, NC, TH, MOSTSEG, 2)), jnp.arange(TH), side="right"))(jax.random.split(arg_keys[1], NRING)).reshape((NRING, TH)).astype(jnp.int32)
    return {"velocity": velocity, "cycle_map": cycle_map}


COMPONENT_PAIRS = ((0, 0), (1, 1), (2, 2), (0, 1), (0, 2), (1, 2))
PAIR_WEIGHTS = (1.0, 1.0, 1.0, 2.0, 2.0, 2.0)
VECTOR_SIGNS = (1.0, -1.0, -1.0)
TENSOR_SIGNS = (1.0, 1.0, 1.0, -1.0, -1.0, 1.0)
time_step = 1.0
epsilon = 1e-06

def pair_number(left_index, right_index):
    return COMPONENT_PAIRS.index((min(left_index, right_index), max(left_index, right_index)))

def trimmed(quantity, margin):
    if margin == 0:
        return quantity
    return quantity[margin:-margin, margin:-margin]

def central(quantity, direction):
    if direction == 0:
        return (quantity[1:-1, 2:] - quantity[1:-1, :-2]) * 0.5
    if direction == 1:
        return (quantity[2:, 1:-1] - quantity[:-2, 1:-1]) * 0.5
    shifted = (jnp.roll(quantity, -1, 2) - jnp.roll(quantity, 1, 2)) * 0.5
    return shifted[1:-1, 1:-1]

def test_filter(quantity):
    along_axis = (quantity[1:-1, :-2] + 2.0 * quantity[1:-1, 1:-1] + quantity[1:-1, 2:]) * 0.25
    return (jnp.roll(along_axis, 1, 2) + 2.0 * along_axis + jnp.roll(along_axis, -1, 2)) * 0.25

def strain_rate(velocity):
    gradient = [[central(velocity[component], direction) for direction in range(3)] for component in range(3)]
    tensor = [0.5 * (gradient[left_index][right_index] + gradient[right_index][left_index]) for left_index, right_index in COMPONENT_PAIRS]
    squares = sum((weight * member * member for weight, member in zip(PAIR_WEIGHTS, tensor)))
    return (tensor, jnp.sqrt(2.0 * squares))

def model_terms(velocity):
    tensor, magnitude = strain_rate(velocity)
    filtered = [test_filter(component) for component in velocity]
    tensor_hat, magnitude_hat = strain_rate(filtered)
    leonard_model = 0.0
    model_model = 0.0
    for number, (left_index, right_index) in enumerate(COMPONENT_PAIRS):
        product_hat = trimmed(test_filter(velocity[left_index] * velocity[right_index]), 1)
        leonard = product_hat - trimmed(filtered[left_index], 1) * trimmed(filtered[right_index], 1)
        model_term = test_filter(magnitude * tensor[number]) - 4.0 * magnitude_hat * tensor_hat[number]
        leonard_model = leonard_model + PAIR_WEIGHTS[number] * leonard * model_term
        model_model = model_model + PAIR_WEIGHTS[number] * model_term * model_term
    return (leonard_model, model_model, tensor, magnitude)

def flux_terms(velocity, tensor, magnitude, coefficient, margin_in, margin_out):
    speed_trim = margin_in - margin_out
    stress_trim = margin_in - 1 - margin_out
    viscosity = 2.0 * coefficient[:, None, None] * trimmed(magnitude, stress_trim)
    fluxes = []
    for number, (left_index, right_index) in enumerate(COMPONENT_PAIRS):
        advected = trimmed(velocity[left_index], speed_trim) * trimmed(velocity[right_index], speed_trim)
        fluxes.append(advected - viscosity * trimmed(tensor[number], stress_trim))
    return jnp.stack(fluxes)

def divergence(fluxes):
    tendencies = []
    for component in range(3):
        summed = 0.0
        for direction in range(3):
            summed = summed + central(fluxes[pair_number(component, direction)], direction)
        tendencies.append(-summed)
    return tendencies

def radial_rims(extended, rim_depth, rad_index, rad_count, sign_values):
    sign_column = jnp.asarray(sign_values, extended.dtype)[:, None, None, None]
    half_turn = extended.shape[3] // 2
    mirrored = sign_column * jnp.roll(extended[:, rim_depth:2 * rim_depth][:, ::-1], half_turn, 3)
    inner_rows = jnp.where(rad_index == 0, mirrored, extended[:, :rim_depth])
    outer_rows = jnp.where(rad_index == rad_count - 1, 0.0, extended[:, -rim_depth:])
    return jnp.concatenate([inner_rows, extended[:, rim_depth:-rim_depth], outer_rows], axis=1)

def coarsen_cycles(velocity, cycle_map):
    labels = jnp.arange(NC, dtype=jnp.int32)
    theta_points = velocity.shape[3]
    cycle_list = []
    for cycle_number in range(NRING):
        one_hot = (cycle_map[cycle_number][:, None] == labels[None, :]).astype(jnp.float32)
        cell_count = lax.optimization_barrier(jnp.sum(one_hot, axis=0))
        cycle_rows = velocity[:, cycle_number].reshape(-1, theta_points)
        cycle_sums = jnp.dot(cycle_rows, one_hot, precision=lax.Precision.HIGHEST, preferred_element_type=jnp.float32)
        cycle_means = cycle_sums / cell_count
        spread = jnp.dot(cycle_means, one_hot.T, precision=lax.Precision.HIGHEST, preferred_element_type=jnp.float32)
        cycle_list.append(spread.reshape(velocity[:, cycle_number].shape))
    return jnp.concatenate([jnp.stack(cycle_list, axis=1), velocity[:, NRING:]], axis=1)

def reference(velocity, cycle_map):
    coarse = coarsen_cycles(velocity, cycle_map)
    extended = radial_rims(jnp.pad(coarse, ((0, 0), (3, 3), (0, 0), (0, 0))), 3, 0, 1, VECTOR_SIGNS)
    total_z = extended.shape[2]

    def block_velocity(block):
        rows_z = (block * Z_DEV - 3 + jnp.arange(Z_DEV + 6, dtype=jnp.int32)) % total_z
        taken = jnp.take(extended, rows_z, axis=2)
        return [taken[0], taken[1], taken[2]]

    def coefficient_block(block):
        leonard_model, model_model, tensor, magnitude = model_terms(block_velocity(block))
        return (lax.optimization_barrier(jnp.sum(trimmed(leonard_model, 1), axis=(1, 2))), lax.optimization_barrier(jnp.sum(trimmed(model_model, 1), axis=(1, 2))))
    blocks = jnp.arange(N_AX, dtype=jnp.int32)
    lm_parts, mm_parts = lax.map(coefficient_block, blocks)
    cell_count = NZ * TH
    coefficient = lax.optimization_barrier(jnp.sum(lm_parts, axis=0)) / cell_count / (lax.optimization_barrier(jnp.sum(mm_parts, axis=0)) / cell_count + epsilon)
    coefficient_rows = jnp.pad(coefficient, 1)

    def update_block(block):
        components = block_velocity(block)
        tensor, magnitude = strain_rate(components)
        fluxes = flux_terms(components, tensor, magnitude, coefficient_rows, 3, 1)
        fluxes = radial_rims(fluxes, 1, 0, 1, TENSOR_SIGNS)
        tendencies = divergence(fluxes)
        return jnp.stack([trimmed(components[component], 3) + time_step * tendencies[component] for component in range(3)])
    result = lax.map(update_block, blocks)
    return jnp.transpose(result, (1, 2, 0, 3, 4)).reshape(3, NR, NZ, TH)
```

```python
import functools

import jax
import jax.numpy as jnp
from jax import lax
from jax.experimental import pallas as pl
from jax.experimental.pallas import tpu as pltpu
from jax.sharding import PartitionSpec as P

NRING = 3
MOSTSEG = 16
SUB = 8
LANES = 128
PAIRS = ((0, 0), (1, 1), (2, 2), (0, 1), (0, 2), (1, 2))
PAIR_WEIGHTS = (1.0, 1.0, 1.0, 2.0, 2.0, 2.0)
SIGNS = (1.0, -1.0, -1.0)
EPSILON = 1e-06
MESH = pl.DeviceIdType.MESH
IN, SEND, HALO, EDGE, SUMS, SEMS = 0, 2, 5, 9, 11, 14


def pair(a, b):
    return PAIRS.index((min(a, b), max(a, b)))


def each(count, body):
    if count <= 16:
        for i in range(count):
            body(i)
    else:
        lax.fori_loop(0, count, lambda i, c: (body(i), c)[1], 0)


def roll(x, shift, axis):
    size = x.shape[axis]
    return pltpu.roll(x, shift % size, axis)


def up(x):
    return roll(x, -1, x.ndim - 1)


def down(x):
    return roll(x, 1, x.ndim - 1)


def smooth_t(x):
    return (down(x) + 2.0 * x + up(x)) * 0.25


def smooth_z(x):
    return (x[:, :-2] + 2.0 * x[:, 1:-1] + x[:, 2:]) * 0.25


def tiles_of(x):
    return [x[:, k : k + LANES] for k in range(0, x.shape[1], LANES)]


def segments(x, wide, pad):
    rows, tiles = x[0].shape[0], len(x)
    total = tiles * LANES
    lane = lax.broadcasted_iota(jnp.int32, (rows, LANES), 1)
    pieces = []
    for s in range(SUB):
        start = (s * wide - pad) % total
        k, off = start // LANES, start % LANES
        first = x[k]
        if off:
            k2 = (k + 1) % tiles
            second = x[k2]
            first = jnp.where(lane < LANES - off, roll(first, -off, 1), roll(second, -off, 1))
        pieces.append(first)
    return pieces


def joined(pieces, wide, pad):
    rows = pieces[0].shape[0]
    lane = lax.broadcasted_iota(jnp.int32, (rows, LANES), 1)
    tiles = []
    for k in range(SUB * wide // LANES):
        lo, hi = k * LANES, (k + 1) * LANES
        s = lo // wide
        out = None
        while s * wide < hi:
            part = roll(pieces[s], s * wide - pad - lo, 1)
            out = part if out is None else jnp.where(lane >= s * wide - lo, part, out)
            s += 1
        tiles.append(out)
    return tiles


def strain(grads):
    tensor = []
    for c, a in PAIRS:
        if c == a:
            tensor.append(0.5 * grads[c][c])
        else:
            tensor.append(0.25 * (grads[c][a] + grads[a][c]))
    squares = sum(w * m * m for w, m in zip(PAIR_WEIGHTS, tensor))
    return tensor, jnp.sqrt(2.0 * squares)


def gradients(f):
    out = []
    for c in range(3):
        mid = f[c][1:-1, 1:-1]
        out.append(
            [
                f[c][1:-1, 2:] - f[c][1:-1, :-2],
                f[c][2:, 1:-1] - f[c][:-2, 1:-1],
                up(mid) - down(mid),
            ]
        )
    return out


def stages(n_ax):
    distances, reach = [], 2
    while reach < n_ax // 2:
        distances.append(reach)
        reach *= 2
    return distances


def offsets(n_ax):
    return sorted({o % n_ax for o in (0, 1, 2, -1, -2)})


def kernel(n_ax, n_rad, v_hbm, map_hbm, out_ref, nat, map_ref, own, maps, ext, hx, part, parts, edge_coef,
           z_out, z_in, z_seg, ready, sems):
    rad = lax.axis_index("rad")
    ax = lax.axis_index("ax")
    R, Z, T = nat.shape[1], nat.shape[2], nat.shape[3]
    wide = T // SUB
    pad = (LANES - wide) // 2
    half = SUB // 2
    right, left = lax.rem(ax + 1, n_ax), lax.rem(ax + n_ax - 1, n_ax)
    has_lo, has_hi = rad > 0, rad < n_rad - 1

    def strips(c, r):
        return [own[pl.ds((c * R + r) * Z * SUB + s, Z, stride=SUB), :] for s in range(SUB)]

    barrier = pltpu.get_barrier_semaphore()

    def greet(to_ax, to_rad):
        pl.semaphore_signal(barrier, inc=1, device_id=(to_ax, to_rad), device_id_type=MESH)

    reach = offsets(n_ax)

    def greet_row(to_rad):
        for o in reach:
            greet(lax.rem(ax + o, n_ax), to_rad)

    for o in reach[1:]:
        greet(lax.rem(ax + o, n_ax), rad)
    pl.when(has_lo)(lambda: greet_row(rad - 1))
    pl.when(has_hi)(lambda: greet_row(rad + 1))

    distances = stages(n_ax)

    def tell(stage):
        d = distances[stage]
        for peer in (lax.rem(ax + d, n_ax), lax.rem(ax + n_ax - d, n_ax)):
            pl.semaphore_signal(ready.at[stage], inc=1, device_id=(peer, rad), device_id_type=MESH)

    def hear(stage):
        pl.semaphore_wait(ready.at[stage], 2)

    fetch = pltpu.make_async_copy(v_hbm, nat, sems.at[IN])
    fetch.start()
    fetch_map = pltpu.make_async_copy(map_hbm, map_ref, sems.at[IN + 1])
    pl.when(rad == 0)(lambda: fetch_map.start())
    fetch.wait()
    for c in range(3):
        for r in range(R):
            for s, piece in enumerate(segments(tiles_of(nat[c, r]), wide, pad)):
                own[pl.ds((c * R + r) * Z * SUB + s, Z, stride=SUB), :] = piece
    for c in range(3):
        for r in range(R):
            for z in range(Z):
                row = ((c * R + r) * Z + z) * SUB
                ext[c, r + 1, z + 2] = own[row : row + SUB, :]

    lane = lax.broadcasted_iota(jnp.int32, (SUB, LANES), 1)
    steps = []
    while 2 ** len(steps) < MOSTSEG:
        steps.append(2 ** len(steps))

    def cell_sums(r):
        label = maps[r * SUB : (r + 1) * SUB, :]
        before = [(roll(label, d, 1) == label).astype(jnp.float32) for d in steps]
        after = [(roll(label, -d, 1) == label).astype(jnp.float32) for d in steps]

        def spread(x):
            total, rest = x, x
            for d, b, a in zip(steps, before, after):
                total = total + b * roll(total, d, 1)
                rest = rest + a * roll(rest, -d, 1)
            return total + rest - x

        return spread

    def coarsen(r, spread, c, z):
        mean = spread(ext[c, r + 1, z]) * maps[(NRING + r) * SUB : (NRING + r + 1) * SUB, :]
        low = roll(roll(mean, -wide, 1), 1, 0)
        high = roll(roll(mean, wide, 1), -1, 0)
        mean = jnp.where(lane < pad, low, mean)
        ext[c, r + 1, z] = jnp.where(lane >= pad + wide, high, mean)

    @pl.when(rad == 0)
    def _():
        fetch_map.wait()
        labels = map_ref[...].astype(jnp.float32)
        for s, piece in enumerate(segments(tiles_of(labels), wide, pad)):
            maps[pl.ds(s, NRING, stride=SUB), :] = piece
        for r in range(NRING):
            spread = cell_sums(r)
            maps[(NRING + r) * SUB : (NRING + r + 1) * SUB, :] = 1.0 / spread(jnp.ones((SUB, LANES), jnp.float32))
            for c in range(3):
                for z in range(Z):
                    coarsen(r, spread, c, z + 2)
                    row = ((c * R + r) * Z + z) * SUB
                    own[row : row + SUB, :] = ext[c, r + 1, z + 2]
                for k, tile in enumerate(joined(strips(c, r), wide, pad)):
                    nat[c, r, :, k * LANES : (k + 1) * LANES] = tile

    n_rows = 3 * R * 2
    for side, first in ((0, Z - 2), (1, 0)):
        for c in range(3):
            for r in range(R):
                for k in range(T // LANES):
                    row = k * n_rows + (c * R + r) * 2
                    z_out[side, row : row + 2, :] = nat[c, r, first : first + 2, k * LANES : (k + 1) * LANES]

    pl.semaphore_wait(barrier, len(reach) * (1 + jnp.where(has_lo, 1, 0) + jnp.where(has_hi, 1, 0)) - 1)

    def z_halo(slot, to_ax):
        return pltpu.make_async_remote_copy(
            src_ref=z_out.at[slot], dst_ref=z_in.at[slot], send_sem=sems.at[SEND],
            recv_sem=sems.at[HALO + slot], device_id=(to_ax, rad), device_id_type=MESH)

    z_lo, z_hi = z_halo(0, right), z_halo(1, left)
    z_lo.start()
    z_hi.start()
    if distances:
        tell(0)

    rows, cols = pl.ds(1, R), pl.ds(2, Z)

    def halo(side, src, dst, to_ax, to_rad):
        return pltpu.make_async_remote_copy(
            src_ref=ext.at[src], dst_ref=ext.at[dst], send_sem=sems.at[SEND + 1 + side],
            recv_sem=sems.at[HALO + 2 + side], device_id=(to_ax, to_rad), device_id_type=MESH)

    def drain(sem, amount):
        pltpu.make_async_copy(z_seg.at[pl.ds(0, amount)], z_seg.at[pl.ds(0, amount)], sems.at[sem]).wait()

    everything = slice(None)

    out_going = [
        halo(0, (everything, R, cols), (everything, 0, cols), ax, rad + 1),
        halo(0, (everything, R, Z + 1), (everything, 0, 1), right, rad + 1),
        halo(0, (everything, R, 2), (everything, 0, Z + 2), left, rad + 1),
    ]
    in_going = [
        halo(1, (everything, 1, cols), (everything, R + 1, cols), ax, rad - 1),
        halo(1, (everything, 1, Z + 1), (everything, R + 1, 1), right, rad - 1),
        halo(1, (everything, 1, 2), (everything, R + 1, Z + 2), left, rad - 1),
    ]

    def start_all(copies):
        for copy in copies:
            copy.start()

    rim = 3 * (Z + 2) * SUB

    pl.when(has_hi)(lambda: start_all(out_going))
    pl.when(has_lo)(lambda: start_all(in_going))
    for side, copy, first in ((0, z_lo, 0), (1, z_hi, Z + 2)):
        copy.wait_recv()
        tiles = [z_in[side, k * n_rows : (k + 1) * n_rows, :] for k in range(T // LANES)]
        for s, piece in enumerate(segments(tiles, wide, pad)):
            z_seg[pl.ds(side * n_rows * SUB + s, n_rows, stride=SUB), :] = piece
        for c in range(3):
            for r in range(R):
                for z in range(2):
                    row = (side * n_rows + (c * R + r) * 2 + z) * SUB
                    ext[c, r + 1, first + z] = z_seg[row : row + SUB, :]

    long = [ext[c, 1 : R + 1, 0 : Z + 4] for c in range(3)]
    mids = [x[:, 1:-1] for x in long]
    grads, w_own, w_grads, leonards = [], [], [], []
    for c in range(3):
        turned = up(mids[c]) - down(mids[c])
        grads.append([long[c][:, 2:] - long[c][:, :-2], None, turned])
        w_own.append(smooth_t(smooth_z(long[c])))
        mid = w_own[c][:, 1:-1]
        w_grads.append([w_own[c][:, 2:] - w_own[c][:, :-2], None, up(mid) - down(mid)])
    for c, a in PAIRS:
        product = smooth_t(smooth_z(mids[c] * mids[a]))
        leonards.append(product - w_own[c][:, 1:-1] * w_own[a][:, 1:-1])

    pl.when(has_lo)(lambda: drain(HALO + 2, rim))
    pl.when(has_hi)(lambda: drain(HALO + 3, rim))

    @pl.when(rad == 0)
    def _():
        for c in range(3):
            for z in range(1, Z + 3):
                ext[c, 0, z] = SIGNS[c] * roll(ext[c, 1, z], half, 0)

    @pl.when(rad == n_rad - 1)
    def _():
        for c in range(3):
            for z in range(1, Z + 3):
                ext[c, R + 1, z] = jnp.zeros((SUB, LANES), jnp.float32)

    below = [ext[c, 0:1, 1 : Z + 3] for c in range(3)]
    above = [ext[c, R + 1 : R + 2, 1 : Z + 3] for c in range(3)]
    for c in range(3):
        column = jnp.concatenate([below[c], mids[c], above[c]], axis=0)
        grads[c][1] = column[2:] - column[:-2]
        column = jnp.concatenate(
            [smooth_t(smooth_z(below[c])), w_own[c][:, 1:-1], smooth_t(smooth_z(above[c]))], axis=0)
        w_grads[c][1] = column[2:] - column[:-2]
    tensor, mag = strain(grads)
    stress = [mag * t for t in tensor]
    w_tensor, w_mag = strain(w_grads)
    w_mag4 = 4.0 * w_mag
    lm, mm = 0.0, 0.0
    for number, leonard in enumerate(leonards):
        model = smooth_t(smooth_z(stress[number])) - w_mag4 * w_tensor[number]
        lm = lm + PAIR_WEIGHTS[number] * leonard * model
        mm = mm + PAIR_WEIGHTS[number] * model * model
    sub_index = lax.broadcasted_iota(jnp.int32, (SUB, LANES), 0)
    lane_index = lax.broadcasted_iota(jnp.int32, (SUB, LANES), 1)
    mine = jnp.zeros((SUB, LANES), jnp.float32)
    for r in range(R):
        for base, quantity in ((0, lm), (half, mm)):
            row = jnp.sum(jnp.sum(quantity[r], axis=0), axis=0, keepdims=True)
            mine = jnp.where(sub_index == base + r, row, mine)
    mine = jnp.where((lane_index >= pad) & (lane_index < pad + wide), mine, 0.0)
    fold = LANES // 2
    while fold >= LANES // SUB:
        mine = mine + roll(mine, fold, 1)
        fold //= 2
    group = lane_index // (LANES // SUB) == sub_index
    part[...] = jnp.sum(jnp.where(group, mine, 0.0), axis=0, keepdims=True)

    def sums(side, i):
        peer = lax.rem(ax + i, n_ax)
        return pltpu.make_async_remote_copy(
            src_ref=part, dst_ref=parts.at[(1 - side) * n_ax + ax],
            send_sem=sems.at[SEND + (0, 1, 2)[side]], recv_sem=sems.at[SUMS + 1 - side],
            device_id=(peer, rad + side), device_id_type=MESH)

    def sums_in(side, amount):
        pltpu.make_async_copy(parts.at[pl.ds(0, amount)], parts.at[pl.ds(0, amount)], sems.at[SUMS + 1 + side]).wait()

    def first_of(side):
        return 1 if side == 0 else 0

    def send_sums(side):
        first = first_of(side)
        each(n_ax - first, lambda i: sums(side, i + first).start())

    for stage in range(len(distances)):
        hear(stage)
        if stage + 1 < len(distances):
            tell(stage + 1)
    send_sums(0)
    pl.when(has_lo)(lambda: send_sums(-1))
    pl.when(has_hi)(lambda: send_sums(1))

    for c in range(3):
        hx[c, 1 : R + 1] = stress[pair(c, 1)][:, 1:-1]

    def edge(slot, src, dst, to_rad):
        return pltpu.make_async_remote_copy(
            src_ref=hx.at[:, src], dst_ref=hx.at[:, dst], send_sem=sems.at[SEND + 1 + slot],
            recv_sem=sems.at[EDGE + slot], device_id=(ax, to_rad), device_id_type=MESH)

    edge_out = edge(0, R, 0, rad + 1)
    edge_in = edge(1, 1, R + 1, rad - 1)
    pl.when(has_hi)(lambda: edge_out.start())
    pl.when(has_lo)(lambda: edge_in.start())

    @pl.when(rad == 0)
    def _():
        for c in range(3):
            for z in range(Z):
                hx[c, 0, z] = SIGNS[c] * SIGNS[1] * roll(hx[c, 1, z], half, 0)

    @pl.when(rad == n_rad - 1)
    def _():
        for c in range(3):
            for z in range(Z):
                hx[c, R + 1, z] = jnp.zeros((SUB, LANES), jnp.float32)

    bases, turns = [], []
    whole = [jnp.concatenate([below[c], mids[c], above[c]], axis=0)[:, 1:-1] for c in range(3)]
    for c in range(3):
        axial = mids[c] * mids[0]
        radial = whole[c] * whole[1]
        around = whole[c][1:-1] * whole[2][1:-1]
        change = axial[:, 2:] - axial[:, :-2] + (radial[2:] - radial[:-2]) + (up(around) - down(around))
        bases.append(whole[c][1:-1] - 0.5 * change)
        along = stress[pair(c, 0)]
        turn = stress[pair(c, 2)][:, 1:-1]
        turns.append(along[:, 2:] - along[:, :-2] + (up(turn) - down(turn)))

    count = n_ax * Z * T
    sums_in(0, n_ax - 1)

    def coefficients(total):
        total = jnp.broadcast_to(jnp.sum(jnp.where(group, total, 0.0), axis=1, keepdims=True), (SUB, LANES)) / count
        return total / (roll(total, -half, 0) + EPSILON)

    def total_of(side):
        first = first_of(side)
        total = part[...] if first else jnp.zeros((1, LANES), jnp.float32)
        if n_ax <= 16:
            for i in range(first, n_ax):
                total = total + parts[(1 + side) * n_ax + lax.rem(ax + i, n_ax)]
            return total
        return lax.fori_loop(
            first, n_ax, lambda i, t: t + parts[(1 + side) * n_ax + lax.rem(ax + i, n_ax)], total)

    coef = coefficients(total_of(0))

    def beside(side, row):
        sums_in(side, n_ax)
        edge_coef[0 if side < 0 else 1] = jnp.broadcast_to(
            coefficients(total_of(side))[row : row + 1], (SUB, LANES))

    pl.when(has_lo)(lambda: beside(-1, R - 1))
    pl.when(has_hi)(lambda: beside(1, 0))

    @pl.when(rad == 0)
    def _():
        edge_coef[0] = jnp.broadcast_to(coef[0:1], (SUB, LANES))

    @pl.when(rad == n_rad - 1)
    def _():
        edge_coef[1] = jnp.zeros((SUB, LANES), jnp.float32)

    pl.when(has_lo)(lambda: edge_out.wait_recv())
    pl.when(has_hi)(lambda: edge_in.wait_recv())
    by_row = [edge_coef[0]] + [jnp.broadcast_to(coef[r : r + 1], (SUB, LANES)) for r in range(R)] + [edge_coef[1]]
    for c in range(3):
        for r in range(R):
            new = bases[c][r] + by_row[r + 1] * turns[c][r]
            new = new + (by_row[r + 2] * hx[c, r + 2] - by_row[r] * hx[c, r])
            for z in range(Z):
                row = ((c * R + r) * Z + z) * SUB
                own[row : row + SUB, :] = new[z]
    for c in range(3):
        for r in range(R):
            for k, tile in enumerate(joined(strips(c, r), wide, pad)):
                out_ref[c, r, :, k * LANES : (k + 1) * LANES] = tile

    drain(SEND, 2 * n_rows * T // LANES + n_ax - 1)
    beyond = rim + 3 * Z * SUB + n_ax
    pl.when(has_hi)(lambda: drain(SEND + 1, beyond))
    pl.when(has_lo)(lambda: drain(SEND + 2, beyond))


def shards(n_ax, n_rad, velocity, cycle_map):
    _, R, Z, T = velocity.shape
    return pl.pallas_call(
        functools.partial(kernel, n_ax, n_rad),
        out_shape=jax.ShapeDtypeStruct(velocity.shape, velocity.dtype),
        in_specs=[pl.BlockSpec(memory_space=pltpu.HBM)] * 2,
        out_specs=pl.BlockSpec(memory_space=pltpu.VMEM),
        scratch_shapes=[
            pltpu.VMEM(velocity.shape, jnp.float32),
            pltpu.VMEM(cycle_map.shape, jnp.int32),
            pltpu.VMEM((3 * R * Z * SUB, LANES), jnp.float32),
            pltpu.VMEM((2 * NRING * SUB, LANES), jnp.float32),
            pltpu.VMEM((3, R + 2, Z + 4, SUB, LANES), jnp.float32),
            pltpu.VMEM((3, R + 2, Z, SUB, LANES), jnp.float32),
            pltpu.VMEM((1, LANES), jnp.float32),
            pltpu.VMEM((3 * n_ax, 1, LANES), jnp.float32),
            pltpu.VMEM((2, SUB, LANES), jnp.float32),
            pltpu.VMEM((2, 3 * R * 2 * T // LANES, LANES), jnp.float32),
            pltpu.VMEM((2, 3 * R * 2 * T // LANES, LANES), jnp.float32),
            pltpu.VMEM((2 * 3 * R * 2 * SUB + 3 * (Z + 2) * SUB + 2 * n_ax, LANES), jnp.float32),
            pltpu.SemaphoreType.REGULAR((max(1, len(stages(n_ax))),)),
            pltpu.SemaphoreType.DMA((SEMS,)),
        ],
        compiler_params=pltpu.CompilerParams(collective_id=0, has_side_effects=True, vmem_limit_bytes=8 << 20),
    )(*(pltpu.with_memory_space_constraint(x, pltpu.HBM) for x in (velocity, cycle_map)))


def solution(mesh):
    n_ax, n_rad = mesh.shape["ax"], mesh.shape["rad"]
    spec = P(None, "rad", "ax", None)
    body = functools.partial(shards, n_ax, n_rad)
    return jax.shard_map(body, mesh=mesh, in_specs=(spec, P()), out_specs=spec, check_vma=False)
```

```python
import functools

import jax
import jax.numpy as jnp
from jax import lax
from jax.experimental import pallas as pl
from jax.experimental.pallas import tpu as pltpu
from jax.sharding import PartitionSpec as P

NRING = 3
MOSTSEG = 16
SUB = 8
LANES = 128
PAIRS = ((0, 0), (1, 1), (2, 2), (0, 1), (0, 2), (1, 2))
SIGNS = (1.0, -1.0, -1.0)
EPSILON = 1e-06
MESH = pl.DeviceIdType.MESH
IN, SEND, ZL, ZR, ROW, LATE, EDGE, SUMS, SEMS = 0, 2, 5, 6, 7, 9, 12, 14, 17


def pair(a, b):
    return PAIRS.index((min(a, b), max(a, b)))


def each(count, body):
    if count <= 16:
        for i in range(count):
            body(i)
    else:
        lax.fori_loop(0, count, lambda i, c: (body(i), c)[1], 0)


def roll(x, shift, axis):
    size = x.shape[axis]
    return pltpu.roll(x, shift % size, axis)


def up(x):
    return roll(x, -1, x.ndim - 1)


def down(x):
    return roll(x, 1, x.ndim - 1)


def smooth_t(x):
    return (down(x) + up(x)) + (x + x)


def smooth_z(x):
    y = x[:-1] + x[1:]
    return y[:-1] + y[1:]


def tiles_of(x):
    return [x[:, k : k + LANES] for k in range(0, x.shape[1], LANES)]


def segments(x, wide, pad):
    rows, tiles = x[0].shape[0], len(x)
    total = tiles * LANES
    lane = lax.broadcasted_iota(jnp.int32, (rows, LANES), 1)
    pieces = []
    for s in range(SUB):
        start = (s * wide - pad) % total
        k, off = start // LANES, start % LANES
        first = x[k]
        if off:
            k2 = (k + 1) % tiles
            second = x[k2]
            first = jnp.where(lane < LANES - off, roll(first, -off, 1), roll(second, -off, 1))
        pieces.append(first)
    return pieces


def joined(pieces, wide, pad):
    rows = pieces[0].shape[0]
    lane = lax.broadcasted_iota(jnp.int32, (rows, LANES), 1)
    tiles = []
    for k in range(SUB * wide // LANES):
        lo, hi = k * LANES, (k + 1) * LANES
        s = lo // wide
        out = None
        while s * wide < hi:
            part = roll(pieces[s], s * wide - pad - lo, 1)
            out = part if out is None else jnp.where(lane >= s * wide - lo, part, out)
            s += 1
        tiles.append(out)
    return tiles


def tensor(grads):
    terms = [grads[c][c] + grads[c][c] if c == a else grads[c][a] + grads[a][c] for c, a in PAIRS]
    squares = [x * x for x in terms]
    total = 0.5 * (squares[0] + squares[1] + squares[2]) + (squares[3] + squares[4] + squares[5])
    return terms, jnp.sqrt(total)


def stages(n_ax):
    distances, reach = [], 2
    while reach < n_ax // 2:
        distances.append(reach)
        reach *= 2
    return distances


def kernel(n_ax, n_rad, v_hbm, map_hbm, out_ref, nat, map_ref, maps, masks, ext, hz, hw, hf, hr, hq, hl, hc, wsc,
           flux, hx, res, acc, part, parts, edge_coef, spare, ready, sems):
    rad = lax.axis_index("rad")
    ax = lax.axis_index("ax")
    R, Z, T = nat.shape[1], nat.shape[2], nat.shape[3]
    K = T // LANES
    wide = T // SUB
    pad = (LANES - wide) // 2
    half = SUB // 2
    near, far = hw.shape[2], 2 - hw.shape[2]
    right, left = lax.rem(ax + 1, n_ax), lax.rem(ax + n_ax - 1, n_ax)
    has_lo, has_hi = rad > 0, rad < n_rad - 1
    first, last, second = ax == 0, ax == n_ax - 1, ax == n_ax - 2

    barrier = pltpu.get_barrier_semaphore()

    def greet(offset, to_rad):
        peer = (lax.rem(ax + offset + n_ax, n_ax), to_rad)
        pl.semaphore_signal(barrier, inc=1, device_id=peer, device_id_type=MESH)

    def greet_row(to_rad, offsets):
        for o in offsets:
            greet(o, to_rad)

    def greet_all(offsets, beside):
        greet_row(rad, offsets)
        pl.when(has_lo)(lambda: greet_row(rad - 1, offsets + beside))
        pl.when(has_hi)(lambda: greet_row(rad + 1, offsets + beside))

    greet_all((-1, -2), (0,))
    pl.when(ax + 1 < n_ax)(lambda: greet_all((1,), ()))
    pl.when(ax + 2 < n_ax)(lambda: greet_all((2,), ()))

    fetch = pltpu.make_async_copy(v_hbm, nat, sems.at[IN])
    fetch.start()
    fetch_map = pltpu.make_async_copy(map_hbm, map_ref, sems.at[IN + 1])
    fetch_map.start()

    distances = stages(n_ax)

    def tell(stage):
        d = distances[stage]
        for peer in (lax.rem(ax + d, n_ax), lax.rem(ax + n_ax - d, n_ax)):
            pl.semaphore_signal(ready.at[stage], inc=1, device_id=(peer, rad), device_id_type=MESH)

    def hear(stage):
        pl.semaphore_wait(ready.at[stage], 2)

    def drain(sem, amount):
        pltpu.make_async_copy(spare.at[pl.ds(0, amount)], spare.at[pl.ds(0, amount)], sems.at[sem]).wait()

    def send(src, dst, group, recv, to_ax, to_rad):
        pltpu.make_async_remote_copy(
            src_ref=src, dst_ref=dst, send_sem=sems.at[SEND + group], recv_sem=sems.at[recv],
            device_id=(to_ax, to_rad), device_id_type=MESH).start()

    beside_sum = jnp.where(has_lo, 1, 0) + jnp.where(has_hi, 1, 0)
    row_sum = 4 - jnp.where(first, 2, 0) - jnp.where(ax == 1, 1, 0)
    pl.semaphore_wait(barrier, row_sum * (1 + beside_sum) + beside_sum)

    send(v_hbm.at[:, :, pl.ds(Z - 2, 2)], hz.at[0], 0, ZL, right, rad)

    @pl.when(last)
    def _():
        send(v_hbm.at[:, :, pl.ds(Z - 2 - near, near)], hw, 0, ZL, right, rad)

    if far:
        @pl.when(second)
        def _():
            send(v_hbm.at[:, :, pl.ds(Z - far, far)], hf, 0, ZL, lax.rem(ax + 2, n_ax), rad)

    @pl.when(ax > 0)
    def _():
        send(v_hbm.at[:, :, pl.ds(0, 2)], hz.at[1], 0, ZR, left, rad)

    def rim(side, group, row, to_rad):
        send(v_hbm.at[:, row, pl.ds(Z - 1, 1)], hr.at[side, :, pl.ds(0, 1)], group, ROW + side, right, to_rad)

        @pl.when(last)
        def _():
            send(v_hbm.at[:, row, pl.ds(Z - 3, 2)], hq.at[side], group, ROW + side, right, to_rad)

        @pl.when(ax > 0)
        def _():
            send(v_hbm.at[:, row, pl.ds(0, 1)], hr.at[side, :, pl.ds(Z + 1, 1)], group, ROW + side, left, to_rad)

        send(v_hbm.at[:, row], hr.at[side, :, pl.ds(1, Z)], group, ROW + side, ax, to_rad)

    pl.when(has_hi)(lambda: rim(0, 1, R - 1, rad + 1))
    pl.when(has_lo)(lambda: rim(1, 2, 0, rad - 1))
    pl.when(ax > 1)(lambda: tell(0))

    def row_of(b, c, r, i):
        return (((b * 3 + c) * (R + 2) + r) * (Z + 4) + i) * SUB

    def get(b, c, r, i, n):
        row = row_of(b, c, r, i)
        return ext[row : row + n * SUB, :].reshape(n, SUB, LANES)

    def put(b, c, r, i, x):
        row = row_of(b, c, r, i)
        ext[row : row + SUB, :] = x

    def unpack(x, b, c, r, i):
        for s, piece in enumerate(segments(tiles_of(x), wide, pad)):
            ext[pl.ds(row_of(b, c, r, i) + s, x.shape[0], stride=SUB), :] = piece

    lane = lax.broadcasted_iota(jnp.int32, (SUB, LANES), 1)
    steps = []
    while 2 ** len(steps) < MOSTSEG:
        steps.append(2 ** len(steps))
    S = len(steps)

    def spread(ring, x):
        total, rest = x, x
        for k, d in enumerate(steps):
            total = total + masks[ring, k] * roll(total, d, x.ndim - 1)
            rest = rest + masks[ring, S + k] * roll(rest, -d, x.ndim - 1)
        return total + rest - x

    def coarsen(ring, b, r, i, count):
        mean = jnp.concatenate([get(b, c, r, i, count) for c in range(3)], axis=0)
        mean = spread(ring, mean) * masks[ring, 2 * S]
        low = roll(roll(mean, -wide, 2), 1, 1)
        high = roll(roll(mean, wide, 2), -1, 1)
        mean = jnp.where(lane < pad, low, mean)
        mean = jnp.where(lane >= pad + wide, high, mean)
        for c in range(3):
            for k in range(count):
                put(b, c, r, i + k, mean[c * count + k])

    def coarsen_block(b, first_i, count):
        @pl.when(rad == 0)
        def _():
            for r in range(NRING):
                coarsen(r, b, r + 1, first_i, count)

    def coarsen_below(b, first_i, count):
        if R == NRING:
            @pl.when(rad == 1)
            def _():
                coarsen(R - 1, b, 0, first_i, count)

    fetch_map.wait()

    @pl.when(rad <= (1 if R == NRING else 0))
    def _():
        labels = map_ref[...].astype(jnp.float32)
        for s, piece in enumerate(segments(tiles_of(labels), wide, pad)):
            maps[pl.ds(s, NRING, stride=SUB), :] = piece
        for ring in range(NRING):
            label = maps[ring * SUB : (ring + 1) * SUB, :]
            for k, d in enumerate(steps):
                masks[ring, k] = (roll(label, d, 1) == label).astype(jnp.float32)
                masks[ring, S + k] = (roll(label, -d, 1) == label).astype(jnp.float32)
            masks[ring, 2 * S] = 1.0 / spread(ring, jnp.ones((SUB, LANES), jnp.float32))

    fetch.wait()
    for c in range(3):
        for r in range(R):
            unpack(nat[c, r], 0, c, r + 1, 2)
    coarsen_block(0, 2, Z)

    @pl.when(ax < 2)
    def _():
        hear(0)
        tell(0)

    @pl.when(first)
    def _():
        send(v_hbm.at[:, :, pl.ds(0, 2)], hl, 0, LATE, left, rad)
        pl.when(has_hi)(lambda: send(v_hbm.at[:, R - 1, pl.ds(0, 1)], hc.at[0], 1, LATE + 1, left, rad + 1))
        pl.when(has_lo)(lambda: send(v_hbm.at[:, 0, pl.ds(0, 1)], hc.at[1], 2, LATE + 2, left, rad - 1))

    def rim_in(side, row):
        line = 3 * K
        pl.when(first)(lambda: drain(ROW + side, line * (Z + 4)))
        pl.when(last)(lambda: drain(ROW + side, line * (Z + 1)))
        pl.when((ax > 0) & (ax < n_ax - 1))(lambda: drain(ROW + side, line * (Z + 2)))
        for c in range(3):
            unpack(hr[side, c], 0, c, row, 1)

        @pl.when(first)
        def _():
            for c in range(3):
                unpack(hq[side, c], 1, c, row, Z - 1)
                unpack(hr[side, c, 0:1], 1, c, row, Z + 1)

    pl.when(has_lo)(lambda: rim_in(0, 0))
    pl.when(has_hi)(lambda: rim_in(1, R + 1))
    coarsen_below(0, 1, Z + 2)
    pl.when(first)(lambda: coarsen_below(1, Z - 1, 3))
    block = 3 * R * K

    @pl.when(first)
    def _():
        drain(ZL, block * 4)
        for c in range(3):
            for r in range(R):
                if far:
                    unpack(hf[c, r], 1, c, r + 1, Z - 2)
                unpack(hw[c, r], 1, c, r + 1, Z - near)
                unpack(hz[0, c, r], 1, c, r + 1, Z)
        coarsen_block(1, Z - 2, 4)
        for c in range(3):
            for r in range(1, R + 1):
                for i in range(2):
                    put(0, c, r, i, get(1, c, r, Z + i, 1)[0])
                    put(1, c, r, Z + 2 + i, get(0, c, r, 2 + i, 1)[0])
            for r in (0, R + 1):
                put(1, c, r, Z + 2, get(0, c, r, 2, 1)[0])

    @pl.when(ax > 0)
    def _():
        drain(ZL, block * 2)
        for c in range(3):
            for r in range(R):
                unpack(hz[0, c, r], 0, c, r + 1, 0)
        coarsen_block(0, 0, 2)

    @pl.when(ax < n_ax - 1)
    def _():
        drain(ZR, block * 2)
        for c in range(3):
            for r in range(R):
                unpack(hz[1, c, r], 0, c, r + 1, Z + 2)
        coarsen_block(0, Z + 2, 2)

    def ends(b, first_i, count):
        @pl.when(rad == 0)
        def _():
            for c in range(3):
                for i in range(first_i, first_i + count):
                    put(b, c, 0, i, SIGNS[c] * roll(get(b, c, 1, i, 1)[0], half, 0))

        @pl.when(rad == n_rad - 1)
        def _():
            for c in range(3):
                for i in range(first_i, first_i + count):
                    put(b, c, R + 1, i, jnp.zeros((SUB, LANES), jnp.float32))

    def phase(b, low_z, high_z):
        n, i0 = high_z - low_z, low_z + 2
        for r in range(1, R + 1):
            grads = []
            for c in range(3):
                long = get(b, c, r, i0 - 2, n + 4)
                after, before = up(long), down(long)
                wsc[c, r, 0 : n + 2] = smooth_z((after + before) + (long + long))
                grads.append([
                    long[2:] - long[:-2],
                    get(b, c, r + 1, i0 - 1, n + 2) - get(b, c, r - 1, i0 - 1, n + 2),
                    after[1:-1] - before[1:-1],
                ])
            terms, size = tensor(grads)
            for p in range(6):
                flux[p, r - 1, 0 : n + 2] = size * terms[p]
        for r in (0, R + 1):
            for c in range(3):
                wsc[c, r, 1 : n + 1] = smooth_t(smooth_z(get(b, c, r, i0 - 1, n + 2)))
        out = []
        for r in range(1, R + 1):
            grads, mids = [], []
            for c in range(3):
                mid = wsc[c, r, 1 : n + 1]
                mids.append(mid)
                grads.append([
                    wsc[c, r, 2 : n + 2] - wsc[c, r, 0:n],
                    wsc[c, r + 1, 1 : n + 1] - wsc[c, r - 1, 1 : n + 1],
                    up(mid) - down(mid),
                ])
            terms, size = tensor(grads)
            size = 0.25 * size
            sums = [[0.0, 0.0], [0.0, 0.0]]
            for p, (c, a) in enumerate(PAIRS):
                product = get(b, c, r, i0 - 1, n + 2) * get(b, a, r, i0 - 1, n + 2)
                leonard = 16.0 * smooth_t(smooth_z(product)) - mids[c] * mids[a]
                model = smooth_t(smooth_z(flux[p, r - 1, 0 : n + 2])) - size * terms[p]
                kind = sums[0 if c == a else 1]
                kind[0] = kind[0] + leonard * model
                kind[1] = kind[1] + model * model
            out.append([sums[0][k] + 2.0 * sums[1][k] for k in range(2)])
        return out

    ends(0, 1, Z + 2)

    @pl.when(first)
    def _():
        ends(1, Z - 1, 4)
        for r, pair_of in enumerate(phase(1, Z - 2, Z)):
            for k in range(2):
                acc[k, r] = jnp.sum(pair_of[k], axis=0)

    @pl.when(ax > 0)
    def _():
        acc[...] = jnp.zeros(acc.shape, jnp.float32)

    sub_index = lax.broadcasted_iota(jnp.int32, (SUB, LANES), 0)
    lane_index = lax.broadcasted_iota(jnp.int32, (SUB, LANES), 1)
    mine = jnp.zeros((SUB, LANES), jnp.float32)
    for r, pair_of in enumerate(phase(0, 0, Z)):
        for k in range(2):
            whole = jnp.sum(pair_of[k][: Z - 2], axis=0)
            rest = jnp.sum(pair_of[k][Z - 2 :], axis=0)
            row = acc[k, r] + whole + jnp.where(last, 0.0, rest)
            row = jnp.sum(row, axis=0, keepdims=True) * (2.0 ** -15, 2.0 ** -14)[k]
            mine = jnp.where(sub_index == k * half + r, row, mine)
    mine = jnp.where((lane_index >= pad) & (lane_index < pad + wide), mine, 0.0)
    fold = LANES // 2
    while fold >= LANES // SUB:
        mine = mine + roll(mine, fold, 1)
        fold //= 2
    group = lane_index // (LANES // SUB) == sub_index
    part[...] = jnp.sum(jnp.where(group, mine, 0.0), axis=0, keepdims=True)

    def sums(side, i):
        peer = lax.rem(ax + i, n_ax)
        send(part, parts.at[(1 - side) * n_ax + ax], (0, 1, 2)[side], SUMS + 1 - side, peer, rad + side)

    def sums_in(side, amount):
        pltpu.make_async_copy(parts.at[pl.ds(0, amount)], parts.at[pl.ds(0, amount)], sems.at[SUMS + 1 + side]).wait()

    def first_of(side):
        return 1 if side == 0 else 0

    def send_sums(side):
        start = first_of(side)
        each(n_ax - start, lambda i: sums(side, i + start))

    pl.when(ax > 1)(lambda: hear(0))
    for stage in range(1, len(distances)):
        tell(stage)
        hear(stage)
    send_sums(0)
    pl.when(has_lo)(lambda: send_sums(-1))
    pl.when(has_hi)(lambda: send_sums(1))

    @pl.when(last)
    def _():
        drain(LATE, block * 2)
        for c in range(3):
            for r in range(R):
                unpack(hl[c, r], 0, c, r + 1, Z + 2)
        coarsen_block(0, Z + 2, 2)

        @pl.when(has_lo)
        def _():
            drain(LATE + 1, 3 * K)
            for c in range(3):
                unpack(hc[0, c], 0, c, 0, Z + 2)

        @pl.when(has_hi)
        def _():
            drain(LATE + 2, 3 * K)
            for c in range(3):
                unpack(hc[1, c], 0, c, R + 1, Z + 2)

        coarsen_below(0, Z + 2, 1)
        ends(0, Z + 2, 1)
        for r in range(1, R + 1):
            grads = []
            for c in range(3):
                long = get(0, c, r, Z, 4)
                mid = long[1:-1]
                grads.append([
                    long[2:] - long[:-2],
                    get(0, c, r + 1, Z + 1, 2) - get(0, c, r - 1, Z + 1, 2),
                    up(mid) - down(mid),
                ])
            terms, size = tensor(grads)
            for p in range(6):
                flux[p, r - 1, Z : Z + 2] = size * terms[p]

    for c in range(3):
        hx[c, 1 : R + 1] = flux[pair(c, 1), :, 1 : Z + 1]
    pl.when(has_hi)(lambda: send(hx.at[:, R], hx.at[:, 0], 1, EDGE, ax, rad + 1))
    pl.when(has_lo)(lambda: send(hx.at[:, 1], hx.at[:, R + 1], 2, EDGE + 1, ax, rad - 1))

    @pl.when(rad == 0)
    def _():
        for c in range(3):
            for z in range(Z):
                hx[c, 0, z] = SIGNS[c] * SIGNS[1] * roll(hx[c, 1, z], half, 0)

    @pl.when(rad == n_rad - 1)
    def _():
        for c in range(3):
            for z in range(Z):
                hx[c, R + 1, z] = jnp.zeros((SUB, LANES), jnp.float32)

    bases, turns = [[], [], []], [[], [], []]
    for r in range(1, R + 1):
        for c in range(3):
            axial = get(0, c, r, 1, Z + 2) * get(0, 0, r, 1, Z + 2)
            outer = get(0, c, r + 1, 2, Z) * get(0, 1, r + 1, 2, Z)
            inner = get(0, c, r - 1, 2, Z) * get(0, 1, r - 1, 2, Z)
            mid = get(0, c, r, 2, Z)
            around = mid * get(0, 2, r, 2, Z)
            change = axial[2:] - axial[:-2] + (outer - inner) + (up(around) - down(around))
            bases[c].append(mid - 0.5 * change)
            turn = flux[pair(c, 2), r - 1, 1 : Z + 1]
            p = pair(c, 0)
            turns[c].append(flux[p, r - 1, 2 : Z + 2] - flux[p, r - 1, 0:Z] + (up(turn) - down(turn)))

    count = n_ax * Z * T
    sums_in(0, n_ax - 1)

    def coefficients(total):
        total = jnp.broadcast_to(jnp.sum(jnp.where(group, total, 0.0), axis=1, keepdims=True), (SUB, LANES)) / count
        return 0.125 * (total / (roll(total, -half, 0) + EPSILON))

    def total_of(side):
        start = first_of(side)
        total = part[...] if start else jnp.zeros((1, LANES), jnp.float32)
        if n_ax <= 16:
            for i in range(start, n_ax):
                total = total + parts[(1 + side) * n_ax + lax.rem(ax + i, n_ax)]
            return total
        return lax.fori_loop(
            start, n_ax, lambda i, t: t + parts[(1 + side) * n_ax + lax.rem(ax + i, n_ax)], total)

    coef = coefficients(total_of(0))

    def beside(side, row):
        sums_in(side, n_ax)
        edge_coef[0 if side < 0 else 1] = jnp.broadcast_to(
            coefficients(total_of(side))[row : row + 1], (SUB, LANES))

    pl.when(has_lo)(lambda: beside(-1, R - 1))
    pl.when(has_hi)(lambda: beside(1, 0))

    @pl.when(rad == 0)
    def _():
        edge_coef[0] = jnp.broadcast_to(coef[0:1], (SUB, LANES))

    @pl.when(rad == n_rad - 1)
    def _():
        edge_coef[1] = jnp.zeros((SUB, LANES), jnp.float32)

    pl.when(has_lo)(lambda: drain(EDGE, 3 * Z * SUB))
    pl.when(has_hi)(lambda: drain(EDGE + 1, 3 * Z * SUB))
    by_row = [edge_coef[0]] + [jnp.broadcast_to(coef[r : r + 1], (SUB, LANES)) for r in range(R)] + [edge_coef[1]]
    for c in range(3):
        for r in range(R):
            new = bases[c][r] + by_row[r + 1] * turns[c][r]
            new = new + (by_row[r + 2] * hx[c, r + 2] - by_row[r] * hx[c, r])
            for z in range(Z):
                row = ((c * R + r) * Z + z) * SUB
                res[row : row + SUB, :] = new[z]
    for c in range(3):
        for r in range(R):
            base = (c * R + r) * Z * SUB
            pieces = [res[pl.ds(base + s, Z, stride=SUB), :] for s in range(SUB)]
            for k, tile in enumerate(joined(pieces, wide, pad)):
                out_ref[c, r, :, k * LANES : (k + 1) * LANES] = tile

    middle = (ax > 0) & (ax < n_ax - 2)

    def sent(group, usual, for_first, for_last, for_second):
        pl.when(middle)(lambda: drain(SEND + group, usual))
        pl.when(first)(lambda: drain(SEND + group, for_first))
        pl.when(last)(lambda: drain(SEND + group, for_last))
        pl.when(second)(lambda: drain(SEND + group, for_second))

    line, total = 3 * K, n_ax - 1
    sent(0, 4 * block + total, 4 * block + total, (4 + near) * block + total, (4 + far) * block + total)
    total = 3 * Z * SUB + n_ax
    usual, more = line * (Z + 2) + total, line * (Z + 4) + total
    pl.when(has_hi)(lambda: sent(1, usual, usual, more, usual))
    pl.when(has_lo)(lambda: sent(2, usual, usual, more, usual))


def shards(n_ax, n_rad, velocity, cycle_map):
    _, R, Z, T = velocity.shape
    near = min(2, Z - 2)
    assert n_ax >= 8 and R >= NRING and Z >= 3

    def vmem(*shape):
        return pltpu.VMEM(shape, jnp.float32)

    return pl.pallas_call(
        functools.partial(kernel, n_ax, n_rad),
        out_shape=jax.ShapeDtypeStruct(velocity.shape, velocity.dtype),
        in_specs=[pl.BlockSpec(memory_space=pltpu.HBM)] * 2,
        out_specs=pl.BlockSpec(memory_space=pltpu.VMEM),
        scratch_shapes=[
            vmem(*velocity.shape),
            pltpu.VMEM(cycle_map.shape, jnp.int32),
            vmem(NRING * SUB, LANES),
            vmem(NRING, 2 * (MOSTSEG - 1).bit_length() + 1, SUB, LANES),
            vmem(2 * 3 * (R + 2) * (Z + 4) * SUB, LANES),
            vmem(2, 3, R, 2, T),
            vmem(3, R, near, T),
            vmem(3, R, max(1, 2 - near), T),
            vmem(2, 3, Z + 2, T),
            vmem(2, 3, 2, T),
            vmem(3, R, 2, T),
            vmem(2, 3, 1, T),
            vmem(3, R + 2, Z + 2, SUB, LANES),
            vmem(6, R, Z + 2, SUB, LANES),
            vmem(3, R + 2, Z, SUB, LANES),
            vmem(3 * R * Z * SUB, LANES),
            vmem(2, R, SUB, LANES),
            vmem(1, LANES),
            vmem(3 * n_ax, 1, LANES),
            vmem(2, SUB, LANES),
            vmem(3 * (R * 6 + Z) * SUB * (T // LANES) + 2 * n_ax, LANES),
            pltpu.SemaphoreType.REGULAR((len(stages(n_ax)),)),
            pltpu.SemaphoreType.DMA((SEMS,)),
        ],
        compiler_params=pltpu.CompilerParams(collective_id=0, has_side_effects=True, vmem_limit_bytes=8 << 20),
    )(*(pltpu.with_memory_space_constraint(x, pltpu.HBM) for x in (velocity, cycle_map)))


def solution(mesh):
    n_ax, n_rad = mesh.shape["ax"], mesh.shape["rad"]
    spec = P(None, "rad", "ax", None)
    body = functools.partial(shards, n_ax, n_rad)
    return jax.shard_map(body, mesh=mesh, in_specs=(spec, P()), out_specs=spec, check_vma=False)
```

```python
import functools

import jax
import jax.numpy as jnp
from jax import lax
from jax.experimental import pallas as pl
from jax.experimental.pallas import tpu as pltpu
from jax.sharding import PartitionSpec as P

NRING = 3
MOSTSEG = 16
SUB = 8
LANES = 128
PAIRS = ((0, 0), (1, 1), (2, 2), (0, 1), (0, 2), (1, 2))
SIGNS = (1.0, -1.0, -1.0)
EPSILON = 1e-06
MESH = pl.DeviceIdType.MESH
IN, SEND, ZL, ZR, ROW, LATE, EDGE, SUMS, SEMS = 0, 2, 5, 6, 7, 9, 12, 14, 17


def pair(a, b):
    return PAIRS.index((min(a, b), max(a, b)))


def each(count, body):
    if count <= 16:
        for i in range(count):
            body(i)
    else:
        lax.fori_loop(0, count, lambda i, c: (body(i), c)[1], 0)


def roll(x, shift, axis):
    size = x.shape[axis]
    return pltpu.roll(x, shift % size, axis)


def up(x):
    return roll(x, -1, x.ndim - 1)


def down(x):
    return roll(x, 1, x.ndim - 1)


def smooth_t(x):
    return (down(x) + up(x)) + (x + x)


def smooth_z(x):
    y = x[:-1] + x[1:]
    return y[:-1] + y[1:]


def tiles_of(x):
    return [x[:, k : k + LANES] for k in range(0, x.shape[1], LANES)]


def segments(x, wide, pad):
    rows, tiles = x[0].shape[0], len(x)
    total = tiles * LANES
    lane = lax.broadcasted_iota(jnp.int32, (rows, LANES), 1)
    pieces = []
    for s in range(SUB):
        start = (s * wide - pad) % total
        k, off = start // LANES, start % LANES
        first = x[k]
        if off:
            k2 = (k + 1) % tiles
            second = x[k2]
            first = jnp.where(lane < LANES - off, roll(first, -off, 1), roll(second, -off, 1))
        pieces.append(first)
    return pieces


def joined(pieces, wide, pad):
    rows = pieces[0].shape[0]
    lane = lax.broadcasted_iota(jnp.int32, (rows, LANES), 1)
    tiles = []
    for k in range(SUB * wide // LANES):
        lo, hi = k * LANES, (k + 1) * LANES
        s = lo // wide
        out = None
        while s * wide < hi:
            part = roll(pieces[s], s * wide - pad - lo, 1)
            out = part if out is None else jnp.where(lane >= s * wide - lo, part, out)
            s += 1
        tiles.append(out)
    return tiles


def tensor(grads):
    terms = [grads[c][c] + grads[c][c] if c == a else grads[c][a] + grads[a][c] for c, a in PAIRS]
    squares = [x * x for x in terms]
    total = 0.5 * (squares[0] + squares[1] + squares[2]) + (squares[3] + squares[4] + squares[5])
    return terms, jnp.sqrt(total)


def stages(n_ax):
    distances, reach = [], 2
    while reach < n_ax // 2:
        distances.append(reach)
        reach *= 2
    return distances


def kernel(n_ax, n_rad, v_hbm, map_hbm, out_ref, nat, map_ref, maps, masks, ext, rims, hz, he, hr, hq, hl, hc, wsc,
           lsc, flux, hx, res, acc, part, parts, edge_coef, spare, ready, sems):
    rad = lax.axis_index("rad")
    ax = lax.axis_index("ax")
    R, Z, T = nat.shape[1], nat.shape[2], nat.shape[3]
    K = T // LANES
    wide = T // SUB
    pad = (LANES - wide) // 2
    half = SUB // 2
    near = min(2, Z - 2)
    far = 2 - near
    right, left = lax.rem(ax + 1, n_ax), lax.rem(ax + n_ax - 1, n_ax)
    has_lo, has_hi = rad > 0, rad < n_rad - 1
    first, last, second = ax == 0, ax == n_ax - 1, ax == n_ax - 2

    barrier = pltpu.get_barrier_semaphore()

    def greet(offset, to_rad):
        peer = (lax.rem(ax + offset + n_ax, n_ax), to_rad)
        pl.semaphore_signal(barrier, inc=1, device_id=peer, device_id_type=MESH)

    def greet_row(to_rad, offsets):
        for o in offsets:
            greet(o, to_rad)

    def greet_all(offsets, beside):
        greet_row(rad, offsets)
        pl.when(has_lo)(lambda: greet_row(rad - 1, offsets + beside))
        pl.when(has_hi)(lambda: greet_row(rad + 1, offsets + beside))

    greet_all((-1, -2), (0,))
    pl.when(ax + 1 < n_ax)(lambda: greet_all((1,), ()))
    pl.when(ax + 2 < n_ax)(lambda: greet_all((2,), ()))

    fetch = pltpu.make_async_copy(v_hbm, nat, sems.at[IN])
    fetch.start()
    fetch_map = pltpu.make_async_copy(map_hbm, map_ref, sems.at[IN + 1])
    fetch_map.start()

    distances = stages(n_ax)

    def tell(stage):
        d = distances[stage]
        for peer in (lax.rem(ax + d, n_ax), lax.rem(ax + n_ax - d, n_ax)):
            pl.semaphore_signal(ready.at[stage], inc=1, device_id=(peer, rad), device_id_type=MESH)

    def hear(stage):
        pl.semaphore_wait(ready.at[stage], 2)

    def drain(sem, amount):
        pltpu.make_async_copy(spare.at[pl.ds(0, amount)], spare.at[pl.ds(0, amount)], sems.at[sem]).wait()

    def send(src, dst, group, recv, to_ax, to_rad):
        pltpu.make_async_remote_copy(
            src_ref=src, dst_ref=dst, send_sem=sems.at[SEND + group], recv_sem=sems.at[recv],
            device_id=(to_ax, to_rad), device_id_type=MESH).start()

    beside_sum = jnp.where(has_lo, 1, 0) + jnp.where(has_hi, 1, 0)
    row_sum = 4 - jnp.where(first, 2, 0) - jnp.where(ax == 1, 1, 0)
    pl.semaphore_wait(barrier, row_sum * (1 + beside_sum) + beside_sum)

    def planes(first_z, count, dst, row, group, recv, to_ax):
        for r in range(R):
            send(v_hbm.at[:, r, pl.ds(first_z, count)], dst.at[:, pl.ds(2 * r + row, count)], group, recv, to_ax, rad)

    @pl.when(last)
    def _():
        planes(Z - 2 - near, near, he, far, 0, ZL, right)

    planes(Z - 2, 2, hz.at[0], 0, 0, ZL, right)
    if far:
        pl.when(second)(lambda: planes(Z - far, far, he, 0, 0, ZL, lax.rem(ax + 2, n_ax)))
    pl.when(ax > 0)(lambda: planes(0, 2, hz.at[1], 0, 0, ZR, left))

    def rim(side, group, row, to_rad):
        send(v_hbm.at[:, row, pl.ds(Z - 1, 1)], hr.at[side, :, pl.ds(0, 1)], group, ROW + side, right, to_rad)

        @pl.when(last)
        def _():
            send(v_hbm.at[:, row, pl.ds(Z - 3, 2)], hq.at[side], group, ROW + side, right, to_rad)

        @pl.when(ax > 0)
        def _():
            send(v_hbm.at[:, row, pl.ds(0, 1)], hr.at[side, :, pl.ds(Z + 1, 1)], group, ROW + side, left, to_rad)

        send(v_hbm.at[:, row], hr.at[side, :, pl.ds(1, Z)], group, ROW + side, ax, to_rad)

    pl.when(has_hi)(lambda: rim(0, 1, R - 1, rad + 1))
    pl.when(has_lo)(lambda: rim(1, 2, 0, rad - 1))
    pl.when(ax > 1)(lambda: tell(0))

    def row_of(b, c, r, i):
        line, pairs = c * R + r - 1, 3 * R * 2
        if b:
            k = i - Z + 2
            return (3 * R * Z + pairs * (2 + k // 2) + line * 2 + k % 2) * SUB
        if 2 <= i < Z + 2:
            return (line * Z + i - 2) * SUB
        return (3 * R * Z + (line * 2 + i if i < 2 else pairs + line * 2 + i - Z - 2)) * SUB

    def rim_of(b, c, r, i):
        return (((b * 3 + c) * 2 + (0 if r == 0 else 1)) * (Z + 4) + i) * SUB

    def place(b, c, r, i):
        inside = 0 < r <= R
        return (ext, row_of(b, c, r, i)) if inside else (rims, rim_of(b, c, r, i))

    def get(b, c, r, i, n):
        blocks = []
        for k in range(n):
            ref, row = place(b, c, r, i + k)
            blocks.append(ref[row : row + SUB, :])
        return jnp.stack(blocks)

    def put(b, c, r, i, x):
        ref, row = place(b, c, r, i)
        ref[row : row + SUB, :] = x

    def unpack(x, target):
        ref, row = target
        for s, piece in enumerate(segments(tiles_of(x), wide, pad)):
            ref[pl.ds(row + s, x.shape[0], stride=SUB), :] = piece

    lane = lax.broadcasted_iota(jnp.int32, (SUB, LANES), 1)
    steps = []
    while 2 ** len(steps) < MOSTSEG:
        steps.append(2 ** len(steps))
    S = len(steps)

    def spread(ring, x):
        total, rest = x, x
        for k, d in enumerate(steps):
            total = total + masks[ring, k] * roll(total, d, x.ndim - 1)
            rest = rest + masks[ring, S + k] * roll(rest, -d, x.ndim - 1)
        return total + rest - x

    def coarsen(ring, b, r, i, count):
        mean = jnp.concatenate([get(b, c, r, i, count) for c in range(3)], axis=0)
        mean = spread(ring, mean) * masks[ring, 2 * S]
        low = roll(roll(mean, -wide, 2), 1, 1)
        high = roll(roll(mean, wide, 2), -1, 1)
        mean = jnp.where(lane < pad, low, mean)
        mean = jnp.where(lane >= pad + wide, high, mean)
        for c in range(3):
            for k in range(count):
                put(b, c, r, i + k, mean[c * count + k])

    def coarsen_block(b, first_i, count):
        @pl.when(rad == 0)
        def _():
            for r in range(NRING):
                coarsen(r, b, r + 1, first_i, count)

    def coarsen_below(b, first_i, count):
        if R == NRING:
            @pl.when(rad == 1)
            def _():
                coarsen(R - 1, b, 0, first_i, count)

    fetch_map.wait()

    @pl.when(rad <= (1 if R == NRING else 0))
    def _():
        labels = map_ref[...].astype(jnp.float32)
        for s, piece in enumerate(segments(tiles_of(labels), wide, pad)):
            maps[pl.ds(s, NRING, stride=SUB), :] = piece
        for ring in range(NRING):
            label = maps[ring * SUB : (ring + 1) * SUB, :]
            for k, d in enumerate(steps):
                masks[ring, k] = (roll(label, d, 1) == label).astype(jnp.float32)
                masks[ring, S + k] = (roll(label, -d, 1) == label).astype(jnp.float32)
            masks[ring, 2 * S] = 1.0 / spread(ring, jnp.ones((SUB, LANES), jnp.float32))

    fetch.wait()
    for c in range(3):
        for r in range(R):
            unpack(nat[c, r], place(0, c, r + 1, 2))
    coarsen_block(0, 2, Z)

    @pl.when(ax < 2)
    def _():
        hear(0)
        tell(0)

    @pl.when(first)
    def _():
        planes(0, 2, hl, 0, 0, LATE, left)
        pl.when(has_hi)(lambda: send(v_hbm.at[:, R - 1, pl.ds(0, 1)], hc.at[0], 1, LATE + 1, left, rad + 1))
        pl.when(has_lo)(lambda: send(v_hbm.at[:, 0, pl.ds(0, 1)], hc.at[1], 2, LATE + 2, left, rad - 1))

    def local(b, low_z, high_z):
        n, i0 = high_z - low_z, low_z + 2
        for r in range(1, R + 1):
            longs, filtered = [], []
            for c in range(3):
                longs.append(get(b, c, r, i0 - 1, n + 2))
                filtered.append(smooth_t(smooth_z(get(b, c, r, i0 - 2, n + 4))))
                wsc[b, c, r, 0 : n + 2] = filtered[c]
            for p, (c, a) in enumerate(PAIRS):
                product = smooth_t(smooth_z(longs[c] * longs[a]))
                lsc[b, p, r - 1, 0:n] = 16.0 * product - filtered[c][1:-1] * filtered[a][1:-1]

    block = 3 * R * K

    @pl.when(first)
    def _():
        drain(ZL, block * 4)
        for c in range(3):
            unpack(he[c], place(1, c, 1, Z - 2))
            unpack(hz[0, c], place(1, c, 1, Z))
        coarsen_block(1, Z - 2, 4)
        for c in range(3):
            for r in range(1, R + 1):
                for i in range(2):
                    put(0, c, r, i, get(1, c, r, Z + i, 1)[0])
                    put(1, c, r, Z + 2 + i, get(0, c, r, 2 + i, 1)[0])
        local(1, Z - 2, Z)

    @pl.when(ax > 0)
    def _():
        drain(ZL, block * 2)
        for c in range(3):
            unpack(hz[0, c], place(0, c, 1, 0))
        coarsen_block(0, 0, 2)

    @pl.when(ax < n_ax - 1)
    def _():
        drain(ZR, block * 2)
        for c in range(3):
            unpack(hz[1, c], place(0, c, 1, Z + 2))
        coarsen_block(0, Z + 2, 2)

    local(0, 0, Z)

    def rim_in(side, row):
        line = 3 * K
        pl.when(first)(lambda: drain(ROW + side, line * (Z + 4)))
        pl.when(last)(lambda: drain(ROW + side, line * (Z + 1)))
        pl.when((ax > 0) & (ax < n_ax - 1))(lambda: drain(ROW + side, line * (Z + 2)))
        for c in range(3):
            unpack(hr[side, c], place(0, c, row, 1))

        @pl.when(first)
        def _():
            for c in range(3):
                unpack(hq[side, c], place(1, c, row, Z - 1))
                unpack(hr[side, c, 0:2], place(1, c, row, Z + 1))

    pl.when(has_lo)(lambda: rim_in(0, 0))
    pl.when(has_hi)(lambda: rim_in(1, R + 1))
    coarsen_below(0, 1, Z + 2)
    pl.when(first)(lambda: coarsen_below(1, Z - 1, 4))

    def ends(b, first_i, count):
        @pl.when(rad == 0)
        def _():
            for c in range(3):
                for i in range(first_i, first_i + count):
                    put(b, c, 0, i, SIGNS[c] * roll(get(b, c, 1, i, 1)[0], half, 0))

        @pl.when(rad == n_rad - 1)
        def _():
            for c in range(3):
                for i in range(first_i, first_i + count):
                    put(b, c, R + 1, i, jnp.zeros((SUB, LANES), jnp.float32))

    def phase(b, low_z, high_z):
        n, i0 = high_z - low_z, low_z + 2
        for r in range(1, R + 1):
            grads = []
            for c in range(3):
                long = get(b, c, r, i0 - 2, n + 4)
                mid = long[1:-1]
                grads.append([
                    long[2:] - long[:-2],
                    get(b, c, r + 1, i0 - 1, n + 2) - get(b, c, r - 1, i0 - 1, n + 2),
                    up(mid) - down(mid),
                ])
            terms, size = tensor(grads)
            for p in range(6):
                flux[p, r - 1, 0 : n + 2] = size * terms[p]
        for r in (0, R + 1):
            for c in range(3):
                wsc[b, c, r, 1 : n + 1] = smooth_t(smooth_z(get(b, c, r, i0 - 1, n + 2)))
        out = []
        for r in range(1, R + 1):
            grads = []
            for c in range(3):
                mid = wsc[b, c, r, 1 : n + 1]
                grads.append([
                    wsc[b, c, r, 2 : n + 2] - wsc[b, c, r, 0:n],
                    wsc[b, c, r + 1, 1 : n + 1] - wsc[b, c, r - 1, 1 : n + 1],
                    up(mid) - down(mid),
                ])
            terms, size = tensor(grads)
            size = 0.25 * size
            sums = [[0.0, 0.0], [0.0, 0.0]]
            for p, (c, a) in enumerate(PAIRS):
                model = smooth_t(smooth_z(flux[p, r - 1, 0 : n + 2])) - size * terms[p]
                kind = sums[0 if c == a else 1]
                kind[0] = kind[0] + lsc[b, p, r - 1, 0:n] * model
                kind[1] = kind[1] + model * model
            out.append([sums[0][k] + 2.0 * sums[1][k] for k in range(2)])
        return out

    ends(0, 1, Z + 2)

    @pl.when(first)
    def _():
        ends(1, Z - 1, 4)
        for r, pair_of in enumerate(phase(1, Z - 2, Z)):
            for k in range(2):
                acc[k, r] = jnp.sum(pair_of[k], axis=0)

    @pl.when(ax > 0)
    def _():
        acc[...] = jnp.zeros(acc.shape, jnp.float32)

    sub_index = lax.broadcasted_iota(jnp.int32, (SUB, LANES), 0)
    lane_index = lax.broadcasted_iota(jnp.int32, (SUB, LANES), 1)
    mine = jnp.zeros((SUB, LANES), jnp.float32)
    for r, pair_of in enumerate(phase(0, 0, Z)):
        for k in range(2):
            whole = jnp.sum(pair_of[k][: Z - 2], axis=0)
            rest = jnp.sum(pair_of[k][Z - 2 :], axis=0)
            row = acc[k, r] + whole + jnp.where(last, 0.0, rest)
            row = jnp.sum(row, axis=0, keepdims=True) * (2.0 ** -15, 2.0 ** -14)[k]
            mine = jnp.where(sub_index == k * half + r, row, mine)
    mine = jnp.where((lane_index >= pad) & (lane_index < pad + wide), mine, 0.0)
    fold = LANES // 2
    while fold >= LANES // SUB:
        mine = mine + roll(mine, fold, 1)
        fold //= 2
    group = lane_index // (LANES // SUB) == sub_index
    part[...] = jnp.sum(jnp.where(group, mine, 0.0), axis=0, keepdims=True)

    def sums(side, i):
        peer = lax.rem(ax + i, n_ax)
        send(part, parts.at[(1 - side) * n_ax + ax], (0, 1, 2)[side], SUMS + 1 - side, peer, rad + side)

    def sums_in(side, amount):
        pltpu.make_async_copy(parts.at[pl.ds(0, amount)], parts.at[pl.ds(0, amount)], sems.at[SUMS + 1 + side]).wait()

    def first_of(side):
        return 1 if side == 0 else 0

    def send_sums(side):
        start = first_of(side)
        each(n_ax - start, lambda i: sums(side, i + start))

    pl.when(ax > 1)(lambda: hear(0))
    for stage in range(1, len(distances)):
        tell(stage)
        hear(stage)
    send_sums(0)
    pl.when(has_lo)(lambda: send_sums(-1))
    pl.when(has_hi)(lambda: send_sums(1))

    @pl.when(last)
    def _():
        drain(LATE, block * 2)
        for c in range(3):
            unpack(hl[c], place(0, c, 1, Z + 2))
        coarsen_block(0, Z + 2, 2)

        @pl.when(has_lo)
        def _():
            drain(LATE + 1, 3 * K)
            for c in range(3):
                unpack(hc[0, c], place(0, c, 0, Z + 2))

        @pl.when(has_hi)
        def _():
            drain(LATE + 2, 3 * K)
            for c in range(3):
                unpack(hc[1, c], place(0, c, R + 1, Z + 2))

        coarsen_below(0, Z + 2, 1)
        ends(0, Z + 2, 1)
        for r in range(1, R + 1):
            grads = []
            for c in range(3):
                long = get(0, c, r, Z, 4)
                mid = long[1:-1]
                grads.append([
                    long[2:] - long[:-2],
                    get(0, c, r + 1, Z + 1, 2) - get(0, c, r - 1, Z + 1, 2),
                    up(mid) - down(mid),
                ])
            terms, size = tensor(grads)
            for p in range(6):
                flux[p, r - 1, Z : Z + 2] = size * terms[p]

    for c in range(3):
        hx[c, 1 : R + 1] = flux[pair(c, 1), :, 1 : Z + 1]
    pl.when(has_hi)(lambda: send(hx.at[:, R], hx.at[:, 0], 1, EDGE, ax, rad + 1))
    pl.when(has_lo)(lambda: send(hx.at[:, 1], hx.at[:, R + 1], 2, EDGE + 1, ax, rad - 1))

    @pl.when(rad == 0)
    def _():
        for c in range(3):
            for z in range(Z):
                hx[c, 0, z] = SIGNS[c] * SIGNS[1] * roll(hx[c, 1, z], half, 0)

    @pl.when(rad == n_rad - 1)
    def _():
        for c in range(3):
            for z in range(Z):
                hx[c, R + 1, z] = jnp.zeros((SUB, LANES), jnp.float32)

    bases, turns = [[], [], []], [[], [], []]
    for r in range(1, R + 1):
        for c in range(3):
            axial = get(0, c, r, 1, Z + 2) * get(0, 0, r, 1, Z + 2)
            outer = get(0, c, r + 1, 2, Z) * get(0, 1, r + 1, 2, Z)
            inner = get(0, c, r - 1, 2, Z) * get(0, 1, r - 1, 2, Z)
            mid = get(0, c, r, 2, Z)
            around = mid * get(0, 2, r, 2, Z)
            change = axial[2:] - axial[:-2] + (outer - inner) + (up(around) - down(around))
            bases[c].append(mid - 0.5 * change)
            turn = flux[pair(c, 2), r - 1, 1 : Z + 1]
            p = pair(c, 0)
            turns[c].append(flux[p, r - 1, 2 : Z + 2] - flux[p, r - 1, 0:Z] + (up(turn) - down(turn)))

    count = n_ax * Z * T
    sums_in(0, n_ax - 1)

    def coefficients(total):
        total = jnp.broadcast_to(jnp.sum(jnp.where(group, total, 0.0), axis=1, keepdims=True), (SUB, LANES)) / count
        return 0.125 * (total / (roll(total, -half, 0) + EPSILON))

    def total_of(side):
        start = first_of(side)
        total = part[...] if start else jnp.zeros((1, LANES), jnp.float32)
        if n_ax <= 16:
            for i in range(start, n_ax):
                total = total + parts[(1 + side) * n_ax + lax.rem(ax + i, n_ax)]
            return total
        return lax.fori_loop(
            start, n_ax, lambda i, t: t + parts[(1 + side) * n_ax + lax.rem(ax + i, n_ax)], total)

    coef = coefficients(total_of(0))

    def beside(side, row):
        sums_in(side, n_ax)
        edge_coef[0 if side < 0 else 1] = jnp.broadcast_to(
            coefficients(total_of(side))[row : row + 1], (SUB, LANES))

    pl.when(has_lo)(lambda: beside(-1, R - 1))
    pl.when(has_hi)(lambda: beside(1, 0))

    @pl.when(rad == 0)
    def _():
        edge_coef[0] = jnp.broadcast_to(coef[0:1], (SUB, LANES))

    @pl.when(rad == n_rad - 1)
    def _():
        edge_coef[1] = jnp.zeros((SUB, LANES), jnp.float32)

    pl.when(has_lo)(lambda: drain(EDGE, 3 * Z * SUB))
    pl.when(has_hi)(lambda: drain(EDGE + 1, 3 * Z * SUB))
    by_row = [edge_coef[0]] + [jnp.broadcast_to(coef[r : r + 1], (SUB, LANES)) for r in range(R)] + [edge_coef[1]]
    for c in range(3):
        for r in range(R):
            new = bases[c][r] + by_row[r + 1] * turns[c][r]
            new = new + (by_row[r + 2] * hx[c, r + 2] - by_row[r] * hx[c, r])
            for z in range(Z):
                row = ((c * R + r) * Z + z) * SUB
                res[row : row + SUB, :] = new[z]
    for c in range(3):
        for r in range(R):
            base = (c * R + r) * Z * SUB
            pieces = [res[pl.ds(base + s, Z, stride=SUB), :] for s in range(SUB)]
            for k, tile in enumerate(joined(pieces, wide, pad)):
                out_ref[c, r, :, k * LANES : (k + 1) * LANES] = tile

    middle = (ax > 0) & (ax < n_ax - 2)

    def sent(group, usual, for_first, for_last, for_second):
        pl.when(middle)(lambda: drain(SEND + group, usual))
        pl.when(first)(lambda: drain(SEND + group, for_first))
        pl.when(last)(lambda: drain(SEND + group, for_last))
        pl.when(second)(lambda: drain(SEND + group, for_second))

    line, total = 3 * K, n_ax - 1
    sent(0, 4 * block + total, 4 * block + total, (4 + near) * block + total, (4 + far) * block + total)
    total = 3 * Z * SUB + n_ax
    usual, more = line * (Z + 2) + total, line * (Z + 4) + total
    pl.when(has_hi)(lambda: sent(1, usual, usual, more, usual))
    pl.when(has_lo)(lambda: sent(2, usual, usual, more, usual))


def shards(n_ax, n_rad, velocity, cycle_map):
    _, R, Z, T = velocity.shape
    assert n_ax >= 8 and R >= NRING and Z >= 3

    def vmem(*shape):
        return pltpu.VMEM(shape, jnp.float32)

    return pl.pallas_call(
        functools.partial(kernel, n_ax, n_rad),
        out_shape=jax.ShapeDtypeStruct(velocity.shape, velocity.dtype),
        in_specs=[pl.BlockSpec(memory_space=pltpu.HBM)] * 2,
        out_specs=pl.BlockSpec(memory_space=pltpu.VMEM),
        scratch_shapes=[
            vmem(*velocity.shape),
            pltpu.VMEM(cycle_map.shape, jnp.int32),
            vmem(NRING * SUB, LANES),
            vmem(NRING, 2 * (MOSTSEG - 1).bit_length() + 1, SUB, LANES),
            vmem(3 * R * (Z + 10) * SUB, LANES),
            vmem(2 * 3 * 2 * (Z + 4) * SUB, LANES),
            vmem(2, 3, 2 * R, T),
            vmem(3, 2 * R, T),
            vmem(2, 3, Z + 2, T),
            vmem(2, 3, 2, T),
            vmem(3, 2 * R, T),
            vmem(2, 3, 1, T),
            vmem(2, 3, R + 2, Z + 2, SUB, LANES),
            vmem(2, 6, R, Z, SUB, LANES),
            vmem(6, R, Z + 2, SUB, LANES),
            vmem(3, R + 2, Z, SUB, LANES),
            vmem(3 * R * Z * SUB, LANES),
            vmem(2, R, SUB, LANES),
            vmem(1, LANES),
            vmem(3 * n_ax, 1, LANES),
            vmem(2, SUB, LANES),
            vmem(3 * (R * 6 + Z) * SUB * (T // LANES) + 2 * n_ax, LANES),
            pltpu.SemaphoreType.REGULAR((len(stages(n_ax)),)),
            pltpu.SemaphoreType.DMA((SEMS,)),
        ],
        compiler_params=pltpu.CompilerParams(collective_id=0, has_side_effects=True, vmem_limit_bytes=8 << 20),
    )(*(pltpu.with_memory_space_constraint(x, pltpu.HBM) for x in (velocity, cycle_map)))


def solution(mesh):
    n_ax, n_rad = mesh.shape["ax"], mesh.shape["rad"]
    spec = P(None, "rad", "ax", None)
    body = functools.partial(shards, n_ax, n_rad)
    return jax.shard_map(body, mesh=mesh, in_specs=(spec, P()), out_specs=spec, check_vma=False)
```

```python
import functools

import jax
import jax.numpy as jnp
from jax import lax
from jax.experimental import pallas as pl
from jax.experimental.pallas import tpu as pltpu
from jax.sharding import PartitionSpec as P

NRING = 3
MOSTSEG = 16
SUB = 8
LANES = 128
PAIRS = ((0, 0), (1, 1), (2, 2), (0, 1), (0, 2), (1, 2))
SIGNS = (1.0, -1.0, -1.0)
EPSILON = 1e-06
MESH = pl.DeviceIdType.MESH
IN, SEND, ZL, ZR, ROW, LATE, EDGE, SUMS, SEMS = 0, 2, 5, 6, 7, 9, 12, 14, 17


def pair(a, b):
    return PAIRS.index((min(a, b), max(a, b)))


def each(count, body):
    if count <= 16:
        for i in range(count):
            body(i)
    else:
        lax.fori_loop(0, count, lambda i, c: (body(i), c)[1], 0)


def roll(x, shift, axis):
    size = x.shape[axis]
    return pltpu.roll(x, shift % size, axis)


def up(x):
    return roll(x, -1, x.ndim - 1)


def down(x):
    return roll(x, 1, x.ndim - 1)


def smooth_t(x):
    return (down(x) + up(x)) + (x + x)


def smooth_z(x):
    y = x[:-1] + x[1:]
    return y[:-1] + y[1:]


def tiles_of(x):
    return [x[:, k : k + LANES] for k in range(0, x.shape[1], LANES)]


def segments(x, wide, pad):
    rows, tiles = x[0].shape[0], len(x)
    total = tiles * LANES
    lane = lax.broadcasted_iota(jnp.int32, (rows, LANES), 1)
    pieces = []
    for s in range(SUB):
        start = (s * wide - pad) % total
        k, off = start // LANES, start % LANES
        first = x[k]
        if off:
            k2 = (k + 1) % tiles
            second = x[k2]
            first = jnp.where(lane < LANES - off, roll(first, -off, 1), roll(second, -off, 1))
        pieces.append(first)
    return pieces


def joined(pieces, wide, pad):
    rows = pieces[0].shape[0]
    lane = lax.broadcasted_iota(jnp.int32, (rows, LANES), 1)
    tiles = []
    for k in range(SUB * wide // LANES):
        lo, hi = k * LANES, (k + 1) * LANES
        s = lo // wide
        out = None
        while s * wide < hi:
            part = roll(pieces[s], s * wide - pad - lo, 1)
            out = part if out is None else jnp.where(lane >= s * wide - lo, part, out)
            s += 1
        tiles.append(out)
    return tiles


def tensor(grads):
    terms = [grads[c][c] + grads[c][c] if c == a else grads[c][a] + grads[a][c] for c, a in PAIRS]
    squares = [x * x for x in terms]
    total = 0.5 * (squares[0] + squares[1] + squares[2]) + (squares[3] + squares[4] + squares[5])
    return terms, jnp.sqrt(total)


def stages(n_ax):
    distances, reach = [], 2
    while reach < n_ax // 2:
        distances.append(reach)
        reach *= 2
    return distances


def kernel(n_ax, n_rad, v_hbm, map_hbm, out_ref, nat, map_ref, maps, masks, ext, rims, hz, he, hr, hl, hc, wsc,
           lsc, around, slope, paired, flux, hx, res, acc, part, parts, edge_coef, spare, ready, sems):
    rad = lax.axis_index("rad")
    ax = lax.axis_index("ax")
    R, Z, T = nat.shape[1], nat.shape[2], nat.shape[3]
    K = T // LANES
    wide = T // SUB
    pad = (LANES - wide) // 2
    half = SUB // 2
    near = min(2, Z - 2)
    far = 2 - near
    right, left = lax.rem(ax + 1, n_ax), lax.rem(ax + n_ax - 1, n_ax)
    has_lo, has_hi = rad > 0, rad < n_rad - 1
    first, last, second = ax == 0, ax == n_ax - 1, ax == n_ax - 2

    barrier = pltpu.get_barrier_semaphore()

    def greet(offset, to_rad):
        peer = (lax.rem(ax + offset + n_ax, n_ax), to_rad)
        pl.semaphore_signal(barrier, inc=1, device_id=peer, device_id_type=MESH)

    def greet_row(to_rad, offsets):
        for o in offsets:
            greet(o, to_rad)

    def greet_all(offsets, beside):
        greet_row(rad, offsets)
        pl.when(has_lo)(lambda: greet_row(rad - 1, offsets + beside))
        pl.when(has_hi)(lambda: greet_row(rad + 1, offsets + beside))

    greet_all((-1, -2), (0,))
    pl.when(ax + 1 < n_ax)(lambda: greet_all((1,), ()))
    pl.when(ax + 2 < n_ax)(lambda: greet_all((2,), ()))

    fetch = pltpu.make_async_copy(v_hbm, nat, sems.at[IN])
    fetch.start()
    fetch_map = pltpu.make_async_copy(map_hbm, map_ref, sems.at[IN + 1])
    fetch_map.start()

    distances = stages(n_ax)

    def tell(stage):
        d = distances[stage]
        for peer in (lax.rem(ax + d, n_ax), lax.rem(ax + n_ax - d, n_ax)):
            pl.semaphore_signal(ready.at[stage], inc=1, device_id=(peer, rad), device_id_type=MESH)

    def hear(stage):
        pl.semaphore_wait(ready.at[stage], 2)

    def drain(sem, amount):
        pltpu.make_async_copy(spare.at[pl.ds(0, amount)], spare.at[pl.ds(0, amount)], sems.at[sem]).wait()

    def send(src, dst, group, recv, to_ax, to_rad):
        pltpu.make_async_remote_copy(
            src_ref=src, dst_ref=dst, send_sem=sems.at[SEND + group], recv_sem=sems.at[recv],
            device_id=(to_ax, to_rad), device_id_type=MESH).start()

    beside_sum = jnp.where(has_lo, 1, 0) + jnp.where(has_hi, 1, 0)
    row_sum = 4 - jnp.where(first, 2, 0) - jnp.where(ax == 1, 1, 0)
    pl.semaphore_wait(barrier, row_sum * (1 + beside_sum) + beside_sum)

    def planes(first_z, count, dst, row, group, recv, to_ax):
        for r in range(R):
            send(v_hbm.at[:, r, pl.ds(first_z, count)], dst.at[:, pl.ds(2 * r + row, count)], group, recv, to_ax, rad)

    pl.when(last)(lambda: planes(Z - 2 - near, near, he, far, 0, ZL, right))
    planes(Z - 2, 2, hz.at[0], 0, 0, ZL, right)
    if far:
        pl.when(second)(lambda: planes(Z - far, far, he, 0, 0, ZL, lax.rem(ax + 2, n_ax)))
    pl.when(ax > 0)(lambda: planes(0, 2, hz.at[1], 0, 0, ZR, left))

    def rim(side, group, row, to_rad):
        send(v_hbm.at[:, row, pl.ds(Z - 1, 1)], hr.at[side, :, pl.ds(2, 1)], group, ROW + side, right, to_rad)

        @pl.when(last)
        def _():
            send(v_hbm.at[:, row, pl.ds(Z - 3, 2)], hr.at[side, :, pl.ds(0, 2)], group, ROW + side, right, to_rad)

        @pl.when(ax > 0)
        def _():
            send(v_hbm.at[:, row, pl.ds(0, 1)], hr.at[side, :, pl.ds(Z + 3, 1)], group, ROW + side, left, to_rad)

        send(v_hbm.at[:, row], hr.at[side, :, pl.ds(3, Z)], group, ROW + side, ax, to_rad)

    pl.when(has_hi)(lambda: rim(0, 1, R - 1, rad + 1))
    pl.when(has_lo)(lambda: rim(1, 2, 0, rad - 1))
    pl.when(ax > 1)(lambda: tell(0))

    def row_of(b, c, r, i):
        line, pairs = c * R + r - 1, 3 * R * 2
        if b:
            k = i - Z + 2
            return (3 * R * Z + pairs * (2 + k // 2) + line * 2 + k % 2) * SUB
        if 2 <= i < Z + 2:
            return (line * Z + i - 2) * SUB
        return (3 * R * Z + (line * 2 + i if i < 2 else pairs + line * 2 + i - Z - 2)) * SUB

    def rim_of(b, c, r, i):
        return ((c * 2 + (0 if r == 0 else 1)) * (Z + 4) + i + 1 - b * Z) * SUB

    def place(b, c, r, i):
        inside = 0 < r <= R
        return (ext, row_of(b, c, r, i)) if inside else (rims, rim_of(b, c, r, i))

    def get(b, c, r, i, n):
        blocks = []
        for k in range(n):
            ref, row = place(b, c, r, i + k)
            blocks.append(ref[row : row + SUB, :])
        return jnp.stack(blocks)

    def put(b, c, r, i, x):
        ref, row = place(b, c, r, i)
        ref[row : row + SUB, :] = x

    def unpack(x, target):
        ref, row = target
        for s, piece in enumerate(segments(tiles_of(x), wide, pad)):
            ref[pl.ds(row + s, x.shape[0], stride=SUB), :] = piece

    lane = lax.broadcasted_iota(jnp.int32, (SUB, LANES), 1)
    steps = []
    while 2 ** len(steps) < MOSTSEG:
        steps.append(2 ** len(steps))
    S = len(steps)

    def spread(ring, x):
        total, rest = x, x
        for k, d in enumerate(steps):
            total = total + masks[ring, k] * roll(total, d, x.ndim - 1)
            rest = rest + masks[ring, S + k] * roll(rest, -d, x.ndim - 1)
        return total + rest - x

    def coarsen(places, count):
        values = [jnp.concatenate([get(b, c, r, i, count) for c in range(3)], axis=0) for _, b, r, i in places]
        total, rest = list(values), list(values)
        for k, d in enumerate(steps):
            for j, (ring, _, _, _) in enumerate(places):
                total[j] = total[j] + masks[ring, k] * roll(total[j], d, 2)
            for j, (ring, _, _, _) in enumerate(places):
                rest[j] = rest[j] + masks[ring, S + k] * roll(rest[j], -d, 2)
        means = [(t + q - x) * masks[p[0], 2 * S] for t, q, x, p in zip(total, rest, values, places)]
        lows = [roll(m, -wide, 2) for m in means]
        highs = [roll(m, wide, 2) for m in means]
        lows, highs = [roll(m, 1, 1) for m in lows], [roll(m, -1, 1) for m in highs]
        for mean, low, high, (_, b, r, i) in zip(means, lows, highs, places):
            mean = jnp.where(lane < pad, low, mean)
            mean = jnp.where(lane >= pad + wide, high, mean)
            for c in range(3):
                for k in range(count):
                    put(b, c, r, i + k, mean[c * count + k])

    def coarsen_block(b, first_i, count):
        @pl.when(rad == 0)
        def _():
            coarsen([(r, b, r + 1, first_i) for r in range(NRING)], count)

    def coarsen_below(first_i, count):
        if R == NRING:
            @pl.when(rad == 1)
            def _():
                coarsen([(R - 1, 0, 0, first_i)], count)

    fetch_map.wait()

    @pl.when(rad <= (1 if R == NRING else 0))
    def _():
        labels = map_ref[...].astype(jnp.float32)
        for s, piece in enumerate(segments(tiles_of(labels), wide, pad)):
            maps[pl.ds(s, NRING, stride=SUB), :] = piece
        for ring in range(NRING):
            label = maps[ring * SUB : (ring + 1) * SUB, :]
            for k, d in enumerate(steps):
                masks[ring, k] = (roll(label, d, 1) == label).astype(jnp.float32)
                masks[ring, S + k] = (roll(label, -d, 1) == label).astype(jnp.float32)
            masks[ring, 2 * S] = 1.0 / spread(ring, jnp.ones((SUB, LANES), jnp.float32))

    fetch.wait()
    for c in range(3):
        for r in range(R):
            unpack(nat[c, r], place(0, c, r + 1, 2))
    coarsen_block(0, 2, Z)

    def turns_of(b, i, count):
        z = i + 2 - b * Z
        for r in range(1, R + 1):
            for c in range(3):
                x = get(b, c, r, i, count)
                after, before = up(x), down(x)
                around[c, r - 1, z : z + count] = (after + before) + (x + x)
                slope[c, r - 1, z : z + count] = after - before

    def products_of(b, i, count):
        z = i + 2 - b * Z
        for r in range(1, R + 1):
            x = [get(b, c, r, i, count) for c in range(3)]
            for p, (c, a) in enumerate(PAIRS):
                paired[p, r - 1, z : z + count] = smooth_t(x[c] * x[a])

    def local(b, low_z):
        n, z = Z - low_z, low_z + 4 - b * Z
        for r in range(1, R + 1):
            filtered = []
            for c in range(3):
                filtered.append(smooth_z(around[c, r - 1, z - 2 : z + n + 2]))
                wsc[b, c, r, 0 : n + 2] = filtered[c]
            for p, (c, a) in enumerate(PAIRS):
                product = smooth_z(paired[p, r - 1, z - 1 : z + n + 1])
                lsc[b, p, r - 1, 0:n] = 16.0 * product - filtered[c][1:-1] * filtered[a][1:-1]

    @pl.when(ax < 2)
    def _():
        hear(0)
        tell(0)

    @pl.when(first)
    def _():
        planes(0, 2, hl, 0, 0, LATE, left)
        pl.when(has_hi)(lambda: send(v_hbm.at[:, R - 1, pl.ds(0, 1)], hc.at[0], 1, LATE + 1, left, rad + 1))
        pl.when(has_lo)(lambda: send(v_hbm.at[:, 0, pl.ds(0, 1)], hc.at[1], 2, LATE + 2, left, rad - 1))

    def axis_end(b, first_i, count):
        for c in range(3):
            for i in range(first_i, first_i + count):
                put(b, c, 0, i, SIGNS[c] * roll(get(b, c, 1, i, 1)[0], half, 0))

    def wall_end():
        for c in range(3):
            for i in range(-1, Z + 3):
                put(0, c, R + 1, i, jnp.zeros((SUB, LANES), jnp.float32))

    def strain(b, low_z, high_z, rows):
        n, i0 = high_z - low_z, low_z + 2
        z = low_z + 4 - b * Z
        for r in rows:
            grads = []
            for c in range(3):
                long = get(b, c, r, i0 - 2, n + 4)
                grads.append([
                    long[2:] - long[:-2],
                    get(b, c, r + 1, i0 - 1, n + 2) - get(b, c, r - 1, i0 - 1, n + 2),
                    slope[c, r - 1, z - 1 : z + n + 1],
                ])
            terms, size = tensor(grads)
            for p in range(6):
                flux[b, p, r - 1, 0 : n + 2] = size * terms[p]

    def outside(b, low_z, r):
        n, i0 = Z - low_z, low_z + 2
        for c in range(3):
            wsc[b, c, r, 1 : n + 1] = smooth_t(smooth_z(get(b, c, r, i0 - 1, n + 2)))

    def collect(b, low_z, high_z, rows):
        n = high_z - low_z
        for r in rows:
            grads = []
            for c in range(3):
                mid = wsc[b, c, r, 1 : n + 1]
                grads.append([
                    wsc[b, c, r, 2 : n + 2] - wsc[b, c, r, 0:n],
                    wsc[b, c, r + 1, 1 : n + 1] - wsc[b, c, r - 1, 1 : n + 1],
                    up(mid) - down(mid),
                ])
            terms, size = tensor(grads)
            size = 0.25 * size
            sums = [[0.0, 0.0], [0.0, 0.0]]
            for p, (c, a) in enumerate(PAIRS):
                model = smooth_t(smooth_z(flux[b, p, r - 1, 0 : n + 2])) - size * terms[p]
                kind = sums[0 if c == a else 1]
                kind[0] = kind[0] + lsc[b, p, r - 1, 0:n] * model
                kind[1] = kind[1] + model * model
            for k in range(2):
                each_z = sums[0][k] + 2.0 * sums[1][k]
                if b:
                    acc[k, r - 1] = acc[k, r - 1] + jnp.sum(each_z, axis=0)
                else:
                    rest = jnp.sum(each_z[Z - 2 :], axis=0)
                    acc[k, r - 1] = acc[k, r - 1] + jnp.sum(each_z[: Z - 2], axis=0) + jnp.where(last, 0.0, rest)

    def sums_of(b, low_z, rows):
        strain(b, low_z, Z, rows)
        collect(b, low_z, Z, rows)

    turns_of(0, 2, Z)
    products_of(0, 2, Z)
    block = 3 * R * K
    acc[...] = jnp.zeros(acc.shape, jnp.float32)

    @pl.when(first)
    def _():
        drain(ZL, block * 4)
        for c in range(3):
            unpack(he[c], place(1, c, 1, Z - 2))
            unpack(hz[0, c], place(1, c, 1, Z))
        coarsen_block(1, Z - 2, 2)
        coarsen_block(1, Z, 2)
        for c in range(3):
            for r in range(1, R + 1):
                for i in range(2):
                    put(0, c, r, i, get(1, c, r, Z + i, 1)[0])
                    put(1, c, r, Z + 2 + i, get(0, c, r, 2 + i, 1)[0])
        turns_of(1, Z - 2, 4)
        products_of(1, Z - 1, 3)
        local(1, Z - 2)
        sums_of(1, Z - 2, range(2, R))

    @pl.when(ax > 0)
    def _():
        drain(ZL, block * 2)
        for c in range(3):
            unpack(hz[0, c], place(0, c, 1, 0))
        coarsen_block(0, 0, 2)
        turns_of(0, 0, 2)
        products_of(0, 1, 1)

    @pl.when(ax < n_ax - 1)
    def _():
        drain(ZR, block * 2)
        for c in range(3):
            unpack(hz[1, c], place(0, c, 1, Z + 2))
        coarsen_block(0, Z + 2, 2)
        turns_of(0, Z + 2, 2)
        products_of(0, Z + 2, 1)

    local(0, 0)
    sums_of(0, 0, range(2, R))

    def rim_in(side, row):
        line = 3 * K
        pl.when(first)(lambda: drain(ROW + side, line * (Z + 4)))
        pl.when(last)(lambda: drain(ROW + side, line * (Z + 1)))
        pl.when((ax > 0) & (ax < n_ax - 1))(lambda: drain(ROW + side, line * (Z + 2)))
        for c in range(3):
            unpack(hr[side, c], place(0, c, row, -1))

    def edge_out(row, end, to_rad):
        group, slot = (2, EDGE + 1) if row == 1 else (1, EDGE)
        send(hx.at[:, row], hx.at[:, end], group, slot, ax, to_rad)

    def edge_rows(row):
        for c in range(3):
            hx[c, row] = flux[0, pair(c, 1), row - 1, 1 : Z + 1]
        if row == 1:
            pl.when(has_lo)(lambda: edge_out(1, R + 1, rad - 1))
        else:
            pl.when(has_hi)(lambda: edge_out(R, 0, rad + 1))

    def finish(row, beyond):
        strain(0, 0, Z, (row,))
        pl.when(ax < n_ax - 1)(lambda: edge_rows(row))

        @pl.when(first)
        def _():
            outside(1, Z - 2, beyond)
            sums_of(1, Z - 2, (row,))

        outside(0, 0, beyond)
        collect(0, 0, Z, (row,))

    pl.when(has_lo)(lambda: rim_in(0, 0))
    coarsen_below(-1, Z + 4)

    @pl.when(rad == 0)
    def _():
        axis_end(0, 1, Z + 2)
        pl.when(first)(lambda: axis_end(1, Z - 1, 2))

    finish(1, 0)
    pl.when(has_hi)(lambda: rim_in(1, R + 1))
    pl.when(rad == n_rad - 1)(wall_end)
    finish(R, R + 1)

    sub_index = lax.broadcasted_iota(jnp.int32, (SUB, LANES), 0)
    lane_index = lax.broadcasted_iota(jnp.int32, (SUB, LANES), 1)
    mine = jnp.zeros((SUB, LANES), jnp.float32)
    for r in range(R):
        for k in range(2):
            row = jnp.sum(acc[k, r], axis=0, keepdims=True) * (2.0 ** -15, 2.0 ** -14)[k]
            mine = jnp.where(sub_index == k * half + r, row, mine)
    mine = jnp.where((lane_index >= pad) & (lane_index < pad + wide), mine, 0.0)
    fold = LANES // 2
    while fold >= LANES // SUB:
        mine = mine + roll(mine, fold, 1)
        fold //= 2
    group = lane_index // (LANES // SUB) == sub_index
    part[...] = jnp.sum(jnp.where(group, mine, 0.0), axis=0, keepdims=True)

    def sums(side, i):
        peer = lax.rem(ax + i, n_ax)
        send(part, parts.at[(1 - side) * n_ax + ax], (0, 1, 2)[side], SUMS + 1 - side, peer, rad + side)

    def sums_in(side, amount):
        pltpu.make_async_copy(parts.at[pl.ds(0, amount)], parts.at[pl.ds(0, amount)], sems.at[SUMS + 1 + side]).wait()

    def first_of(side):
        return 1 if side == 0 else 0

    def send_sums(side):
        start = first_of(side)
        each(n_ax - start, lambda i: sums(side, i + start))

    pl.when(ax > 1)(lambda: hear(0))
    for stage in range(1, len(distances)):
        tell(stage)
        hear(stage)
    send_sums(0)
    pl.when(has_lo)(lambda: send_sums(-1))
    pl.when(has_hi)(lambda: send_sums(1))

    @pl.when(last)
    def _():
        drain(LATE, block * 2)
        for c in range(3):
            unpack(hl[c], place(0, c, 1, Z + 2))
        coarsen_block(0, Z + 2, 2)

        @pl.when(has_lo)
        def _():
            drain(LATE + 1, 3 * K)
            for c in range(3):
                unpack(hc[0, c], place(0, c, 0, Z + 2))

        @pl.when(has_hi)
        def _():
            drain(LATE + 2, 3 * K)
            for c in range(3):
                unpack(hc[1, c], place(0, c, R + 1, Z + 2))

        coarsen_below(Z + 2, 1)
        pl.when(rad == 0)(lambda: axis_end(0, Z + 2, 1))
        for r in range(1, R + 1):
            grads = []
            for c in range(3):
                long = get(0, c, r, Z, 4)
                mid = long[1:-1]
                grads.append([
                    long[2:] - long[:-2],
                    get(0, c, r + 1, Z + 1, 2) - get(0, c, r - 1, Z + 1, 2),
                    up(mid) - down(mid),
                ])
            terms, size = tensor(grads)
            for p in range(6):
                flux[0, p, r - 1, Z : Z + 2] = size * terms[p]

    @pl.when(last)
    def _():
        edge_rows(1)
        edge_rows(R)

    for c in range(3):
        hx[c, 2:R] = flux[0, pair(c, 1), 1 : R - 1, 1 : Z + 1]

    @pl.when(rad == 0)
    def _():
        for c in range(3):
            for z in range(Z):
                hx[c, 0, z] = SIGNS[c] * SIGNS[1] * roll(hx[c, 1, z], half, 0)

    @pl.when(rad == n_rad - 1)
    def _():
        for c in range(3):
            for z in range(Z):
                hx[c, R + 1, z] = jnp.zeros((SUB, LANES), jnp.float32)

    bases, turns = [[], [], []], [[], [], []]
    for r in range(1, R + 1):
        for c in range(3):
            axial = get(0, c, r, 1, Z + 2) * get(0, 0, r, 1, Z + 2)
            outer = get(0, c, r + 1, 2, Z) * get(0, 1, r + 1, 2, Z)
            inner = get(0, c, r - 1, 2, Z) * get(0, 1, r - 1, 2, Z)
            mid = get(0, c, r, 2, Z)
            spin = mid * get(0, 2, r, 2, Z)
            change = axial[2:] - axial[:-2] + (outer - inner) + (up(spin) - down(spin))
            bases[c].append(mid - 0.5 * change)
            turn = flux[0, pair(c, 2), r - 1, 1 : Z + 1]
            p = pair(c, 0)
            turns[c].append(flux[0, p, r - 1, 2 : Z + 2] - flux[0, p, r - 1, 0:Z] + (up(turn) - down(turn)))

    count = n_ax * Z * T
    sums_in(0, n_ax - 1)

    def coefficients(total):
        total = jnp.broadcast_to(jnp.sum(jnp.where(group, total, 0.0), axis=1, keepdims=True), (SUB, LANES)) / count
        return 0.125 * (total / (roll(total, -half, 0) + EPSILON))

    def total_of(side):
        start = first_of(side)
        total = part[...] if start else jnp.zeros((1, LANES), jnp.float32)
        if n_ax <= 16:
            for i in range(start, n_ax):
                total = total + parts[(1 + side) * n_ax + lax.rem(ax + i, n_ax)]
            return total
        return lax.fori_loop(
            start, n_ax, lambda i, t: t + parts[(1 + side) * n_ax + lax.rem(ax + i, n_ax)], total)

    coef = coefficients(total_of(0))

    def beside(side, row):
        sums_in(side, n_ax)
        edge_coef[0 if side < 0 else 1] = jnp.broadcast_to(
            coefficients(total_of(side))[row : row + 1], (SUB, LANES))

    pl.when(has_lo)(lambda: beside(-1, R - 1))
    pl.when(has_hi)(lambda: beside(1, 0))

    @pl.when(rad == 0)
    def _():
        edge_coef[0] = jnp.broadcast_to(coef[0:1], (SUB, LANES))

    @pl.when(rad == n_rad - 1)
    def _():
        edge_coef[1] = jnp.zeros((SUB, LANES), jnp.float32)

    pl.when(has_lo)(lambda: drain(EDGE, 3 * Z * SUB))
    pl.when(has_hi)(lambda: drain(EDGE + 1, 3 * Z * SUB))
    by_row = [edge_coef[0]] + [jnp.broadcast_to(coef[r : r + 1], (SUB, LANES)) for r in range(R)] + [edge_coef[1]]
    for c in range(3):
        for r in range(R):
            new = bases[c][r] + by_row[r + 1] * turns[c][r]
            new = new + (by_row[r + 2] * hx[c, r + 2] - by_row[r] * hx[c, r])
            for z in range(Z):
                row = ((c * R + r) * Z + z) * SUB
                res[row : row + SUB, :] = new[z]
    for c in range(3):
        for r in range(R):
            base = (c * R + r) * Z * SUB
            pieces = [res[pl.ds(base + s, Z, stride=SUB), :] for s in range(SUB)]
            for k, tile in enumerate(joined(pieces, wide, pad)):
                out_ref[c, r, :, k * LANES : (k + 1) * LANES] = tile

    middle = (ax > 0) & (ax < n_ax - 2)

    def sent(group, usual, for_first, for_last, for_second):
        pl.when(middle)(lambda: drain(SEND + group, usual))
        pl.when(first)(lambda: drain(SEND + group, for_first))
        pl.when(last)(lambda: drain(SEND + group, for_last))
        pl.when(second)(lambda: drain(SEND + group, for_second))

    line, total = 3 * K, n_ax - 1
    sent(0, 4 * block + total, 4 * block + total, (4 + near) * block + total, (4 + far) * block + total)
    total = 3 * Z * SUB + n_ax
    usual, more = line * (Z + 2) + total, line * (Z + 4) + total
    pl.when(has_hi)(lambda: sent(1, usual, usual, more, usual))
    pl.when(has_lo)(lambda: sent(2, usual, usual, more, usual))


def shards(n_ax, n_rad, velocity, cycle_map):
    _, R, Z, T = velocity.shape
    assert n_ax >= 8 and R >= NRING and Z >= 3

    def vmem(*shape):
        return pltpu.VMEM(shape, jnp.float32)

    return pl.pallas_call(
        functools.partial(kernel, n_ax, n_rad),
        out_shape=jax.ShapeDtypeStruct(velocity.shape, velocity.dtype),
        in_specs=[pl.BlockSpec(memory_space=pltpu.HBM)] * 2,
        out_specs=pl.BlockSpec(memory_space=pltpu.VMEM),
        scratch_shapes=[
            vmem(*velocity.shape),
            pltpu.VMEM(cycle_map.shape, jnp.int32),
            vmem(NRING * SUB, LANES),
            vmem(NRING, 2 * (MOSTSEG - 1).bit_length() + 1, SUB, LANES),
            vmem(3 * R * (Z + 10) * SUB, LANES),
            vmem(3 * 2 * (Z + 4) * SUB, LANES),
            vmem(2, 3, 2 * R, T),
            vmem(3, 2 * R, T),
            vmem(2, 3, Z + 4, T),
            vmem(3, 2 * R, T),
            vmem(2, 3, 1, T),
            vmem(2, 3, R + 2, Z + 2, SUB, LANES),
            vmem(2, 6, R, Z, SUB, LANES),
            vmem(3, R, Z + 6, SUB, LANES),
            vmem(3, R, Z + 6, SUB, LANES),
            vmem(6, R, Z + 6, SUB, LANES),
            vmem(2, 6, R, Z + 2, SUB, LANES),
            vmem(3, R + 2, Z, SUB, LANES),
            vmem(3 * R * Z * SUB, LANES),
            vmem(2, R, SUB, LANES),
            vmem(1, LANES),
            vmem(3 * n_ax, 1, LANES),
            vmem(2, SUB, LANES),
            vmem(3 * (R * 6 + Z) * SUB * (T // LANES) + 2 * n_ax, LANES),
            pltpu.SemaphoreType.REGULAR((len(stages(n_ax)),)),
            pltpu.SemaphoreType.DMA((SEMS,)),
        ],
        compiler_params=pltpu.CompilerParams(collective_id=0, has_side_effects=True, vmem_limit_bytes=8 << 20),
    )(*(pltpu.with_memory_space_constraint(x, pltpu.HBM) for x in (velocity, cycle_map)))


def solution(mesh):
    n_ax, n_rad = mesh.shape["ax"], mesh.shape["rad"]
    spec = P(None, "rad", "ax", None)
    body = functools.partial(shards, n_ax, n_rad)
    return jax.shard_map(body, mesh=mesh, in_specs=(spec, P()), out_specs=spec, check_vma=False)
```

```python
import functools

import jax
import jax.numpy as jnp
from jax import lax
from jax.experimental import pallas as pl
from jax.experimental.pallas import tpu as pltpu
from jax.sharding import PartitionSpec as P

NRING = 3
MOSTSEG = 16
SUB = 8
LANES = 128
PAIRS = ((0, 0), (1, 1), (2, 2), (0, 1), (0, 2), (1, 2))
SIGNS = (1.0, -1.0, -1.0)
EPSILON = 1e-06
MESH = pl.DeviceIdType.MESH
IN, SEND, ZL, ZR, ROW, LATE, EDGE, SUMS, SEMS = 0, 2, 5, 6, 7, 9, 12, 14, 17


def pair(a, b):
    return PAIRS.index((min(a, b), max(a, b)))


def each(count, body):
    if count <= 16:
        for i in range(count):
            body(i)
    else:
        lax.fori_loop(0, count, lambda i, c: (body(i), c)[1], 0)


def roll(x, shift, axis):
    size = x.shape[axis]
    return pltpu.roll(x, shift % size, axis)


def up(x):
    return roll(x, -1, x.ndim - 1)


def down(x):
    return roll(x, 1, x.ndim - 1)


def smooth_t(x):
    return (down(x) + up(x)) + (x + x)


def smooth_z(x):
    y = x[:-1] + x[1:]
    return y[:-1] + y[1:]


def tiles_of(x):
    return [x[:, k : k + LANES] for k in range(0, x.shape[1], LANES)]


def segments(x, wide, pad):
    rows, tiles = x[0].shape[0], len(x)
    total = tiles * LANES
    lane = lax.broadcasted_iota(jnp.int32, (rows, LANES), 1)
    pieces = []
    for s in range(SUB):
        start = (s * wide - pad) % total
        k, off = start // LANES, start % LANES
        first = x[k]
        if off:
            k2 = (k + 1) % tiles
            second = x[k2]
            first = jnp.where(lane < LANES - off, roll(first, -off, 1), roll(second, -off, 1))
        pieces.append(first)
    return pieces


def joined(pieces, wide, pad):
    rows = pieces[0].shape[0]
    lane = lax.broadcasted_iota(jnp.int32, (rows, LANES), 1)
    tiles = []
    for k in range(SUB * wide // LANES):
        lo, hi = k * LANES, (k + 1) * LANES
        s = lo // wide
        out = None
        while s * wide < hi:
            part = roll(pieces[s], s * wide - pad - lo, 1)
            out = part if out is None else jnp.where(lane >= s * wide - lo, part, out)
            s += 1
        tiles.append(out)
    return tiles


def tensor(grads):
    terms = [grads[c][c] + grads[c][c] if c == a else grads[c][a] + grads[a][c] for c, a in PAIRS]
    squares = [x * x for x in terms]
    total = 0.5 * (squares[0] + squares[1] + squares[2]) + (squares[3] + squares[4] + squares[5])
    return terms, jnp.sqrt(total)


def stages(n_ax):
    distances, reach = [], 2
    while reach < n_ax // 2:
        distances.append(reach)
        reach *= 2
    return distances


def kernel(n_ax, n_rad, v_hbm, map_hbm, out_ref, nat, map_ref, maps, masks, ext, rims, hz, he, hr, hl, hc, wsc,
           lsc, around, slope, paired, flux, hx, res, acc, part, parts, spare, ready, sems):
    rad = lax.axis_index("rad")
    ax = lax.axis_index("ax")
    R, Z, T = nat.shape[1], nat.shape[2], nat.shape[3]
    K = T // LANES
    wide = T // SUB
    pad = (LANES - wide) // 2
    half = SUB // 2
    near = min(2, Z - 2)
    far = 2 - near
    right, left = lax.rem(ax + 1, n_ax), lax.rem(ax + n_ax - 1, n_ax)
    has_lo, has_hi = rad > 0, rad < n_rad - 1
    first, last, second = ax == 0, ax == n_ax - 1, ax == n_ax - 2

    barrier = pltpu.get_barrier_semaphore()

    def greet(offset, to_rad):
        peer = (lax.rem(ax + offset + n_ax, n_ax), to_rad)
        pl.semaphore_signal(barrier, inc=1, device_id=peer, device_id_type=MESH)

    def greet_row(to_rad, offsets):
        for o in offsets:
            greet(o, to_rad)

    def greet_all(offsets, beside):
        greet_row(rad, offsets)
        pl.when(has_lo)(lambda: greet_row(rad - 1, offsets + beside))
        pl.when(has_hi)(lambda: greet_row(rad + 1, offsets + beside))

    greet_all((-1, -2), (0,))
    pl.when(ax + 1 < n_ax)(lambda: greet_all((1,), ()))
    pl.when(ax + 2 < n_ax)(lambda: greet_all((2,), ()))

    fetch = pltpu.make_async_copy(v_hbm, nat, sems.at[IN])
    fetch.start()
    fetch_map = pltpu.make_async_copy(map_hbm, map_ref, sems.at[IN + 1])
    fetch_map.start()

    distances = stages(n_ax)

    def tell(stage):
        d = distances[stage]
        for peer in (lax.rem(ax + d, n_ax), lax.rem(ax + n_ax - d, n_ax)):
            pl.semaphore_signal(ready.at[stage], inc=1, device_id=(peer, rad), device_id_type=MESH)

    def hear(stage):
        pl.semaphore_wait(ready.at[stage], 2)

    def drain(sem, amount):
        pltpu.make_async_copy(spare.at[pl.ds(0, amount)], spare.at[pl.ds(0, amount)], sems.at[sem]).wait()

    def send(src, dst, group, recv, to_ax, to_rad):
        pltpu.make_async_remote_copy(
            src_ref=src, dst_ref=dst, send_sem=sems.at[SEND + group], recv_sem=sems.at[recv],
            device_id=(to_ax, to_rad), device_id_type=MESH).start()

    beside_sum = jnp.where(has_lo, 1, 0) + jnp.where(has_hi, 1, 0)
    row_sum = 4 - jnp.where(first, 2, 0) - jnp.where(ax == 1, 1, 0)
    pl.semaphore_wait(barrier, row_sum * (1 + beside_sum) + beside_sum)

    def planes(first_z, count, dst, row, group, recv, to_ax):
        for r in range(R):
            send(v_hbm.at[:, r, pl.ds(first_z, count)], dst.at[:, pl.ds(2 * r + row, count)], group, recv, to_ax, rad)

    pl.when(last)(lambda: planes(Z - 2 - near, near, he, far, 0, ZL, right))
    planes(Z - 2, 2, hz.at[0], 0, 0, ZL, right)
    if far:
        pl.when(second)(lambda: planes(Z - far, far, he, 0, 0, ZL, lax.rem(ax + 2, n_ax)))
    pl.when(ax > 0)(lambda: planes(0, 2, hz.at[1], 0, 0, ZR, left))

    def rim(side, group, row, to_rad):
        send(v_hbm.at[:, row, pl.ds(Z - 1, 1)], hr.at[side, :, pl.ds(2, 1)], group, ROW + side, right, to_rad)

        @pl.when(last)
        def _():
            send(v_hbm.at[:, row, pl.ds(Z - 3, 2)], hr.at[side, :, pl.ds(0, 2)], group, ROW + side, right, to_rad)

        @pl.when(ax > 0)
        def _():
            send(v_hbm.at[:, row, pl.ds(0, 1)], hr.at[side, :, pl.ds(Z + 3, 1)], group, ROW + side, left, to_rad)

        send(v_hbm.at[:, row], hr.at[side, :, pl.ds(3, Z)], group, ROW + side, ax, to_rad)

    pl.when(has_hi)(lambda: rim(0, 1, R - 1, rad + 1))
    pl.when(has_lo)(lambda: rim(1, 2, 0, rad - 1))
    pl.when(ax > 1)(lambda: tell(0))

    def row_of(b, c, r, i):
        line, pairs = c * R + r - 1, 3 * R * 2
        if b:
            k = i - Z + 2
            return (3 * R * Z + pairs * (2 + k // 2) + line * 2 + k % 2) * SUB
        if 2 <= i < Z + 2:
            return (line * Z + i - 2) * SUB
        return (3 * R * Z + (line * 2 + i if i < 2 else pairs + line * 2 + i - Z - 2)) * SUB

    def rim_of(b, c, r, i):
        return ((c * 2 + (0 if r == 0 else 1)) * (Z + 4) + i + 1 - b * Z) * SUB

    def place(b, c, r, i):
        inside = 0 < r <= R
        return (ext, row_of(b, c, r, i)) if inside else (rims, rim_of(b, c, r, i))

    def get(b, c, r, i, n):
        blocks = []
        for k in range(n):
            ref, row = place(b, c, r, i + k)
            blocks.append(ref[row : row + SUB, :])
        return jnp.stack(blocks)

    def put(b, c, r, i, x):
        ref, row = place(b, c, r, i)
        ref[row : row + SUB, :] = x

    def unpack(x, target):
        ref, row = target
        for s, piece in enumerate(segments(tiles_of(x), wide, pad)):
            ref[pl.ds(row + s, x.shape[0], stride=SUB), :] = piece

    lane = lax.broadcasted_iota(jnp.int32, (SUB, LANES), 1)
    steps = []
    while 2 ** len(steps) < MOSTSEG:
        steps.append(2 ** len(steps))
    S = len(steps)

    def spread(ring, x):
        total, rest = x, x
        for k, d in enumerate(steps):
            total = total + masks[ring, k] * roll(total, d, x.ndim - 1)
            rest = rest + masks[ring, S + k] * roll(rest, -d, x.ndim - 1)
        return total + rest - x

    def coarsen(places, count):
        values = [jnp.concatenate([get(b, c, r, i, count) for c in range(3)], axis=0) for _, b, r, i in places]
        total, rest = list(values), list(values)
        for k, d in enumerate(steps):
            for j, (ring, _, _, _) in enumerate(places):
                total[j] = total[j] + masks[ring, k] * roll(total[j], d, 2)
            for j, (ring, _, _, _) in enumerate(places):
                rest[j] = rest[j] + masks[ring, S + k] * roll(rest[j], -d, 2)
        means = [(t + q - x) * masks[p[0], 2 * S] for t, q, x, p in zip(total, rest, values, places)]
        lows = [roll(m, -wide, 2) for m in means]
        highs = [roll(m, wide, 2) for m in means]
        lows, highs = [roll(m, 1, 1) for m in lows], [roll(m, -1, 1) for m in highs]
        for mean, low, high, (_, b, r, i) in zip(means, lows, highs, places):
            mean = jnp.where(lane < pad, low, mean)
            mean = jnp.where(lane >= pad + wide, high, mean)
            for c in range(3):
                for k in range(count):
                    put(b, c, r, i + k, mean[c * count + k])

    def coarsen_block(b, first_i, count):
        @pl.when(rad == 0)
        def _():
            coarsen([(r, b, r + 1, first_i) for r in range(NRING)], count)

    def coarsen_below(first_i, count):
        if R == NRING:
            @pl.when(rad == 1)
            def _():
                coarsen([(R - 1, 0, 0, first_i)], count)

    fetch_map.wait()

    @pl.when(rad <= (1 if R == NRING else 0))
    def _():
        labels = map_ref[...].astype(jnp.float32)
        for s, piece in enumerate(segments(tiles_of(labels), wide, pad)):
            maps[pl.ds(s, NRING, stride=SUB), :] = piece
        for ring in range(NRING):
            label = maps[ring * SUB : (ring + 1) * SUB, :]
            for k, d in enumerate(steps):
                masks[ring, k] = (roll(label, d, 1) == label).astype(jnp.float32)
                masks[ring, S + k] = (roll(label, -d, 1) == label).astype(jnp.float32)
            masks[ring, 2 * S] = 1.0 / spread(ring, jnp.ones((SUB, LANES), jnp.float32))

    fetch.wait()
    for c in range(3):
        for r in range(R):
            unpack(nat[c, r], place(0, c, r + 1, 2))
    coarsen_block(0, 2, Z)

    def turns_of(b, i, count):
        z = i + 2 - b * Z
        for r in range(1, R + 1):
            for c in range(3):
                x = get(b, c, r, i, count)
                after, before = up(x), down(x)
                around[c, r - 1, z : z + count] = (after + before) + (x + x)
                slope[c, r - 1, z : z + count] = after - before

    def products_of(b, i, count):
        z = i + 2 - b * Z
        for r in range(1, R + 1):
            x = [get(b, c, r, i, count) for c in range(3)]
            for p, (c, a) in enumerate(PAIRS):
                paired[p, r - 1, z : z + count] = smooth_t(x[c] * x[a])

    def local(b, low_z):
        n, z = Z - low_z, low_z + 4 - b * Z
        for r in range(1, R + 1):
            filtered = []
            for c in range(3):
                filtered.append(smooth_z(around[c, r - 1, z - 2 : z + n + 2]))
                wsc[b, c, r, 0 : n + 2] = filtered[c]
            for p, (c, a) in enumerate(PAIRS):
                product = smooth_z(paired[p, r - 1, z - 1 : z + n + 1])
                lsc[b, p, r - 1, 0:n] = 16.0 * product - filtered[c][1:-1] * filtered[a][1:-1]

    @pl.when(ax < 2)
    def _():
        hear(0)
        tell(0)

    @pl.when(first)
    def _():
        planes(0, 2, hl, 0, 0, LATE, left)
        pl.when(has_hi)(lambda: send(v_hbm.at[:, R - 1, pl.ds(0, 1)], hc.at[0], 1, LATE + 1, left, rad + 1))
        pl.when(has_lo)(lambda: send(v_hbm.at[:, 0, pl.ds(0, 1)], hc.at[1], 2, LATE + 2, left, rad - 1))

    def axis_end(b, first_i, count):
        for c in range(3):
            for i in range(first_i, first_i + count):
                put(b, c, 0, i, SIGNS[c] * roll(get(b, c, 1, i, 1)[0], half, 0))

    def wall_end():
        for c in range(3):
            for i in range(-1, Z + 3):
                put(0, c, R + 1, i, jnp.zeros((SUB, LANES), jnp.float32))

    def strain(b, low_z, high_z, rows):
        n, i0 = high_z - low_z, low_z + 2
        z = low_z + 4 - b * Z
        for r in rows:
            grads = []
            for c in range(3):
                long = get(b, c, r, i0 - 2, n + 4)
                grads.append([
                    long[2:] - long[:-2],
                    get(b, c, r + 1, i0 - 1, n + 2) - get(b, c, r - 1, i0 - 1, n + 2),
                    slope[c, r - 1, z - 1 : z + n + 1],
                ])
            terms, size = tensor(grads)
            for p in range(6):
                flux[b, p, r - 1, 0 : n + 2] = size * terms[p]

    def outside(b, low_z, r):
        n, i0 = Z - low_z, low_z + 2
        for c in range(3):
            wsc[b, c, r, 1 : n + 1] = smooth_t(smooth_z(get(b, c, r, i0 - 1, n + 2)))

    def collect(b, low_z, high_z, rows):
        n = high_z - low_z
        for r in rows:
            grads = []
            for c in range(3):
                mid = wsc[b, c, r, 1 : n + 1]
                grads.append([
                    wsc[b, c, r, 2 : n + 2] - wsc[b, c, r, 0:n],
                    wsc[b, c, r + 1, 1 : n + 1] - wsc[b, c, r - 1, 1 : n + 1],
                    up(mid) - down(mid),
                ])
            terms, size = tensor(grads)
            size = 0.25 * size
            sums = [[0.0, 0.0], [0.0, 0.0]]
            for p, (c, a) in enumerate(PAIRS):
                model = smooth_t(smooth_z(flux[b, p, r - 1, 0 : n + 2])) - size * terms[p]
                kind = sums[0 if c == a else 1]
                kind[0] = kind[0] + lsc[b, p, r - 1, 0:n] * model
                kind[1] = kind[1] + model * model
            for k in range(2):
                each_z = sums[0][k] + 2.0 * sums[1][k]
                if b:
                    acc[k, r - 1] = acc[k, r - 1] + jnp.sum(each_z, axis=0)
                else:
                    rest = jnp.sum(each_z[Z - 2 :], axis=0)
                    acc[k, r - 1] = acc[k, r - 1] + jnp.sum(each_z[: Z - 2], axis=0) + jnp.where(last, 0.0, rest)

    def sums_of(b, low_z, rows):
        strain(b, low_z, Z, rows)
        collect(b, low_z, Z, rows)

    turns_of(0, 2, Z)
    products_of(0, 2, Z)
    block = 3 * R * K
    acc[...] = jnp.zeros(acc.shape, jnp.float32)

    @pl.when(first)
    def _():
        drain(ZL, block * 4)
        for c in range(3):
            unpack(he[c], place(1, c, 1, Z - 2))
            unpack(hz[0, c], place(1, c, 1, Z))
        coarsen_block(1, Z - 2, 2)
        coarsen_block(1, Z, 2)
        for c in range(3):
            for r in range(1, R + 1):
                for i in range(2):
                    put(0, c, r, i, get(1, c, r, Z + i, 1)[0])
                    put(1, c, r, Z + 2 + i, get(0, c, r, 2 + i, 1)[0])
        turns_of(1, Z - 2, 4)
        products_of(1, Z - 1, 3)
        local(1, Z - 2)
        sums_of(1, Z - 2, range(2, R))

    @pl.when(ax > 0)
    def _():
        drain(ZL, block * 2)
        for c in range(3):
            unpack(hz[0, c], place(0, c, 1, 0))
        coarsen_block(0, 0, 2)
        turns_of(0, 0, 2)
        products_of(0, 1, 1)

    @pl.when(ax < n_ax - 1)
    def _():
        drain(ZR, block * 2)
        for c in range(3):
            unpack(hz[1, c], place(0, c, 1, Z + 2))
        coarsen_block(0, Z + 2, 2)
        turns_of(0, Z + 2, 2)
        products_of(0, Z + 2, 1)

    local(0, 0)
    sums_of(0, 0, range(2, R))

    def rim_in(side, row):
        line = 3 * K
        pl.when(first)(lambda: drain(ROW + side, line * (Z + 4)))
        pl.when(last)(lambda: drain(ROW + side, line * (Z + 1)))
        pl.when((ax > 0) & (ax < n_ax - 1))(lambda: drain(ROW + side, line * (Z + 2)))
        for c in range(3):
            unpack(hr[side, c], place(0, c, row, -1))

    def edge_out(row, end, to_rad):
        group, slot = (2, EDGE + 1) if row == 1 else (1, EDGE)
        send(hx.at[:, row], hx.at[:, end], group, slot, ax, to_rad)

    def edge_rows(row):
        for c in range(3):
            hx[c, row] = flux[0, pair(c, 1), row - 1, 1 : Z + 1]
        if row == 1:
            pl.when(has_lo)(lambda: edge_out(1, R + 1, rad - 1))
        else:
            pl.when(has_hi)(lambda: edge_out(R, 0, rad + 1))

    def finish(row, beyond):
        strain(0, 0, Z, (row,))
        pl.when(ax < n_ax - 1)(lambda: edge_rows(row))

        @pl.when(first)
        def _():
            outside(1, Z - 2, beyond)
            sums_of(1, Z - 2, (row,))

        outside(0, 0, beyond)
        collect(0, 0, Z, (row,))

    pl.when(has_lo)(lambda: rim_in(0, 0))
    coarsen_below(1, Z + 2)
    pl.when(first)(lambda: coarsen_below(-1, 2))

    @pl.when(rad == 0)
    def _():
        axis_end(0, 1, Z + 2)
        pl.when(first)(lambda: axis_end(1, Z - 1, 2))

    finish(1, 0)
    pl.when(has_hi)(lambda: rim_in(1, R + 1))
    pl.when(rad == n_rad - 1)(wall_end)
    finish(R, R + 1)

    sub_index = lax.broadcasted_iota(jnp.int32, (SUB, LANES), 0)
    lane_index = lax.broadcasted_iota(jnp.int32, (SUB, LANES), 1)
    mine = jnp.zeros((SUB, LANES), jnp.float32)
    for r in range(R):
        for k in range(2):
            row = jnp.sum(acc[k, r], axis=0, keepdims=True) * (2.0 ** -15, 2.0 ** -14)[k]
            mine = jnp.where(sub_index == k * half + r, row, mine)
    mine = jnp.where((lane_index >= pad) & (lane_index < pad + wide), mine, 0.0)
    fold = LANES // 2
    while fold >= LANES // SUB:
        mine = mine + roll(mine, fold, 1)
        fold //= 2
    group = lane_index // (LANES // SUB) == sub_index
    part[...] = jnp.sum(jnp.where(group, mine, 0.0), axis=0, keepdims=True)
    parts[n_ax + ax] = part[...]

    def sums(side, i):
        peer = lax.rem(ax + i, n_ax)
        send(part, parts.at[(1 - side) * n_ax + ax], (0, 1, 2)[side], SUMS + 1 - side, peer, rad + side)

    def sums_in(side, amount):
        pltpu.make_async_copy(parts.at[pl.ds(0, amount)], parts.at[pl.ds(0, amount)], sems.at[SUMS + 1 + side]).wait()

    def first_of(side):
        return 1 if side == 0 else 0

    def send_sums(side):
        start = first_of(side)
        each(n_ax - start, lambda i: sums(side, i + start))

    pl.when(ax > 1)(lambda: hear(0))
    for stage in range(1, len(distances)):
        tell(stage)
        hear(stage)
    send_sums(0)
    pl.when(has_lo)(lambda: send_sums(-1))
    pl.when(has_hi)(lambda: send_sums(1))

    @pl.when(last)
    def _():
        drain(LATE, block * 2)
        for c in range(3):
            unpack(hl[c], place(0, c, 1, Z + 2))
        coarsen_block(0, Z + 2, 2)

        @pl.when(has_lo)
        def _():
            drain(LATE + 1, 3 * K)
            for c in range(3):
                unpack(hc[0, c], place(0, c, 0, Z + 2))

        @pl.when(has_hi)
        def _():
            drain(LATE + 2, 3 * K)
            for c in range(3):
                unpack(hc[1, c], place(0, c, R + 1, Z + 2))

        coarsen_below(Z + 2, 1)
        pl.when(rad == 0)(lambda: axis_end(0, Z + 2, 1))
        for r in range(1, R + 1):
            grads = []
            for c in range(3):
                long = get(0, c, r, Z, 4)
                mid = long[1:-1]
                grads.append([
                    long[2:] - long[:-2],
                    get(0, c, r + 1, Z + 1, 2) - get(0, c, r - 1, Z + 1, 2),
                    up(mid) - down(mid),
                ])
            terms, size = tensor(grads)
            for p in range(6):
                flux[0, p, r - 1, Z : Z + 2] = size * terms[p]

    @pl.when(last)
    def _():
        edge_rows(1)
        edge_rows(R)

    for c in range(3):
        hx[c, 2:R] = flux[0, pair(c, 1), 1 : R - 1, 1 : Z + 1]

    @pl.when(rad == 0)
    def _():
        for c in range(3):
            for z in range(Z):
                hx[c, 0, z] = SIGNS[c] * SIGNS[1] * roll(hx[c, 1, z], half, 0)

    @pl.when(rad == n_rad - 1)
    def _():
        for c in range(3):
            for z in range(Z):
                hx[c, R + 1, z] = jnp.zeros((SUB, LANES), jnp.float32)

    bases, turns = [[], [], []], [[], [], []]
    for r in range(1, R + 1):
        for c in range(3):
            axial = get(0, c, r, 1, Z + 2) * get(0, 0, r, 1, Z + 2)
            outer = get(0, c, r + 1, 2, Z) * get(0, 1, r + 1, 2, Z)
            inner = get(0, c, r - 1, 2, Z) * get(0, 1, r - 1, 2, Z)
            mid = get(0, c, r, 2, Z)
            spin = mid * get(0, 2, r, 2, Z)
            change = axial[2:] - axial[:-2] + (outer - inner) + (up(spin) - down(spin))
            bases[c].append(mid - 0.5 * change)
            turn = flux[0, pair(c, 2), r - 1, 1 : Z + 1]
            p = pair(c, 0)
            turns[c].append(flux[0, p, r - 1, 2 : Z + 2] - flux[0, p, r - 1, 0:Z] + (up(turn) - down(turn)))

    count = n_ax * Z * T
    def coefficients(total):
        total = jnp.broadcast_to(jnp.sum(jnp.where(group, total, 0.0), axis=1, keepdims=True), (SUB, LANES)) / count
        return 0.125 * (total / (roll(total, -half, 0) + EPSILON))

    def total_of(side):
        terms = parts[pl.ds((1 + side) * n_ax, n_ax)]
        while terms.shape[0] % 2 == 0:
            terms = terms[: terms.shape[0] // 2] + terms[terms.shape[0] // 2 :]
        return jnp.sum(terms, axis=0)

    def spread_row(x):
        return jnp.broadcast_to(x, (SUB, LANES))

    pl.when(has_lo)(lambda: drain(EDGE, 3 * Z * SUB))
    pl.when(has_hi)(lambda: drain(EDGE + 1, 3 * Z * SUB))
    sums_in(0, n_ax - 1)
    pl.when(has_lo)(lambda: sums_in(-1, n_ax))
    pl.when(has_hi)(lambda: sums_in(1, n_ax))
    lower, coef, higher = [coefficients(total_of(side)) for side in (-1, 0, 1)]
    by_row = [spread_row(jnp.where(rad == 0, coef[0:1], lower[R - 1 : R]))]
    by_row = by_row + [spread_row(coef[r : r + 1]) for r in range(R)]
    by_row = by_row + [spread_row(jnp.where(rad == n_rad - 1, 0.0, higher[0:1]))]
    for c in range(3):
        for r in range(R):
            new = bases[c][r] + by_row[r + 1] * turns[c][r]
            new = new + (by_row[r + 2] * hx[c, r + 2] - by_row[r] * hx[c, r])
            for z in range(Z):
                row = ((c * R + r) * Z + z) * SUB
                res[row : row + SUB, :] = new[z]
    for c in range(3):
        for r in range(R):
            base = (c * R + r) * Z * SUB
            pieces = [res[pl.ds(base + s, Z, stride=SUB), :] for s in range(SUB)]
            for k, tile in enumerate(joined(pieces, wide, pad)):
                out_ref[c, r, :, k * LANES : (k + 1) * LANES] = tile

    middle = (ax > 0) & (ax < n_ax - 2)

    def sent(group, usual, for_first, for_last, for_second):
        pl.when(middle)(lambda: drain(SEND + group, usual))
        pl.when(first)(lambda: drain(SEND + group, for_first))
        pl.when(last)(lambda: drain(SEND + group, for_last))
        pl.when(second)(lambda: drain(SEND + group, for_second))

    line, total = 3 * K, n_ax - 1
    sent(0, 4 * block + total, 4 * block + total, (4 + near) * block + total, (4 + far) * block + total)
    total = 3 * Z * SUB + n_ax
    usual, more = line * (Z + 2) + total, line * (Z + 4) + total
    pl.when(has_hi)(lambda: sent(1, usual, usual, more, usual))
    pl.when(has_lo)(lambda: sent(2, usual, usual, more, usual))


def shards(n_ax, n_rad, velocity, cycle_map):
    _, R, Z, T = velocity.shape
    assert n_ax >= 8 and R >= NRING and Z >= 3

    def vmem(*shape):
        return pltpu.VMEM(shape, jnp.float32)

    return pl.pallas_call(
        functools.partial(kernel, n_ax, n_rad),
        out_shape=jax.ShapeDtypeStruct(velocity.shape, velocity.dtype),
        in_specs=[pl.BlockSpec(memory_space=pltpu.HBM)] * 2,
        out_specs=pl.BlockSpec(memory_space=pltpu.VMEM),
        scratch_shapes=[
            vmem(*velocity.shape),
            pltpu.VMEM(cycle_map.shape, jnp.int32),
            vmem(NRING * SUB, LANES),
            vmem(NRING, 2 * (MOSTSEG - 1).bit_length() + 1, SUB, LANES),
            vmem(3 * R * (Z + 10) * SUB, LANES),
            vmem(3 * 2 * (Z + 4) * SUB, LANES),
            vmem(2, 3, 2 * R, T),
            vmem(3, 2 * R, T),
            vmem(2, 3, Z + 4, T),
            vmem(3, 2 * R, T),
            vmem(2, 3, 1, T),
            vmem(2, 3, R + 2, Z + 2, SUB, LANES),
            vmem(2, 6, R, Z, SUB, LANES),
            vmem(3, R, Z + 6, SUB, LANES),
            vmem(3, R, Z + 6, SUB, LANES),
            vmem(6, R, Z + 6, SUB, LANES),
            vmem(2, 6, R, Z + 2, SUB, LANES),
            vmem(3, R + 2, Z, SUB, LANES),
            vmem(3 * R * Z * SUB, LANES),
            vmem(2, R, SUB, LANES),
            vmem(1, LANES),
            vmem(3 * n_ax, 1, LANES),
            vmem(3 * (R * 6 + Z) * SUB * (T // LANES) + 2 * n_ax, LANES),
            pltpu.SemaphoreType.REGULAR((len(stages(n_ax)),)),
            pltpu.SemaphoreType.DMA((SEMS,)),
        ],
        compiler_params=pltpu.CompilerParams(collective_id=0, has_side_effects=True, vmem_limit_bytes=8 << 20),
    )(*(pltpu.with_memory_space_constraint(x, pltpu.HBM) for x in (velocity, cycle_map)))


def solution(mesh):
    n_ax, n_rad = mesh.shape["ax"], mesh.shape["rad"]
    spec = P(None, "rad", "ax", None)
    body = functools.partial(shards, n_ax, n_rad)
    return jax.shard_map(body, mesh=mesh, in_specs=(spec, P()), out_specs=spec, check_vma=False)
```

```python
import functools

import jax
import jax.numpy as jnp
from jax import lax
from jax.experimental import pallas as pl
from jax.experimental.pallas import tpu as pltpu
from jax.sharding import PartitionSpec as P

NRING = 3
MOSTSEG = 16
SUB = 8
LANES = 128
PAIRS = ((0, 0), (1, 1), (2, 2), (0, 1), (0, 2), (1, 2))
SIGNS = (1.0, -1.0, -1.0)
EPSILON = 1e-06
MESH = pl.DeviceIdType.MESH
IN, SEND, ZL, ZR, ROW, LATE, EDGE, SUMS, SEMS = 0, 2, 5, 6, 7, 9, 12, 14, 17


def pair(a, b):
    return PAIRS.index((min(a, b), max(a, b)))


def each(count, body):
    if count <= 16:
        for i in range(count):
            body(i)
    else:
        lax.fori_loop(0, count, lambda i, c: (body(i), c)[1], 0)


def roll(x, shift, axis):
    size = x.shape[axis]
    return pltpu.roll(x, shift % size, axis)


def up(x):
    return roll(x, -1, x.ndim - 1)


def down(x):
    return roll(x, 1, x.ndim - 1)


def smooth_t(x):
    return (down(x) + up(x)) + (x + x)


def smooth_z(x):
    y = x[:-1] + x[1:]
    return y[:-1] + y[1:]


def tiles_of(x):
    return [x[:, k : k + LANES] for k in range(0, x.shape[1], LANES)]


def segments(x, wide, pad):
    rows, tiles = x[0].shape[0], len(x)
    total = tiles * LANES
    lane = lax.broadcasted_iota(jnp.int32, (rows, LANES), 1)
    pieces = []
    for s in range(SUB):
        start = (s * wide - pad) % total
        k, off = start // LANES, start % LANES
        first = x[k]
        if off:
            k2 = (k + 1) % tiles
            second = x[k2]
            first = jnp.where(lane < LANES - off, roll(first, -off, 1), roll(second, -off, 1))
        pieces.append(first)
    return pieces


def joined(pieces, wide, pad):
    rows = pieces[0].shape[0]
    lane = lax.broadcasted_iota(jnp.int32, (rows, LANES), 1)
    tiles = []
    for k in range(SUB * wide // LANES):
        lo, hi = k * LANES, (k + 1) * LANES
        s = lo // wide
        out = None
        while s * wide < hi:
            part = roll(pieces[s], s * wide - pad - lo, 1)
            out = part if out is None else jnp.where(lane >= s * wide - lo, part, out)
            s += 1
        tiles.append(out)
    return tiles


def tensor(grads):
    terms = [grads[c][c] + grads[c][c] if c == a else grads[c][a] + grads[a][c] for c, a in PAIRS]
    squares = [x * x for x in terms]
    total = 0.5 * (squares[0] + squares[1] + squares[2]) + (squares[3] + squares[4] + squares[5])
    return terms, jnp.sqrt(total)


def stages(n_ax):
    distances, reach = [], 2
    while reach < n_ax // 2:
        distances.append(reach)
        reach *= 2
    return distances


def kernel(n_ax, n_rad, v_hbm, map_hbm, out_ref, nat, map_ref, maps, masks, ext, rims, hz, he, hr, hl, hc, wsc,
           lsc, around, slope, paired, flux, hx, res, acc, part, parts, spare, ready, sems):
    rad = lax.axis_index("rad")
    ax = lax.axis_index("ax")
    R, Z, T = nat.shape[1], nat.shape[2], nat.shape[3]
    K = T // LANES
    wide = T // SUB
    pad = (LANES - wide) // 2
    half = SUB // 2
    near = min(2, Z - 2)
    far = 2 - near
    right, left = lax.rem(ax + 1, n_ax), lax.rem(ax + n_ax - 1, n_ax)
    has_lo, has_hi = rad > 0, rad < n_rad - 1
    first, last, second = ax == 0, ax == n_ax - 1, ax == n_ax - 2

    barrier = pltpu.get_barrier_semaphore()

    def greet(offset, to_rad):
        peer = (lax.rem(ax + offset + n_ax, n_ax), to_rad)
        pl.semaphore_signal(barrier, inc=1, device_id=peer, device_id_type=MESH)

    def greet_row(to_rad, offsets):
        for o in offsets:
            greet(o, to_rad)

    def greet_all(offsets, beside):
        greet_row(rad, offsets)
        pl.when(has_lo)(lambda: greet_row(rad - 1, offsets + beside))
        pl.when(has_hi)(lambda: greet_row(rad + 1, offsets + beside))

    greet_all((-1, -2), (0,))
    pl.when(ax + 1 < n_ax)(lambda: greet_all((1,), ()))
    pl.when(ax + 2 < n_ax)(lambda: greet_all((2,), ()))

    fetch = pltpu.make_async_copy(v_hbm, nat, sems.at[IN])
    fetch.start()
    fetch_map = pltpu.make_async_copy(map_hbm, map_ref, sems.at[IN + 1])
    fetch_map.start()

    distances = stages(n_ax)

    def tell(stage):
        d = distances[stage]
        for peer in (lax.rem(ax + d, n_ax), lax.rem(ax + n_ax - d, n_ax)):
            pl.semaphore_signal(ready.at[stage], inc=1, device_id=(peer, rad), device_id_type=MESH)

    def hear(stage):
        pl.semaphore_wait(ready.at[stage], 2)

    def drain(sem, amount):
        pltpu.make_async_copy(spare.at[pl.ds(0, amount)], spare.at[pl.ds(0, amount)], sems.at[sem]).wait()

    def send(src, dst, group, recv, to_ax, to_rad):
        pltpu.make_async_remote_copy(
            src_ref=src, dst_ref=dst, send_sem=sems.at[SEND + group], recv_sem=sems.at[recv],
            device_id=(to_ax, to_rad), device_id_type=MESH).start()

    beside_sum = jnp.where(has_lo, 1, 0) + jnp.where(has_hi, 1, 0)
    row_sum = 4 - jnp.where(first, 2, 0) - jnp.where(ax == 1, 1, 0)
    pl.semaphore_wait(barrier, row_sum * (1 + beside_sum) + beside_sum)

    def planes(src, first_z, count, dst, row, group, recv, to_ax):
        for r in range(R):
            send(src.at[:, r, pl.ds(first_z, count)], dst.at[:, pl.ds(2 * r + row, count)], group, recv, to_ax, rad)

    def rim(src, at_end, side, group, row, to_rad):
        send(src.at[:, row, pl.ds(Z - 1, 1)], hr.at[side, :, pl.ds(2, 1)], group, ROW + side, right, to_rad)
        if at_end:
            send(src.at[:, row, pl.ds(Z - 3, 2)], hr.at[side, :, pl.ds(0, 2)], group, ROW + side, right, to_rad)

        @pl.when(ax > 0)
        def _():
            send(src.at[:, row, pl.ds(0, 1)], hr.at[side, :, pl.ds(Z + 3, 1)], group, ROW + side, left, to_rad)

        send(src.at[:, row], hr.at[side, :, pl.ds(3, Z)], group, ROW + side, ax, to_rad)

    def halos(src, at_end):
        if at_end:
            planes(src, Z - 2 - near, near, he, far, 0, ZL, right)
        planes(src, Z - 2, 2, hz.at[0], 0, 0, ZL, right)
        if far and not at_end:
            pl.when(second)(lambda: planes(src, Z - far, far, he, 0, 0, ZL, lax.rem(ax + 2, n_ax)))
        pl.when(ax > 0)(lambda: planes(src, 0, 2, hz.at[1], 0, 0, ZR, left))
        pl.when(has_hi)(lambda: rim(src, at_end, 0, 1, R - 1, rad + 1))
        pl.when(has_lo)(lambda: rim(src, at_end, 1, 2, 0, rad - 1))

    pl.when(last)(lambda: halos(v_hbm, True))
    fetch.wait()
    pl.when(ax < n_ax - 1)(lambda: halos(nat, False))
    pl.when(ax > 1)(lambda: tell(0))

    def row_of(b, c, r, i):
        line, pairs = c * R + r - 1, 3 * R * 2
        if b:
            k = i - Z + 2
            return (3 * R * Z + pairs * (2 + k // 2) + line * 2 + k % 2) * SUB
        if 2 <= i < Z + 2:
            return (line * Z + i - 2) * SUB
        return (3 * R * Z + (line * 2 + i if i < 2 else pairs + line * 2 + i - Z - 2)) * SUB

    def rim_of(b, c, r, i):
        return ((c * 2 + (0 if r == 0 else 1)) * (Z + 4) + i + 1 - b * Z) * SUB

    def place(b, c, r, i):
        inside = 0 < r <= R
        return (ext, row_of(b, c, r, i)) if inside else (rims, rim_of(b, c, r, i))

    def get(b, c, r, i, n):
        blocks = []
        for k in range(n):
            ref, row = place(b, c, r, i + k)
            blocks.append(ref[row : row + SUB, :])
        return jnp.stack(blocks)

    def put(b, c, r, i, x):
        ref, row = place(b, c, r, i)
        ref[row : row + SUB, :] = x

    def unpack(x, target):
        ref, row = target
        for s, piece in enumerate(segments(tiles_of(x), wide, pad)):
            ref[pl.ds(row + s, x.shape[0], stride=SUB), :] = piece

    lane = lax.broadcasted_iota(jnp.int32, (SUB, LANES), 1)
    steps = []
    while 2 ** len(steps) < MOSTSEG:
        steps.append(2 ** len(steps))
    S = len(steps)

    def spread(ring, x):
        total, rest = x, x
        for k, d in enumerate(steps):
            total = total + masks[ring, k] * roll(total, d, x.ndim - 1)
            rest = rest + masks[ring, S + k] * roll(rest, -d, x.ndim - 1)
        return total + rest - x

    def coarsen(places, count):
        values = [jnp.concatenate([get(b, c, r, i, count) for c in range(3)], axis=0) for _, b, r, i in places]
        total, rest = list(values), list(values)
        for k, d in enumerate(steps):
            for j, (ring, _, _, _) in enumerate(places):
                total[j] = total[j] + masks[ring, k] * roll(total[j], d, 2)
            for j, (ring, _, _, _) in enumerate(places):
                rest[j] = rest[j] + masks[ring, S + k] * roll(rest[j], -d, 2)
        means = [(t + q - x) * masks[p[0], 2 * S] for t, q, x, p in zip(total, rest, values, places)]
        lows = [roll(m, -wide, 2) for m in means]
        highs = [roll(m, wide, 2) for m in means]
        lows, highs = [roll(m, 1, 1) for m in lows], [roll(m, -1, 1) for m in highs]
        for mean, low, high, (_, b, r, i) in zip(means, lows, highs, places):
            mean = jnp.where(lane < pad, low, mean)
            mean = jnp.where(lane >= pad + wide, high, mean)
            for c in range(3):
                for k in range(count):
                    put(b, c, r, i + k, mean[c * count + k])

    def coarsen_block(b, first_i, count):
        @pl.when(rad == 0)
        def _():
            coarsen([(r, b, r + 1, first_i) for r in range(NRING)], count)

    def coarsen_below(first_i, count):
        if R == NRING:
            @pl.when(rad == 1)
            def _():
                coarsen([(R - 1, 0, 0, first_i)], count)

    fetch_map.wait()

    @pl.when(rad <= (1 if R == NRING else 0))
    def _():
        labels = map_ref[...].astype(jnp.float32)
        for s, piece in enumerate(segments(tiles_of(labels), wide, pad)):
            maps[pl.ds(s, NRING, stride=SUB), :] = piece
        for ring in range(NRING):
            label = maps[ring * SUB : (ring + 1) * SUB, :]
            for k, d in enumerate(steps):
                masks[ring, k] = (roll(label, d, 1) == label).astype(jnp.float32)
                masks[ring, S + k] = (roll(label, -d, 1) == label).astype(jnp.float32)
            masks[ring, 2 * S] = 1.0 / spread(ring, jnp.ones((SUB, LANES), jnp.float32))

    for c in range(3):
        for r in range(R):
            unpack(nat[c, r], place(0, c, r + 1, 2))
    coarsen_block(0, 2, Z)

    def turns_of(b, i, count):
        z = i + 2 - b * Z
        for r in range(1, R + 1):
            for c in range(3):
                x = get(b, c, r, i, count)
                after, before = up(x), down(x)
                around[c, r - 1, z : z + count] = (after + before) + (x + x)
                slope[c, r - 1, z : z + count] = after - before

    def products_of(b, i, count):
        z = i + 2 - b * Z
        for r in range(1, R + 1):
            x = [get(b, c, r, i, count) for c in range(3)]
            for p, (c, a) in enumerate(PAIRS):
                paired[p, r - 1, z : z + count] = smooth_t(x[c] * x[a])

    def local(b, low_z):
        n, z = Z - low_z, low_z + 4 - b * Z
        for r in range(1, R + 1):
            filtered = []
            for c in range(3):
                filtered.append(smooth_z(around[c, r - 1, z - 2 : z + n + 2]))
                wsc[b, c, r, 0 : n + 2] = filtered[c]
            for p, (c, a) in enumerate(PAIRS):
                product = smooth_z(paired[p, r - 1, z - 1 : z + n + 1])
                lsc[b, p, r - 1, 0:n] = 16.0 * product - filtered[c][1:-1] * filtered[a][1:-1]

    @pl.when(ax < 2)
    def _():
        hear(0)
        tell(0)

    @pl.when(first)
    def _():
        planes(nat, 0, 2, hl, 0, 0, LATE, left)
        pl.when(has_hi)(lambda: send(nat.at[:, R - 1, pl.ds(0, 1)], hc.at[0], 1, LATE + 1, left, rad + 1))
        pl.when(has_lo)(lambda: send(nat.at[:, 0, pl.ds(0, 1)], hc.at[1], 2, LATE + 2, left, rad - 1))

    def axis_end(b, first_i, count):
        for c in range(3):
            for i in range(first_i, first_i + count):
                put(b, c, 0, i, SIGNS[c] * roll(get(b, c, 1, i, 1)[0], half, 0))

    def wall_end():
        for c in range(3):
            for i in range(-1, Z + 3):
                put(0, c, R + 1, i, jnp.zeros((SUB, LANES), jnp.float32))

    def strain(b, low_z, high_z, rows):
        n, i0 = high_z - low_z, low_z + 2
        z = low_z + 4 - b * Z
        for r in rows:
            grads = []
            for c in range(3):
                long = get(b, c, r, i0 - 2, n + 4)
                grads.append([
                    long[2:] - long[:-2],
                    get(b, c, r + 1, i0 - 1, n + 2) - get(b, c, r - 1, i0 - 1, n + 2),
                    slope[c, r - 1, z - 1 : z + n + 1],
                ])
            terms, size = tensor(grads)
            for p in range(6):
                flux[b, p, r - 1, 0 : n + 2] = size * terms[p]

    def outside(b, low_z, r):
        n, i0 = Z - low_z, low_z + 2
        for c in range(3):
            wsc[b, c, r, 1 : n + 1] = smooth_t(smooth_z(get(b, c, r, i0 - 1, n + 2)))

    def collect(b, low_z, high_z, rows):
        n = high_z - low_z
        for r in rows:
            grads = []
            for c in range(3):
                mid = wsc[b, c, r, 1 : n + 1]
                grads.append([
                    wsc[b, c, r, 2 : n + 2] - wsc[b, c, r, 0:n],
                    wsc[b, c, r + 1, 1 : n + 1] - wsc[b, c, r - 1, 1 : n + 1],
                    up(mid) - down(mid),
                ])
            terms, size = tensor(grads)
            size = 0.25 * size
            sums = [[0.0, 0.0], [0.0, 0.0]]
            for p, (c, a) in enumerate(PAIRS):
                model = smooth_t(smooth_z(flux[b, p, r - 1, 0 : n + 2])) - size * terms[p]
                kind = sums[0 if c == a else 1]
                kind[0] = kind[0] + lsc[b, p, r - 1, 0:n] * model
                kind[1] = kind[1] + model * model
            for k in range(2):
                each_z = sums[0][k] + 2.0 * sums[1][k]
                if b:
                    acc[k, r - 1] = acc[k, r - 1] + jnp.sum(each_z, axis=0)
                else:
                    rest = jnp.sum(each_z[Z - 2 :], axis=0)
                    acc[k, r - 1] = acc[k, r - 1] + jnp.sum(each_z[: Z - 2], axis=0) + jnp.where(last, 0.0, rest)

    def sums_of(b, low_z, rows):
        strain(b, low_z, Z, rows)
        collect(b, low_z, Z, rows)

    turns_of(0, 2, Z)
    products_of(0, 2, Z)
    block = 3 * R * K
    acc[...] = jnp.zeros(acc.shape, jnp.float32)

    @pl.when(first)
    def _():
        drain(ZL, block * 4)
        for c in range(3):
            unpack(he[c], place(1, c, 1, Z - 2))
            unpack(hz[0, c], place(1, c, 1, Z))
        coarsen_block(1, Z - 2, 2)
        coarsen_block(1, Z, 2)
        for c in range(3):
            for r in range(1, R + 1):
                for i in range(2):
                    put(0, c, r, i, get(1, c, r, Z + i, 1)[0])
                    put(1, c, r, Z + 2 + i, get(0, c, r, 2 + i, 1)[0])
        turns_of(1, Z - 2, 4)
        products_of(1, Z - 1, 3)
        local(1, Z - 2)
        sums_of(1, Z - 2, range(2, R))

    @pl.when(ax > 0)
    def _():
        drain(ZL, block * 2)
        for c in range(3):
            unpack(hz[0, c], place(0, c, 1, 0))
        coarsen_block(0, 0, 2)
        turns_of(0, 0, 2)
        products_of(0, 1, 1)

    @pl.when(ax < n_ax - 1)
    def _():
        drain(ZR, block * 2)
        for c in range(3):
            unpack(hz[1, c], place(0, c, 1, Z + 2))
        coarsen_block(0, Z + 2, 2)
        turns_of(0, Z + 2, 2)
        products_of(0, Z + 2, 1)

    local(0, 0)
    sums_of(0, 0, range(2, R))

    def rim_in(side, row):
        line = 3 * K
        pl.when(first)(lambda: drain(ROW + side, line * (Z + 4)))
        pl.when(last)(lambda: drain(ROW + side, line * (Z + 1)))
        pl.when((ax > 0) & (ax < n_ax - 1))(lambda: drain(ROW + side, line * (Z + 2)))
        for c in range(3):
            unpack(hr[side, c], place(0, c, row, -1))

    def edge_out(row, end, to_rad):
        group, slot = (2, EDGE + 1) if row == 1 else (1, EDGE)
        send(hx.at[:, row], hx.at[:, end], group, slot, ax, to_rad)

    def edge_rows(row):
        for c in range(3):
            hx[c, row] = flux[0, pair(c, 1), row - 1, 1 : Z + 1]
        if row == 1:
            pl.when(has_lo)(lambda: edge_out(1, R + 1, rad - 1))
        else:
            pl.when(has_hi)(lambda: edge_out(R, 0, rad + 1))

    def finish(row, beyond):
        strain(0, 0, Z, (row,))
        pl.when(ax < n_ax - 1)(lambda: edge_rows(row))

        @pl.when(first)
        def _():
            outside(1, Z - 2, beyond)
            sums_of(1, Z - 2, (row,))

        outside(0, 0, beyond)
        collect(0, 0, Z, (row,))

    pl.when(has_lo)(lambda: rim_in(0, 0))
    coarsen_below(1, Z + 2)
    pl.when(first)(lambda: coarsen_below(-1, 2))

    @pl.when(rad == 0)
    def _():
        axis_end(0, 1, Z + 2)
        pl.when(first)(lambda: axis_end(1, Z - 1, 2))

    finish(1, 0)
    pl.when(has_hi)(lambda: rim_in(1, R + 1))
    pl.when(rad == n_rad - 1)(wall_end)
    finish(R, R + 1)

    sub_index = lax.broadcasted_iota(jnp.int32, (SUB, LANES), 0)
    lane_index = lax.broadcasted_iota(jnp.int32, (SUB, LANES), 1)
    mine = jnp.zeros((SUB, LANES), jnp.float32)
    for r in range(R):
        for k in range(2):
            row = jnp.sum(acc[k, r], axis=0, keepdims=True) * (2.0 ** -15, 2.0 ** -14)[k]
            mine = jnp.where(sub_index == k * half + r, row, mine)
    mine = jnp.where((lane_index >= pad) & (lane_index < pad + wide), mine, 0.0)
    fold = LANES // 2
    while fold >= LANES // SUB:
        mine = mine + roll(mine, fold, 1)
        fold //= 2
    group = lane_index // (LANES // SUB) == sub_index
    part[...] = jnp.sum(jnp.where(group, mine, 0.0), axis=0, keepdims=True)
    parts[n_ax + ax] = part[...]

    def sums(side, i):
        peer = lax.rem(ax + i, n_ax)
        send(part, parts.at[(1 - side) * n_ax + ax], (0, 1, 2)[side], SUMS + 1 - side, peer, rad + side)

    def sums_in(side, amount):
        pltpu.make_async_copy(parts.at[pl.ds(0, amount)], parts.at[pl.ds(0, amount)], sems.at[SUMS + 1 + side]).wait()

    def first_of(side):
        return 1 if side == 0 else 0

    def send_sums(side):
        start = first_of(side)
        each(n_ax - start, lambda i: sums(side, i + start))

    pl.when(ax > 1)(lambda: hear(0))
    for stage in range(1, len(distances)):
        tell(stage)
        hear(stage)
    send_sums(0)
    pl.when(has_lo)(lambda: send_sums(-1))
    pl.when(has_hi)(lambda: send_sums(1))

    @pl.when(last)
    def _():
        drain(LATE, block * 2)
        for c in range(3):
            unpack(hl[c], place(0, c, 1, Z + 2))
        coarsen_block(0, Z + 2, 2)

        @pl.when(has_lo)
        def _():
            drain(LATE + 1, 3 * K)
            for c in range(3):
                unpack(hc[0, c], place(0, c, 0, Z + 2))

        @pl.when(has_hi)
        def _():
            drain(LATE + 2, 3 * K)
            for c in range(3):
                unpack(hc[1, c], place(0, c, R + 1, Z + 2))

        coarsen_below(Z + 2, 1)
        pl.when(rad == 0)(lambda: axis_end(0, Z + 2, 1))
        for r in range(1, R + 1):
            grads = []
            for c in range(3):
                long = get(0, c, r, Z, 4)
                mid = long[1:-1]
                grads.append([
                    long[2:] - long[:-2],
                    get(0, c, r + 1, Z + 1, 2) - get(0, c, r - 1, Z + 1, 2),
                    up(mid) - down(mid),
                ])
            terms, size = tensor(grads)
            for p in range(6):
                flux[0, p, r - 1, Z : Z + 2] = size * terms[p]

    @pl.when(last)
    def _():
        edge_rows(1)
        edge_rows(R)

    for c in range(3):
        hx[c, 2:R] = flux[0, pair(c, 1), 1 : R - 1, 1 : Z + 1]

    @pl.when(rad == 0)
    def _():
        for c in range(3):
            for z in range(Z):
                hx[c, 0, z] = SIGNS[c] * SIGNS[1] * roll(hx[c, 1, z], half, 0)

    @pl.when(rad == n_rad - 1)
    def _():
        for c in range(3):
            for z in range(Z):
                hx[c, R + 1, z] = jnp.zeros((SUB, LANES), jnp.float32)

    bases, turns = [[], [], []], [[], [], []]
    for r in range(1, R + 1):
        for c in range(3):
            axial = get(0, c, r, 1, Z + 2) * get(0, 0, r, 1, Z + 2)
            outer = get(0, c, r + 1, 2, Z) * get(0, 1, r + 1, 2, Z)
            inner = get(0, c, r - 1, 2, Z) * get(0, 1, r - 1, 2, Z)
            mid = get(0, c, r, 2, Z)
            spin = mid * get(0, 2, r, 2, Z)
            change = axial[2:] - axial[:-2] + (outer - inner) + (up(spin) - down(spin))
            bases[c].append(mid - 0.5 * change)
            turn = flux[0, pair(c, 2), r - 1, 1 : Z + 1]
            p = pair(c, 0)
            turns[c].append(flux[0, p, r - 1, 2 : Z + 2] - flux[0, p, r - 1, 0:Z] + (up(turn) - down(turn)))

    count = n_ax * Z * T
    def coefficients(total):
        total = jnp.broadcast_to(jnp.sum(jnp.where(group, total, 0.0), axis=1, keepdims=True), (SUB, LANES)) / count
        return 0.125 * (total / (roll(total, -half, 0) + EPSILON))

    def total_of(side):
        terms = parts[pl.ds((1 + side) * n_ax, n_ax)]
        while terms.shape[0] % 2 == 0:
            terms = terms[: terms.shape[0] // 2] + terms[terms.shape[0] // 2 :]
        return jnp.sum(terms, axis=0)

    def spread_row(x):
        return jnp.broadcast_to(x, (SUB, LANES))

    pl.when(has_lo)(lambda: drain(EDGE, 3 * Z * SUB))
    pl.when(has_hi)(lambda: drain(EDGE + 1, 3 * Z * SUB))
    sums_in(0, n_ax - 1)
    pl.when(has_lo)(lambda: sums_in(-1, n_ax))
    pl.when(has_hi)(lambda: sums_in(1, n_ax))
    lower, coef, higher = [coefficients(total_of(side)) for side in (-1, 0, 1)]
    by_row = [spread_row(jnp.where(rad == 0, coef[0:1], lower[R - 1 : R]))]
    by_row = by_row + [spread_row(coef[r : r + 1]) for r in range(R)]
    by_row = by_row + [spread_row(jnp.where(rad == n_rad - 1, 0.0, higher[0:1]))]
    for c in range(3):
        for r in range(R):
            new = bases[c][r] + by_row[r + 1] * turns[c][r]
            new = new + (by_row[r + 2] * hx[c, r + 2] - by_row[r] * hx[c, r])
            for z in range(Z):
                row = ((c * R + r) * Z + z) * SUB
                res[row : row + SUB, :] = new[z]
    for c in range(3):
        for r in range(R):
            base = (c * R + r) * Z * SUB
            pieces = [res[pl.ds(base + s, Z, stride=SUB), :] for s in range(SUB)]
            for k, tile in enumerate(joined(pieces, wide, pad)):
                out_ref[c, r, :, k * LANES : (k + 1) * LANES] = tile

    middle = (ax > 0) & (ax < n_ax - 2)

    def sent(group, usual, for_first, for_last, for_second):
        pl.when(middle)(lambda: drain(SEND + group, usual))
        pl.when(first)(lambda: drain(SEND + group, for_first))
        pl.when(last)(lambda: drain(SEND + group, for_last))
        pl.when(second)(lambda: drain(SEND + group, for_second))

    line, total = 3 * K, n_ax - 1
    sent(0, 4 * block + total, 4 * block + total, (4 + near) * block + total, (4 + far) * block + total)
    total = 3 * Z * SUB + n_ax
    usual, more = line * (Z + 2) + total, line * (Z + 4) + total
    pl.when(has_hi)(lambda: sent(1, usual, usual, more, usual))
    pl.when(has_lo)(lambda: sent(2, usual, usual, more, usual))


def shards(n_ax, n_rad, velocity, cycle_map):
    _, R, Z, T = velocity.shape
    assert n_ax >= 8 and R >= NRING and Z >= 3

    def vmem(*shape):
        return pltpu.VMEM(shape, jnp.float32)

    return pl.pallas_call(
        functools.partial(kernel, n_ax, n_rad),
        out_shape=jax.ShapeDtypeStruct(velocity.shape, velocity.dtype),
        in_specs=[pl.BlockSpec(memory_space=pltpu.HBM)] * 2,
        out_specs=pl.BlockSpec(memory_space=pltpu.VMEM),
        scratch_shapes=[
            vmem(*velocity.shape),
            pltpu.VMEM(cycle_map.shape, jnp.int32),
            vmem(NRING * SUB, LANES),
            vmem(NRING, 2 * (MOSTSEG - 1).bit_length() + 1, SUB, LANES),
            vmem(3 * R * (Z + 10) * SUB, LANES),
            vmem(3 * 2 * (Z + 4) * SUB, LANES),
            vmem(2, 3, 2 * R, T),
            vmem(3, 2 * R, T),
            vmem(2, 3, Z + 4, T),
            vmem(3, 2 * R, T),
            vmem(2, 3, 1, T),
            vmem(2, 3, R + 2, Z + 2, SUB, LANES),
            vmem(2, 6, R, Z, SUB, LANES),
            vmem(3, R, Z + 6, SUB, LANES),
            vmem(3, R, Z + 6, SUB, LANES),
            vmem(6, R, Z + 6, SUB, LANES),
            vmem(2, 6, R, Z + 2, SUB, LANES),
            vmem(3, R + 2, Z, SUB, LANES),
            vmem(3 * R * Z * SUB, LANES),
            vmem(2, R, SUB, LANES),
            vmem(1, LANES),
            vmem(3 * n_ax, 1, LANES),
            vmem(3 * (R * 6 + Z) * SUB * (T // LANES) + 2 * n_ax, LANES),
            pltpu.SemaphoreType.REGULAR((len(stages(n_ax)),)),
            pltpu.SemaphoreType.DMA((SEMS,)),
        ],
        compiler_params=pltpu.CompilerParams(collective_id=0, has_side_effects=True, vmem_limit_bytes=8 << 20),
    )(*(pltpu.with_memory_space_constraint(x, pltpu.HBM) for x in (velocity, cycle_map)))


def solution(mesh):
    n_ax, n_rad = mesh.shape["ax"], mesh.shape["rad"]
    spec = P(None, "rad", "ax", None)
    body = functools.partial(shards, n_ax, n_rad)
    return jax.shard_map(body, mesh=mesh, in_specs=(spec, P()), out_specs=spec, check_vma=False)
```

```python
import functools

import jax
import jax.numpy as jnp
from jax import lax
from jax.experimental import pallas as pl
from jax.experimental.pallas import tpu as pltpu
from jax.sharding import PartitionSpec as P

NRING = 3
MOSTSEG = 16
SUB = 8
LANES = 128
PAIRS = ((0, 0), (1, 1), (2, 2), (0, 1), (0, 2), (1, 2))
SIGNS = (1.0, -1.0, -1.0)
EPSILON = 1e-06
MESH = pl.DeviceIdType.MESH
IN, SEND, ZL, ZR, ROW, LATE, EDGE, SUMS, SEMS = 0, 2, 5, 6, 7, 9, 12, 14, 17


def pair(a, b):
    return PAIRS.index((min(a, b), max(a, b)))


def each(count, body):
    if count <= 16:
        for i in range(count):
            body(i)
    else:
        lax.fori_loop(0, count, lambda i, c: (body(i), c)[1], 0)


def roll(x, shift, axis):
    size = x.shape[axis]
    return pltpu.roll(x, shift % size, axis)


def up(x):
    return roll(x, -1, x.ndim - 1)


def down(x):
    return roll(x, 1, x.ndim - 1)


def smooth_t(x):
    return (down(x) + up(x)) + (x + x)


def smooth_z(x):
    y = x[:-1] + x[1:]
    return y[:-1] + y[1:]


def tiles_of(x):
    return [x[:, k : k + LANES] for k in range(0, x.shape[1], LANES)]


def segments(x, wide, pad):
    rows, tiles = x[0].shape[0], len(x)
    total = tiles * LANES
    lane = lax.broadcasted_iota(jnp.int32, (rows, LANES), 1)
    pieces = []
    for s in range(SUB):
        start = (s * wide - pad) % total
        k, off = start // LANES, start % LANES
        first = x[k]
        if off:
            k2 = (k + 1) % tiles
            second = x[k2]
            first = jnp.where(lane < LANES - off, roll(first, -off, 1), roll(second, -off, 1))
        pieces.append(first)
    return pieces


def joined(pieces, wide, pad):
    rows = pieces[0].shape[0]
    lane = lax.broadcasted_iota(jnp.int32, (rows, LANES), 1)
    tiles = []
    for k in range(SUB * wide // LANES):
        lo, hi = k * LANES, (k + 1) * LANES
        s = lo // wide
        out = None
        while s * wide < hi:
            part = roll(pieces[s], s * wide - pad - lo, 1)
            out = part if out is None else jnp.where(lane >= s * wide - lo, part, out)
            s += 1
        tiles.append(out)
    return tiles


def tensor(grads):
    terms = [grads[c][c] + grads[c][c] if c == a else grads[c][a] + grads[a][c] for c, a in PAIRS]
    squares = [x * x for x in terms]
    total = 0.5 * (squares[0] + squares[1] + squares[2]) + (squares[3] + squares[4] + squares[5])
    return terms, jnp.sqrt(total)


def stages(n_ax):
    distances, reach = [], 2
    while reach < n_ax // 2:
        distances.append(reach)
        reach *= 2
    return distances


def kernel(n_ax, n_rad, v_hbm, map_hbm, out_ref, nat, map_ref, maps, masks, ext, rims, hz, he, hr, hl, hc, wsc,
           lsc, around, slope, paired, flux, hx, res, flat, acc, part, parts, spare, ready, sems):
    rad = lax.axis_index("rad")
    ax = lax.axis_index("ax")
    R, Z, T = nat.shape[1], nat.shape[2], nat.shape[3]
    K = T // LANES
    wide = T // SUB
    pad = (LANES - wide) // 2
    half = SUB // 2
    near = min(2, Z - 2)
    far = 2 - near
    right, left = lax.rem(ax + 1, n_ax), lax.rem(ax + n_ax - 1, n_ax)
    has_lo, has_hi = rad > 0, rad < n_rad - 1
    first, last, second = ax == 0, ax == n_ax - 1, ax == n_ax - 2

    barrier = pltpu.get_barrier_semaphore()

    def greet(offset, to_rad):
        peer = (lax.rem(ax + offset + n_ax, n_ax), to_rad)
        pl.semaphore_signal(barrier, inc=1, device_id=peer, device_id_type=MESH)

    def greet_row(to_rad, offsets):
        for o in offsets:
            greet(o, to_rad)

    def greet_all(offsets, beside):
        greet_row(rad, offsets)
        pl.when(has_lo)(lambda: greet_row(rad - 1, offsets + beside))
        pl.when(has_hi)(lambda: greet_row(rad + 1, offsets + beside))

    greet_all((-1, -2), (0,))
    pl.when(ax + 1 < n_ax)(lambda: greet_all((1,), ()))
    pl.when(ax + 2 < n_ax)(lambda: greet_all((2,), ()))

    fetch = pltpu.make_async_copy(v_hbm, nat, sems.at[IN])
    fetch.start()
    fetch_map = pltpu.make_async_copy(map_hbm, map_ref, sems.at[IN + 1])
    fetch_map.start()

    distances = stages(n_ax)

    def tell(stage):
        d = distances[stage]
        for peer in (lax.rem(ax + d, n_ax), lax.rem(ax + n_ax - d, n_ax)):
            pl.semaphore_signal(ready.at[stage], inc=1, device_id=(peer, rad), device_id_type=MESH)

    def hear(stage):
        pl.semaphore_wait(ready.at[stage], 2)

    def drain(sem, amount):
        pltpu.make_async_copy(spare.at[pl.ds(0, amount)], spare.at[pl.ds(0, amount)], sems.at[sem]).wait()

    def send(src, dst, group, recv, to_ax, to_rad):
        pltpu.make_async_remote_copy(
            src_ref=src, dst_ref=dst, send_sem=sems.at[SEND + group], recv_sem=sems.at[recv],
            device_id=(to_ax, to_rad), device_id_type=MESH).start()

    beside_sum = jnp.where(has_lo, 1, 0) + jnp.where(has_hi, 1, 0)
    row_sum = 4 - jnp.where(first, 2, 0) - jnp.where(ax == 1, 1, 0)
    pl.semaphore_wait(barrier, row_sum * (1 + beside_sum) + beside_sum)

    def planes(src, first_z, count, dst, row, group, recv, to_ax):
        for r in range(R):
            send(src.at[:, r, pl.ds(first_z, count)], dst.at[:, pl.ds(2 * r + row, count)], group, recv, to_ax, rad)

    def rim(src, at_end, side, group, row, to_rad):
        send(src.at[:, row, pl.ds(Z - 1, 1)], hr.at[side, :, pl.ds(2, 1)], group, ROW + side, right, to_rad)
        if at_end:
            send(src.at[:, row, pl.ds(Z - 3, 2)], hr.at[side, :, pl.ds(0, 2)], group, ROW + side, right, to_rad)

        @pl.when(ax > 0)
        def _():
            send(src.at[:, row, pl.ds(0, 1)], hr.at[side, :, pl.ds(Z + 3, 1)], group, ROW + side, left, to_rad)

        send(src.at[:, row], hr.at[side, :, pl.ds(3, Z)], group, ROW + side, ax, to_rad)

    def halos(src, at_end):
        if at_end:
            planes(src, Z - 2 - near, near, he, far, 0, ZL, right)
        planes(src, Z - 2, 2, hz.at[0], 0, 0, ZL, right)
        if far and not at_end:
            pl.when(second)(lambda: planes(src, Z - far, far, he, 0, 0, ZL, lax.rem(ax + 2, n_ax)))
        pl.when(ax > 0)(lambda: planes(src, 0, 2, hz.at[1], 0, 0, ZR, left))
        pl.when(has_hi)(lambda: rim(src, at_end, 0, 1, R - 1, rad + 1))
        pl.when(has_lo)(lambda: rim(src, at_end, 1, 2, 0, rad - 1))

    pl.when(last)(lambda: halos(v_hbm, True))
    fetch.wait()
    pl.when(ax < n_ax - 1)(lambda: halos(nat, False))
    pl.when(ax > 1)(lambda: tell(0))

    def row_of(b, c, r, i):
        line, pairs = c * R + r - 1, 3 * R * 2
        if b:
            k = i - Z + 2
            return (3 * R * Z + pairs * (2 + k // 2) + line * 2 + k % 2) * SUB
        if 2 <= i < Z + 2:
            return (line * Z + i - 2) * SUB
        return (3 * R * Z + (line * 2 + i if i < 2 else pairs + line * 2 + i - Z - 2)) * SUB

    def rim_of(b, c, r, i):
        return ((c * 2 + (0 if r == 0 else 1)) * (Z + 4) + i + 1 - b * Z) * SUB

    def place(b, c, r, i):
        inside = 0 < r <= R
        return (ext, row_of(b, c, r, i)) if inside else (rims, rim_of(b, c, r, i))

    def get(b, c, r, i, n):
        blocks = []
        for k in range(n):
            ref, row = place(b, c, r, i + k)
            blocks.append(ref[row : row + SUB, :])
        return jnp.stack(blocks)

    def put(b, c, r, i, x):
        ref, row = place(b, c, r, i)
        ref[row : row + SUB, :] = x

    def unpack(x, target):
        ref, row = target
        for s, piece in enumerate(segments(tiles_of(x), wide, pad)):
            ref[pl.ds(row + s, x.shape[0], stride=SUB), :] = piece

    lane = lax.broadcasted_iota(jnp.int32, (SUB, LANES), 1)
    steps = []
    while 2 ** len(steps) < MOSTSEG:
        steps.append(2 ** len(steps))
    S = len(steps)

    def spread(ring, x):
        total, rest = x, x
        for k, d in enumerate(steps):
            total = total + masks[ring, k] * roll(total, d, x.ndim - 1)
            rest = rest + masks[ring, S + k] * roll(rest, -d, x.ndim - 1)
        return total + rest - x

    def coarsen(places, count):
        values = [jnp.concatenate([get(b, c, r, i, count) for c in range(3)], axis=0) for _, b, r, i in places]
        total, rest = list(values), list(values)
        for k, d in enumerate(steps):
            for j, (ring, _, _, _) in enumerate(places):
                total[j] = total[j] + masks[ring, k] * roll(total[j], d, 2)
            for j, (ring, _, _, _) in enumerate(places):
                rest[j] = rest[j] + masks[ring, S + k] * roll(rest[j], -d, 2)
        means = [(t + q - x) * masks[p[0], 2 * S] for t, q, x, p in zip(total, rest, values, places)]
        lows = [roll(m, -wide, 2) for m in means]
        highs = [roll(m, wide, 2) for m in means]
        lows, highs = [roll(m, 1, 1) for m in lows], [roll(m, -1, 1) for m in highs]
        for mean, low, high, (_, b, r, i) in zip(means, lows, highs, places):
            mean = jnp.where(lane < pad, low, mean)
            mean = jnp.where(lane >= pad + wide, high, mean)
            for c in range(3):
                for k in range(count):
                    put(b, c, r, i + k, mean[c * count + k])

    def coarsen_block(b, first_i, count):
        @pl.when(rad == 0)
        def _():
            coarsen([(r, b, r + 1, first_i) for r in range(NRING)], count)

    def coarsen_below(first_i, count):
        if R == NRING:
            @pl.when(rad == 1)
            def _():
                coarsen([(R - 1, 0, 0, first_i)], count)

    fetch_map.wait()

    @pl.when(rad <= (1 if R == NRING else 0))
    def _():
        labels = map_ref[...].astype(jnp.float32)
        for s, piece in enumerate(segments(tiles_of(labels), wide, pad)):
            maps[pl.ds(s, NRING, stride=SUB), :] = piece
        for ring in range(NRING):
            label = maps[ring * SUB : (ring + 1) * SUB, :]
            for k, d in enumerate(steps):
                masks[ring, k] = (roll(label, d, 1) == label).astype(jnp.float32)
                masks[ring, S + k] = (roll(label, -d, 1) == label).astype(jnp.float32)
            masks[ring, 2 * S] = 1.0 / spread(ring, jnp.ones((SUB, LANES), jnp.float32))

    for c in range(3):
        for r in range(R):
            unpack(nat[c, r], place(0, c, r + 1, 2))
    coarsen_block(0, 2, Z)

    def turns_of(b, i, count):
        z = i + 2 - b * Z
        for r in range(1, R + 1):
            for c in range(3):
                x = get(b, c, r, i, count)
                after, before = up(x), down(x)
                around[c, r - 1, z : z + count] = (after + before) + (x + x)
                slope[c, r - 1, z : z + count] = after - before

    def products_of(b, i, count):
        z = i + 2 - b * Z
        for r in range(1, R + 1):
            x = [get(b, c, r, i, count) for c in range(3)]
            for p, (c, a) in enumerate(PAIRS):
                paired[p, r - 1, z : z + count] = smooth_t(x[c] * x[a])

    def local(b, low_z):
        n, z = Z - low_z, low_z + 4 - b * Z
        for r in range(1, R + 1):
            filtered = []
            for c in range(3):
                filtered.append(smooth_z(around[c, r - 1, z - 2 : z + n + 2]))
                wsc[b, c, r, 0 : n + 2] = filtered[c]
            for p, (c, a) in enumerate(PAIRS):
                product = smooth_z(paired[p, r - 1, z - 1 : z + n + 1])
                lsc[b, p, r - 1, 0:n] = 16.0 * product - filtered[c][1:-1] * filtered[a][1:-1]

    @pl.when(ax < 2)
    def _():
        hear(0)
        tell(0)

    @pl.when(first)
    def _():
        planes(nat, 0, 2, hl, 0, 0, LATE, left)
        pl.when(has_hi)(lambda: send(nat.at[:, R - 1, pl.ds(0, 1)], hc.at[0], 1, LATE + 1, left, rad + 1))
        pl.when(has_lo)(lambda: send(nat.at[:, 0, pl.ds(0, 1)], hc.at[1], 2, LATE + 2, left, rad - 1))

    def axis_end(b, first_i, count):
        for c in range(3):
            for i in range(first_i, first_i + count):
                put(b, c, 0, i, SIGNS[c] * roll(get(b, c, 1, i, 1)[0], half, 0))

    def wall_end():
        for c in range(3):
            for i in range(-1, Z + 3):
                put(0, c, R + 1, i, jnp.zeros((SUB, LANES), jnp.float32))

    def strain(b, low_z, high_z, rows):
        n, i0 = high_z - low_z, low_z + 2
        z = low_z + 4 - b * Z
        for r in rows:
            grads = []
            for c in range(3):
                long = get(b, c, r, i0 - 2, n + 4)
                grads.append([
                    long[2:] - long[:-2],
                    get(b, c, r + 1, i0 - 1, n + 2) - get(b, c, r - 1, i0 - 1, n + 2),
                    slope[c, r - 1, z - 1 : z + n + 1],
                ])
            terms, size = tensor(grads)
            for p in range(6):
                flux[b, p, r - 1, 0 : n + 2] = size * terms[p]

    def outside(b, low_z, r):
        n, i0 = Z - low_z, low_z + 2
        for c in range(3):
            wsc[b, c, r, 1 : n + 1] = smooth_t(smooth_z(get(b, c, r, i0 - 1, n + 2)))

    def collect(b, low_z, high_z, rows):
        n = high_z - low_z
        for r in rows:
            grads = []
            for c in range(3):
                mid = wsc[b, c, r, 1 : n + 1]
                grads.append([
                    wsc[b, c, r, 2 : n + 2] - wsc[b, c, r, 0:n],
                    wsc[b, c, r + 1, 1 : n + 1] - wsc[b, c, r - 1, 1 : n + 1],
                    up(mid) - down(mid),
                ])
            terms, size = tensor(grads)
            size = 0.25 * size
            sums = [[0.0, 0.0], [0.0, 0.0]]
            for p, (c, a) in enumerate(PAIRS):
                model = smooth_t(smooth_z(flux[b, p, r - 1, 0 : n + 2])) - size * terms[p]
                kind = sums[0 if c == a else 1]
                kind[0] = kind[0] + lsc[b, p, r - 1, 0:n] * model
                kind[1] = kind[1] + model * model
            for k in range(2):
                each_z = sums[0][k] + 2.0 * sums[1][k]
                if b:
                    acc[k, r - 1] = acc[k, r - 1] + jnp.sum(each_z, axis=0)
                else:
                    rest = jnp.sum(each_z[Z - 2 :], axis=0)
                    acc[k, r - 1] = acc[k, r - 1] + jnp.sum(each_z[: Z - 2], axis=0) + jnp.where(last, 0.0, rest)

    def sums_of(b, low_z, rows):
        strain(b, low_z, Z, rows)
        collect(b, low_z, Z, rows)

    turns_of(0, 2, Z)
    products_of(0, 2, Z)
    block = 3 * R * K
    acc[...] = jnp.zeros(acc.shape, jnp.float32)

    @pl.when(first)
    def _():
        drain(ZL, block * 4)
        for c in range(3):
            unpack(he[c], place(1, c, 1, Z - 2))
            unpack(hz[0, c], place(1, c, 1, Z))
        coarsen_block(1, Z - 2, 2)
        coarsen_block(1, Z, 2)
        for c in range(3):
            for r in range(1, R + 1):
                for i in range(2):
                    put(0, c, r, i, get(1, c, r, Z + i, 1)[0])
                    put(1, c, r, Z + 2 + i, get(0, c, r, 2 + i, 1)[0])
        turns_of(1, Z - 2, 4)
        products_of(1, Z - 1, 3)
        local(1, Z - 2)
        sums_of(1, Z - 2, range(2, R))

    @pl.when(ax > 0)
    def _():
        drain(ZL, block * 2)
        for c in range(3):
            unpack(hz[0, c], place(0, c, 1, 0))
        coarsen_block(0, 0, 2)
        turns_of(0, 0, 2)
        products_of(0, 1, 1)

    @pl.when(ax < n_ax - 1)
    def _():
        drain(ZR, block * 2)
        for c in range(3):
            unpack(hz[1, c], place(0, c, 1, Z + 2))
        coarsen_block(0, Z + 2, 2)
        turns_of(0, Z + 2, 2)
        products_of(0, Z + 2, 1)

    local(0, 0)
    sums_of(0, 0, range(2, R))

    def rim_in(side, row):
        line = 3 * K
        pl.when(first)(lambda: drain(ROW + side, line * (Z + 4)))
        pl.when(last)(lambda: drain(ROW + side, line * (Z + 1)))
        pl.when((ax > 0) & (ax < n_ax - 1))(lambda: drain(ROW + side, line * (Z + 2)))
        for c in range(3):
            unpack(hr[side, c], place(0, c, row, -1))

    def edge_out(row, end, to_rad):
        group, slot = (2, EDGE + 1) if row == 1 else (1, EDGE)
        send(hx.at[:, row], hx.at[:, end], group, slot, ax, to_rad)

    def edge_rows(row):
        for c in range(3):
            hx[c, row] = flux[0, pair(c, 1), row - 1, 1 : Z + 1]
        if row == 1:
            pl.when(has_lo)(lambda: edge_out(1, R + 1, rad - 1))
        else:
            pl.when(has_hi)(lambda: edge_out(R, 0, rad + 1))

    def finish(row, beyond):
        strain(0, 0, Z, (row,))
        pl.when(ax < n_ax - 1)(lambda: edge_rows(row))

        @pl.when(first)
        def _():
            outside(1, Z - 2, beyond)
            sums_of(1, Z - 2, (row,))

        outside(0, 0, beyond)
        collect(0, 0, Z, (row,))

    pl.when(has_lo)(lambda: rim_in(0, 0))
    coarsen_below(1, Z + 2)
    pl.when(first)(lambda: coarsen_below(-1, 2))

    @pl.when(rad == 0)
    def _():
        axis_end(0, 1, Z + 2)
        pl.when(first)(lambda: axis_end(1, Z - 1, 2))

    finish(1, 0)
    pl.when(has_hi)(lambda: rim_in(1, R + 1))
    pl.when(rad == n_rad - 1)(wall_end)
    finish(R, R + 1)

    sub_index = lax.broadcasted_iota(jnp.int32, (SUB, LANES), 0)
    lane_index = lax.broadcasted_iota(jnp.int32, (SUB, LANES), 1)
    mine = jnp.zeros((SUB, LANES), jnp.float32)
    for r in range(R):
        for k in range(2):
            row = jnp.sum(acc[k, r], axis=0, keepdims=True) * (2.0 ** -15, 2.0 ** -14)[k]
            mine = jnp.where(sub_index == k * half + r, row, mine)
    mine = jnp.where((lane_index >= pad) & (lane_index < pad + wide), mine, 0.0)
    fold = LANES // 2
    while fold >= LANES // SUB:
        mine = mine + roll(mine, fold, 1)
        fold //= 2
    group = lane_index // (LANES // SUB) == sub_index
    part[...] = jnp.sum(jnp.where(group, mine, 0.0), axis=0, keepdims=True)
    parts[n_ax + ax] = part[...]

    def sums(side, i):
        peer = lax.rem(ax + i, n_ax)
        send(part, parts.at[(1 - side) * n_ax + ax], (0, 1, 2)[side], SUMS + 1 - side, peer, rad + side)

    def sums_in(side, amount):
        pltpu.make_async_copy(parts.at[pl.ds(0, amount)], parts.at[pl.ds(0, amount)], sems.at[SUMS + 1 + side]).wait()

    def first_of(side):
        return 1 if side == 0 else 0

    def send_sums(side):
        start = first_of(side)
        each(n_ax - start, lambda i: sums(side, i + start))

    pl.when(ax > 1)(lambda: hear(0))
    for stage in range(1, len(distances)):
        tell(stage)
        hear(stage)
    send_sums(0)
    pl.when(has_lo)(lambda: send_sums(-1))
    pl.when(has_hi)(lambda: send_sums(1))

    @pl.when(last)
    def _():
        drain(LATE, block * 2)
        for c in range(3):
            unpack(hl[c], place(0, c, 1, Z + 2))
        coarsen_block(0, Z + 2, 2)

        @pl.when(has_lo)
        def _():
            drain(LATE + 1, 3 * K)
            for c in range(3):
                unpack(hc[0, c], place(0, c, 0, Z + 2))

        @pl.when(has_hi)
        def _():
            drain(LATE + 2, 3 * K)
            for c in range(3):
                unpack(hc[1, c], place(0, c, R + 1, Z + 2))

        coarsen_below(Z + 2, 1)
        pl.when(rad == 0)(lambda: axis_end(0, Z + 2, 1))
        for r in range(1, R + 1):
            grads = []
            for c in range(3):
                long = get(0, c, r, Z, 4)
                mid = long[1:-1]
                grads.append([
                    long[2:] - long[:-2],
                    get(0, c, r + 1, Z + 1, 2) - get(0, c, r - 1, Z + 1, 2),
                    up(mid) - down(mid),
                ])
            terms, size = tensor(grads)
            for p in range(6):
                flux[0, p, r - 1, Z : Z + 2] = size * terms[p]

    @pl.when(last)
    def _():
        edge_rows(1)
        edge_rows(R)

    for c in range(3):
        hx[c, 2:R] = flux[0, pair(c, 1), 1 : R - 1, 1 : Z + 1]

    @pl.when(rad == 0)
    def _():
        for c in range(3):
            for z in range(Z):
                hx[c, 0, z] = SIGNS[c] * SIGNS[1] * roll(hx[c, 1, z], half, 0)

    @pl.when(rad == n_rad - 1)
    def _():
        for c in range(3):
            for z in range(Z):
                hx[c, R + 1, z] = jnp.zeros((SUB, LANES), jnp.float32)

    def lay(slot, x):
        base = slot * Z * SUB
        for z in range(Z):
            res[base + z * SUB : base + (z + 1) * SUB, :] = x[z]
        pieces = [res[pl.ds(base + s, Z, stride=SUB), :] for s in range(SUB)]
        for k, tile in enumerate(joined(pieces, wide, pad)):
            flat[slot, :, k * LANES : (k + 1) * LANES] = tile

    def slot_of(kind, c, r):
        return (kind * 3 + c) * (R + 2) + r

    for r in range(1, R + 1):
        for c in range(3):
            axial = get(0, c, r, 1, Z + 2) * get(0, 0, r, 1, Z + 2)
            outer = get(0, c, r + 1, 2, Z) * get(0, 1, r + 1, 2, Z)
            inner = get(0, c, r - 1, 2, Z) * get(0, 1, r - 1, 2, Z)
            mid = get(0, c, r, 2, Z)
            spin = mid * get(0, 2, r, 2, Z)
            change = axial[2:] - axial[:-2] + (outer - inner) + (up(spin) - down(spin))
            lay(slot_of(0, c, r), mid - 0.5 * change)
            turn = flux[0, pair(c, 2), r - 1, 1 : Z + 1]
            p = pair(c, 0)
            along = flux[0, p, r - 1, 2 : Z + 2] - flux[0, p, r - 1, 0:Z]
            lay(slot_of(1, c, r), along + (up(turn) - down(turn)))
            lay(slot_of(2, c, r), hx[c, r])

    count = n_ax * Z * T
    def coefficients(total):
        total = jnp.broadcast_to(jnp.sum(jnp.where(group, total, 0.0), axis=1, keepdims=True), (SUB, LANES)) / count
        return 0.125 * (total / (roll(total, -half, 0) + EPSILON))

    def total_of(side):
        terms = parts[pl.ds((1 + side) * n_ax, n_ax)]
        while terms.shape[0] % 2 == 0:
            terms = terms[: terms.shape[0] // 2] + terms[terms.shape[0] // 2 :]
        return jnp.sum(terms, axis=0)

    def spread_row(x):
        return jnp.broadcast_to(x, (Z, LANES))

    pl.when(has_lo)(lambda: drain(EDGE, 3 * Z * SUB))
    pl.when(has_hi)(lambda: drain(EDGE + 1, 3 * Z * SUB))
    for c in range(3):
        for r in (0, R + 1):
            lay(slot_of(2, c, r), hx[c, r])
    sums_in(0, n_ax - 1)
    pl.when(has_lo)(lambda: sums_in(-1, n_ax))
    pl.when(has_hi)(lambda: sums_in(1, n_ax))
    lower, coef, higher = [coefficients(total_of(side)) for side in (-1, 0, 1)]
    by_row = [spread_row(jnp.where(rad == 0, coef[0:1], lower[R - 1 : R]))]
    by_row = by_row + [spread_row(coef[r : r + 1]) for r in range(R)]
    by_row = by_row + [spread_row(jnp.where(rad == n_rad - 1, 0.0, higher[0:1]))]
    for c in range(3):
        for r in range(1, R + 1):
            for k in range(K):
                lanes = slice(k * LANES, (k + 1) * LANES)
                base, turn, outer, inner = [
                    flat[slot_of(*at), :, lanes] for at in ((0, c, r), (1, c, r), (2, c, r + 1), (2, c, r - 1))]
                out_ref[c, r - 1, :, lanes] = base + by_row[r] * turn + (by_row[r + 1] * outer - by_row[r - 1] * inner)

    middle = (ax > 0) & (ax < n_ax - 2)

    def sent(group, usual, for_first, for_last, for_second):
        pl.when(middle)(lambda: drain(SEND + group, usual))
        pl.when(first)(lambda: drain(SEND + group, for_first))
        pl.when(last)(lambda: drain(SEND + group, for_last))
        pl.when(second)(lambda: drain(SEND + group, for_second))

    line, total = 3 * K, n_ax - 1
    sent(0, 4 * block + total, 4 * block + total, (4 + near) * block + total, (4 + far) * block + total)
    total = 3 * Z * SUB + n_ax
    usual, more = line * (Z + 2) + total, line * (Z + 4) + total
    pl.when(has_hi)(lambda: sent(1, usual, usual, more, usual))
    pl.when(has_lo)(lambda: sent(2, usual, usual, more, usual))


def shards(n_ax, n_rad, velocity, cycle_map):
    _, R, Z, T = velocity.shape
    assert n_ax >= 8 and R >= NRING and Z >= 3

    def vmem(*shape):
        return pltpu.VMEM(shape, jnp.float32)

    return pl.pallas_call(
        functools.partial(kernel, n_ax, n_rad),
        out_shape=jax.ShapeDtypeStruct(velocity.shape, velocity.dtype),
        in_specs=[pl.BlockSpec(memory_space=pltpu.HBM)] * 2,
        out_specs=pl.BlockSpec(memory_space=pltpu.VMEM),
        scratch_shapes=[
            vmem(*velocity.shape),
            pltpu.VMEM(cycle_map.shape, jnp.int32),
            vmem(NRING * SUB, LANES),
            vmem(NRING, 2 * (MOSTSEG - 1).bit_length() + 1, SUB, LANES),
            vmem(3 * R * (Z + 10) * SUB, LANES),
            vmem(3 * 2 * (Z + 4) * SUB, LANES),
            vmem(2, 3, 2 * R, T),
            vmem(3, 2 * R, T),
            vmem(2, 3, Z + 4, T),
            vmem(3, 2 * R, T),
            vmem(2, 3, 1, T),
            vmem(2, 3, R + 2, Z + 2, SUB, LANES),
            vmem(2, 6, R, Z, SUB, LANES),
            vmem(3, R, Z + 6, SUB, LANES),
            vmem(3, R, Z + 6, SUB, LANES),
            vmem(6, R, Z + 6, SUB, LANES),
            vmem(2, 6, R, Z + 2, SUB, LANES),
            vmem(3, R + 2, Z, SUB, LANES),
            vmem(9 * (R + 2) * Z * SUB, LANES),
            vmem(9 * (R + 2), Z, T),
            vmem(2, R, SUB, LANES),
            vmem(1, LANES),
            vmem(3 * n_ax, 1, LANES),
            vmem(3 * (R * 6 + Z) * SUB * (T // LANES) + 2 * n_ax, LANES),
            pltpu.SemaphoreType.REGULAR((len(stages(n_ax)),)),
            pltpu.SemaphoreType.DMA((SEMS,)),
        ],
        compiler_params=pltpu.CompilerParams(collective_id=0, has_side_effects=True, vmem_limit_bytes=8 << 20),
    )(*(pltpu.with_memory_space_constraint(x, pltpu.HBM) for x in (velocity, cycle_map)))


def solution(mesh):
    n_ax, n_rad = mesh.shape["ax"], mesh.shape["rad"]
    spec = P(None, "rad", "ax", None)
    body = functools.partial(shards, n_ax, n_rad)
    return jax.shard_map(body, mesh=mesh, in_specs=(spec, P()), out_specs=spec, check_vma=False)
```

```python
import functools

import jax
import jax.numpy as jnp
from jax import lax
from jax.experimental import pallas as pl
from jax.experimental.pallas import tpu as pltpu
from jax.sharding import PartitionSpec as P

NRING = 3
MOSTSEG = 16
SUB = 8
LANES = 128
PAIRS = ((0, 0), (1, 1), (2, 2), (0, 1), (0, 2), (1, 2))
SIGNS = (1.0, -1.0, -1.0)
EPSILON = 1e-06
MESH = pl.DeviceIdType.MESH
IN, SEND, ZL, ZR, ROW, LATE, EDGE, SUMS, SEMS = 0, 2, 5, 6, 7, 9, 12, 14, 17


def pair(a, b):
    return PAIRS.index((min(a, b), max(a, b)))


def each(count, body):
    if count <= 16:
        for i in range(count):
            body(i)
    else:
        lax.fori_loop(0, count, lambda i, c: (body(i), c)[1], 0)


def roll(x, shift, axis):
    size = x.shape[axis]
    return pltpu.roll(x, shift % size, axis)


def up(x):
    return roll(x, -1, x.ndim - 1)


def down(x):
    return roll(x, 1, x.ndim - 1)


def smooth_t(x):
    return (down(x) + up(x)) + (x + x)


def smooth_z(x):
    y = x[:-1] + x[1:]
    return y[:-1] + y[1:]


def tiles_of(x):
    return [x[:, k : k + LANES] for k in range(0, x.shape[1], LANES)]


def segments(x, wide, pad):
    rows, tiles = x[0].shape[0], len(x)
    total = tiles * LANES
    lane = lax.broadcasted_iota(jnp.int32, (rows, LANES), 1)
    pieces = []
    for s in range(SUB):
        start = (s * wide - pad) % total
        k, off = start // LANES, start % LANES
        first = x[k]
        if off:
            k2 = (k + 1) % tiles
            second = x[k2]
            first = jnp.where(lane < LANES - off, roll(first, -off, 1), roll(second, -off, 1))
        pieces.append(first)
    return pieces


def joined(pieces, wide, pad):
    rows = pieces[0].shape[0]
    lane = lax.broadcasted_iota(jnp.int32, (rows, LANES), 1)
    tiles = []
    for k in range(SUB * wide // LANES):
        lo, hi = k * LANES, (k + 1) * LANES
        s = lo // wide
        out = None
        while s * wide < hi:
            part = roll(pieces[s], s * wide - pad - lo, 1)
            out = part if out is None else jnp.where(lane >= s * wide - lo, part, out)
            s += 1
        tiles.append(out)
    return tiles


def tensor(grads):
    terms = [grads[c][c] + grads[c][c] if c == a else grads[c][a] + grads[a][c] for c, a in PAIRS]
    squares = [x * x for x in terms]
    total = 0.5 * (squares[0] + squares[1] + squares[2]) + (squares[3] + squares[4] + squares[5])
    return terms, jnp.sqrt(total)


def stages(n_ax):
    distances, reach = [], 2
    while reach < n_ax // 2:
        distances.append(reach)
        reach *= 2
    return distances


def kernel(n_ax, n_rad, v_hbm, map_hbm, out_ref, nat, map_ref, maps, masks, ext, rims, hz, he, hr, hl, hc, wsc,
           lsc, around, slope, paired, flux, hx, res, flat, acc, part, parts, spare, ready, sems):
    rad = lax.axis_index("rad")
    ax = lax.axis_index("ax")
    R, Z, T = nat.shape[1], nat.shape[2], nat.shape[3]
    K = T // LANES
    wide = T // SUB
    pad = (LANES - wide) // 2
    half = SUB // 2
    near = min(2, Z - 2)
    far = 2 - near
    right, left = lax.rem(ax + 1, n_ax), lax.rem(ax + n_ax - 1, n_ax)
    has_lo, has_hi = rad > 0, rad < n_rad - 1
    first, last, second = ax == 0, ax == n_ax - 1, ax == n_ax - 2

    barrier = pltpu.get_barrier_semaphore()

    def greet(offset, to_rad):
        peer = (lax.rem(ax + offset + n_ax, n_ax), to_rad)
        pl.semaphore_signal(barrier, inc=1, device_id=peer, device_id_type=MESH)

    def greet_row(to_rad, offsets):
        for o in offsets:
            greet(o, to_rad)

    def greet_all(offsets, beside):
        greet_row(rad, offsets)
        pl.when(has_lo)(lambda: greet_row(rad - 1, offsets + beside))
        pl.when(has_hi)(lambda: greet_row(rad + 1, offsets + beside))

    greet_all((-1, -2), (0,))
    pl.when(ax + 1 < n_ax)(lambda: greet_all((1,), ()))
    pl.when(ax + 2 < n_ax)(lambda: greet_all((2,), ()))

    fetch = pltpu.make_async_copy(v_hbm, nat, sems.at[IN])
    fetch.start()
    fetch_map = pltpu.make_async_copy(map_hbm, map_ref, sems.at[IN + 1])
    fetch_map.start()

    distances = stages(n_ax)

    def tell(stage):
        d = distances[stage]
        for peer in (lax.rem(ax + d, n_ax), lax.rem(ax + n_ax - d, n_ax)):
            pl.semaphore_signal(ready.at[stage], inc=1, device_id=(peer, rad), device_id_type=MESH)

    def hear(stage):
        pl.semaphore_wait(ready.at[stage], 2)

    def drain(sem, amount):
        pltpu.make_async_copy(spare.at[pl.ds(0, amount)], spare.at[pl.ds(0, amount)], sems.at[sem]).wait()

    def send(src, dst, group, recv, to_ax, to_rad):
        pltpu.make_async_remote_copy(
            src_ref=src, dst_ref=dst, send_sem=sems.at[SEND + group], recv_sem=sems.at[recv],
            device_id=(to_ax, to_rad), device_id_type=MESH).start()

    beside_sum = jnp.where(has_lo, 1, 0) + jnp.where(has_hi, 1, 0)
    row_sum = 4 - jnp.where(first, 2, 0) - jnp.where(ax == 1, 1, 0)
    pl.semaphore_wait(barrier, row_sum * (1 + beside_sum) + beside_sum)

    def planes(src, first_z, count, dst, row, group, recv, to_ax):
        for r in range(R):
            send(src.at[:, r, pl.ds(first_z, count)], dst.at[:, pl.ds(2 * r + row, count)], group, recv, to_ax, rad)

    def rim(src, at_end, side, group, row, to_rad):
        send(src.at[:, row, pl.ds(Z - 1, 1)], hr.at[side, :, pl.ds(2, 1)], group, ROW + side, right, to_rad)
        if at_end:
            send(src.at[:, row, pl.ds(Z - 3, 2)], hr.at[side, :, pl.ds(0, 2)], group, ROW + side, right, to_rad)

        @pl.when(ax > 0)
        def _():
            send(src.at[:, row, pl.ds(0, 1)], hr.at[side, :, pl.ds(Z + 3, 1)], group, ROW + side, left, to_rad)

        send(src.at[:, row], hr.at[side, :, pl.ds(3, Z)], group, ROW + side, ax, to_rad)

    def halos(src, at_end):
        if at_end:
            planes(src, Z - 2 - near, near, he, far, 0, ZL, right)
        planes(src, Z - 2, 2, hz.at[0], 0, 0, ZL, right)
        if far and not at_end:
            pl.when(second)(lambda: planes(src, Z - far, far, he, 0, 0, ZL, lax.rem(ax + 2, n_ax)))
        pl.when(ax > 0)(lambda: planes(src, 0, 2, hz.at[1], 0, 0, ZR, left))
        pl.when(has_hi)(lambda: rim(src, at_end, 0, 1, R - 1, rad + 1))
        pl.when(has_lo)(lambda: rim(src, at_end, 1, 2, 0, rad - 1))

    pl.when(last)(lambda: halos(v_hbm, True))
    fetch.wait()
    pl.when(ax < n_ax - 1)(lambda: halos(nat, False))
    pl.when(ax > 1)(lambda: tell(0))

    def row_of(b, c, r, i):
        line, pairs = c * R + r - 1, 3 * R * 2
        if b:
            k = i - Z + 2
            return (3 * R * Z + pairs * (2 + k // 2) + line * 2 + k % 2) * SUB
        if 2 <= i < Z + 2:
            return (line * Z + i - 2) * SUB
        return (3 * R * Z + (line * 2 + i if i < 2 else pairs + line * 2 + i - Z - 2)) * SUB

    def rim_of(b, c, r, i):
        return ((c * 2 + (0 if r == 0 else 1)) * (Z + 4) + i + 1 - b * Z) * SUB

    def place(b, c, r, i):
        inside = 0 < r <= R
        return (ext, row_of(b, c, r, i)) if inside else (rims, rim_of(b, c, r, i))

    def get(b, c, r, i, n):
        blocks = []
        for k in range(n):
            ref, row = place(b, c, r, i + k)
            blocks.append(ref[row : row + SUB, :])
        return jnp.stack(blocks)

    def put(b, c, r, i, x):
        ref, row = place(b, c, r, i)
        ref[row : row + SUB, :] = x

    def unpack(x, target):
        ref, row = target
        for s, piece in enumerate(segments(tiles_of(x), wide, pad)):
            ref[pl.ds(row + s, x.shape[0], stride=SUB), :] = piece

    lane = lax.broadcasted_iota(jnp.int32, (SUB, LANES), 1)
    steps = []
    while 2 ** len(steps) < MOSTSEG:
        steps.append(2 ** len(steps))
    S = len(steps)

    def spread(ring, x):
        total, rest = x, x
        for k, d in enumerate(steps):
            total = total + masks[ring, k] * roll(total, d, x.ndim - 1)
            rest = rest + masks[ring, S + k] * roll(rest, -d, x.ndim - 1)
        return total + rest - x

    def coarsen(places, count):
        values = [jnp.concatenate([get(b, c, r, i, count) for c in range(3)], axis=0) for _, b, r, i in places]
        total, rest = list(values), list(values)
        for k, d in enumerate(steps):
            for j, (ring, _, _, _) in enumerate(places):
                total[j] = total[j] + masks[ring, k] * roll(total[j], d, 2)
            for j, (ring, _, _, _) in enumerate(places):
                rest[j] = rest[j] + masks[ring, S + k] * roll(rest[j], -d, 2)
        means = [(t + q - x) * masks[p[0], 2 * S] for t, q, x, p in zip(total, rest, values, places)]
        lows = [roll(m, -wide, 2) for m in means]
        highs = [roll(m, wide, 2) for m in means]
        lows, highs = [roll(m, 1, 1) for m in lows], [roll(m, -1, 1) for m in highs]
        for mean, low, high, (_, b, r, i) in zip(means, lows, highs, places):
            mean = jnp.where(lane < pad, low, mean)
            mean = jnp.where(lane >= pad + wide, high, mean)
            for c in range(3):
                for k in range(count):
                    put(b, c, r, i + k, mean[c * count + k])

    def coarsen_block(b, first_i, count):
        @pl.when(rad == 0)
        def _():
            coarsen([(r, b, r + 1, first_i) for r in range(NRING)], count)

    def coarsen_below(first_i, count):
        if R == NRING:
            @pl.when(rad == 1)
            def _():
                coarsen([(R - 1, 0, 0, first_i)], count)

    fetch_map.wait()

    @pl.when(rad <= (1 if R == NRING else 0))
    def _():
        labels = map_ref[...].astype(jnp.float32)
        for s, piece in enumerate(segments(tiles_of(labels), wide, pad)):
            maps[pl.ds(s, NRING, stride=SUB), :] = piece
        for ring in range(NRING):
            label = maps[ring * SUB : (ring + 1) * SUB, :]
            for k, d in enumerate(steps):
                masks[ring, k] = (roll(label, d, 1) == label).astype(jnp.float32)
                masks[ring, S + k] = (roll(label, -d, 1) == label).astype(jnp.float32)
            masks[ring, 2 * S] = 1.0 / spread(ring, jnp.ones((SUB, LANES), jnp.float32))

    for c in range(3):
        for r in range(R):
            unpack(nat[c, r], place(0, c, r + 1, 2))
    coarsen_block(0, 2, Z)

    def turns_of(b, i, count):
        z = i + 2 - b * Z
        for r in range(1, R + 1):
            for c in range(3):
                x = get(b, c, r, i, count)
                after, before = up(x), down(x)
                around[c, r - 1, z : z + count] = (after + before) + (x + x)
                slope[c, r - 1, z : z + count] = after - before

    def products_of(b, i, count):
        z = i + 2 - b * Z
        for r in range(1, R + 1):
            x = [get(b, c, r, i, count) for c in range(3)]
            for p, (c, a) in enumerate(PAIRS):
                paired[p, r - 1, z : z + count] = smooth_t(x[c] * x[a])

    def local(b, low_z):
        n, z = Z - low_z, low_z + 4 - b * Z
        for r in range(1, R + 1):
            filtered = []
            for c in range(3):
                filtered.append(smooth_z(around[c, r - 1, z - 2 : z + n + 2]))
                wsc[b, c, r, 0 : n + 2] = filtered[c]
            for p, (c, a) in enumerate(PAIRS):
                product = smooth_z(paired[p, r - 1, z - 1 : z + n + 1])
                lsc[b, p, r - 1, 0:n] = 16.0 * product - filtered[c][1:-1] * filtered[a][1:-1]

    @pl.when(ax < 2)
    def _():
        hear(0)
        tell(0)

    @pl.when(first)
    def _():
        planes(nat, 0, 2, hl, 0, 0, LATE, left)
        pl.when(has_hi)(lambda: send(nat.at[:, R - 1, pl.ds(0, 1)], hc.at[0], 1, LATE + 1, left, rad + 1))
        pl.when(has_lo)(lambda: send(nat.at[:, 0, pl.ds(0, 1)], hc.at[1], 2, LATE + 2, left, rad - 1))

    def axis_end(b, first_i, count):
        for c in range(3):
            for i in range(first_i, first_i + count):
                put(b, c, 0, i, SIGNS[c] * roll(get(b, c, 1, i, 1)[0], half, 0))

    def wall_end():
        for c in range(3):
            for i in range(-1, Z + 3):
                put(0, c, R + 1, i, jnp.zeros((SUB, LANES), jnp.float32))

    def strain(b, low_z, high_z, rows):
        n, i0 = high_z - low_z, low_z + 2
        z = low_z + 4 - b * Z
        for r in rows:
            grads = []
            for c in range(3):
                long = get(b, c, r, i0 - 2, n + 4)
                grads.append([
                    long[2:] - long[:-2],
                    get(b, c, r + 1, i0 - 1, n + 2) - get(b, c, r - 1, i0 - 1, n + 2),
                    slope[c, r - 1, z - 1 : z + n + 1],
                ])
            terms, size = tensor(grads)
            for p in range(6):
                flux[b, p, r - 1, 0 : n + 2] = size * terms[p]

    def outside(b, low_z, r):
        n, i0 = Z - low_z, low_z + 2
        for c in range(3):
            wsc[b, c, r, 1 : n + 1] = smooth_t(smooth_z(get(b, c, r, i0 - 1, n + 2)))

    def collect(b, low_z, high_z, rows):
        n = high_z - low_z
        for r in rows:
            grads = []
            for c in range(3):
                mid = wsc[b, c, r, 1 : n + 1]
                grads.append([
                    wsc[b, c, r, 2 : n + 2] - wsc[b, c, r, 0:n],
                    wsc[b, c, r + 1, 1 : n + 1] - wsc[b, c, r - 1, 1 : n + 1],
                    up(mid) - down(mid),
                ])
            terms, size = tensor(grads)
            size = 0.25 * size
            sums = [[0.0, 0.0], [0.0, 0.0]]
            for p, (c, a) in enumerate(PAIRS):
                model = smooth_t(smooth_z(flux[b, p, r - 1, 0 : n + 2])) - size * terms[p]
                kind = sums[0 if c == a else 1]
                kind[0] = kind[0] + lsc[b, p, r - 1, 0:n] * model
                kind[1] = kind[1] + model * model
            for k in range(2):
                each_z = sums[0][k] + 2.0 * sums[1][k]
                if b:
                    acc[k, r - 1] = acc[k, r - 1] + jnp.sum(each_z, axis=0)
                else:
                    rest = jnp.sum(each_z[Z - 2 :], axis=0)
                    acc[k, r - 1] = acc[k, r - 1] + jnp.sum(each_z[: Z - 2], axis=0) + jnp.where(last, 0.0, rest)

    def sums_of(b, low_z, rows):
        strain(b, low_z, Z, rows)
        collect(b, low_z, Z, rows)

    turns_of(0, 2, Z)
    products_of(0, 2, Z)
    block = 3 * R * K
    acc[...] = jnp.zeros(acc.shape, jnp.float32)

    @pl.when(first)
    def _():
        drain(ZL, block * 4)
        for c in range(3):
            unpack(he[c], place(1, c, 1, Z - 2))
            unpack(hz[0, c], place(1, c, 1, Z))
        coarsen_block(1, Z - 2, 2)
        coarsen_block(1, Z, 2)
        for c in range(3):
            for r in range(1, R + 1):
                for i in range(2):
                    put(0, c, r, i, get(1, c, r, Z + i, 1)[0])
                    put(1, c, r, Z + 2 + i, get(0, c, r, 2 + i, 1)[0])
        turns_of(1, Z - 2, 4)
        products_of(1, Z - 1, 3)
        local(1, Z - 2)
        sums_of(1, Z - 2, range(2, R))

    @pl.when(ax > 0)
    def _():
        drain(ZL, block * 2)
        for c in range(3):
            unpack(hz[0, c], place(0, c, 1, 0))
        coarsen_block(0, 0, 2)
        turns_of(0, 0, 2)
        products_of(0, 1, 1)

    @pl.when(ax < n_ax - 1)
    def _():
        drain(ZR, block * 2)
        for c in range(3):
            unpack(hz[1, c], place(0, c, 1, Z + 2))
        coarsen_block(0, Z + 2, 2)
        turns_of(0, Z + 2, 2)
        products_of(0, Z + 2, 1)

    local(0, 0)
    sums_of(0, 0, range(2, R))

    def rim_in(side, row):
        line = 3 * K
        pl.when(first)(lambda: drain(ROW + side, line * (Z + 4)))
        pl.when(last)(lambda: drain(ROW + side, line * (Z + 1)))
        pl.when((ax > 0) & (ax < n_ax - 1))(lambda: drain(ROW + side, line * (Z + 2)))
        for c in range(3):
            unpack(hr[side, c], place(0, c, row, -1))

    def edge_out(row, end, to_rad):
        group, slot = (2, EDGE + 1) if row == 1 else (1, EDGE)
        send(hx.at[:, row], hx.at[:, end], group, slot, ax, to_rad)

    def edge_rows(row):
        for c in range(3):
            hx[c, row] = flux[0, pair(c, 1), row - 1, 1 : Z + 1]
        if row == 1:
            pl.when(has_lo)(lambda: edge_out(1, R + 1, rad - 1))
        else:
            pl.when(has_hi)(lambda: edge_out(R, 0, rad + 1))

    def finish(row, beyond):
        strain(0, 0, Z, (row,))
        pl.when(ax < n_ax - 1)(lambda: edge_rows(row))

        @pl.when(first)
        def _():
            outside(1, Z - 2, beyond)
            sums_of(1, Z - 2, (row,))

        outside(0, 0, beyond)
        collect(0, 0, Z, (row,))

    pl.when(has_lo)(lambda: rim_in(0, 0))
    coarsen_below(1, Z + 2)
    pl.when(first)(lambda: coarsen_below(-1, 2))

    @pl.when(rad == 0)
    def _():
        axis_end(0, 1, Z + 2)
        pl.when(first)(lambda: axis_end(1, Z - 1, 2))

    finish(1, 0)
    pl.when(has_hi)(lambda: rim_in(1, R + 1))
    pl.when(rad == n_rad - 1)(wall_end)
    finish(R, R + 1)

    sub_index = lax.broadcasted_iota(jnp.int32, (SUB, LANES), 0)
    lane_index = lax.broadcasted_iota(jnp.int32, (SUB, LANES), 1)
    mine = jnp.zeros((SUB, LANES), jnp.float32)
    for r in range(R):
        for k in range(2):
            row = jnp.sum(acc[k, r], axis=0, keepdims=True) * (2.0 ** -15, 2.0 ** -14)[k]
            mine = jnp.where(sub_index == k * half + r, row, mine)
    mine = jnp.where((lane_index >= pad) & (lane_index < pad + wide), mine, 0.0)
    fold = LANES // 2
    while fold >= LANES // SUB:
        mine = mine + roll(mine, fold, 1)
        fold //= 2
    group = lane_index // (LANES // SUB) == sub_index
    part[...] = jnp.sum(jnp.where(group, mine, 0.0), axis=0, keepdims=True)
    parts[n_ax + ax] = part[...]

    def sums(side, i):
        peer = lax.rem(ax + i, n_ax)
        send(part, parts.at[(1 - side) * n_ax + ax], (0, 1, 2)[side], SUMS + 1 - side, peer, rad + side)

    def sums_in(side, amount):
        pltpu.make_async_copy(parts.at[pl.ds(0, amount)], parts.at[pl.ds(0, amount)], sems.at[SUMS + 1 + side]).wait()

    def first_of(side):
        return 1 if side == 0 else 0

    def send_sums(side):
        start = first_of(side)
        each(n_ax - start, lambda i: sums(side, i + start))

    pl.when(ax > 1)(lambda: hear(0))
    for stage in range(1, len(distances)):
        tell(stage)
        hear(stage)
    send_sums(0)
    pl.when(has_lo)(lambda: send_sums(-1))
    pl.when(has_hi)(lambda: send_sums(1))

    @pl.when(last)
    def _():
        drain(LATE, block * 2)
        for c in range(3):
            unpack(hl[c], place(0, c, 1, Z + 2))
        coarsen_block(0, Z + 2, 2)

        @pl.when(has_lo)
        def _():
            drain(LATE + 1, 3 * K)
            for c in range(3):
                unpack(hc[0, c], place(0, c, 0, Z + 2))

        @pl.when(has_hi)
        def _():
            drain(LATE + 2, 3 * K)
            for c in range(3):
                unpack(hc[1, c], place(0, c, R + 1, Z + 2))

        coarsen_below(Z + 2, 1)
        pl.when(rad == 0)(lambda: axis_end(0, Z + 2, 1))
        for r in range(1, R + 1):
            grads = []
            for c in range(3):
                long = get(0, c, r, Z, 4)
                mid = long[1:-1]
                grads.append([
                    long[2:] - long[:-2],
                    get(0, c, r + 1, Z + 1, 2) - get(0, c, r - 1, Z + 1, 2),
                    up(mid) - down(mid),
                ])
            terms, size = tensor(grads)
            for p in range(6):
                flux[0, p, r - 1, Z : Z + 2] = size * terms[p]

    @pl.when(last)
    def _():
        edge_rows(1)
        edge_rows(R)

    for c in range(3):
        hx[c, 2:R] = flux[0, pair(c, 1), 1 : R - 1, 1 : Z + 1]

    @pl.when(rad == 0)
    def _():
        for c in range(3):
            for z in range(Z):
                hx[c, 0, z] = SIGNS[c] * SIGNS[1] * roll(hx[c, 1, z], half, 0)

    @pl.when(rad == n_rad - 1)
    def _():
        for c in range(3):
            for z in range(Z):
                hx[c, R + 1, z] = jnp.zeros((SUB, LANES), jnp.float32)

    def lay(slot, x):
        base = slot * Z * SUB
        for z in range(Z):
            res[base + z * SUB : base + (z + 1) * SUB, :] = x[z]
        pieces = [res[pl.ds(base + s, Z, stride=SUB), :] for s in range(SUB)]
        for k, tile in enumerate(joined(pieces, wide, pad)):
            flat[slot, :, k * LANES : (k + 1) * LANES] = tile

    def slot_of(kind, c, r):
        return (kind * 3 + c) * (R + 2) + r

    for r in range(1, R + 1):
        for c in range(3):
            axial = get(0, c, r, 1, Z + 2) * get(0, 0, r, 1, Z + 2)
            outer = get(0, c, r + 1, 2, Z) * get(0, 1, r + 1, 2, Z)
            inner = get(0, c, r - 1, 2, Z) * get(0, 1, r - 1, 2, Z)
            mid = get(0, c, r, 2, Z)
            spin = mid * get(0, 2, r, 2, Z)
            change = axial[2:] - axial[:-2] + (outer - inner) + (up(spin) - down(spin))
            lay(slot_of(0, c, r), mid - 0.5 * change)
            turn = flux[0, pair(c, 2), r - 1, 1 : Z + 1]
            p = pair(c, 0)
            along = flux[0, p, r - 1, 2 : Z + 2] - flux[0, p, r - 1, 0:Z]
            lay(slot_of(1, c, r), along + (up(turn) - down(turn)))
            lay(slot_of(2, c, r), hx[c, r])

    count = n_ax * Z * T
    def coefficients(total):
        total = jnp.broadcast_to(jnp.sum(jnp.where(group, total, 0.0), axis=1, keepdims=True), (SUB, LANES)) / count
        return 0.125 * (total / (roll(total, -half, 0) + EPSILON))

    def total_of(side):
        terms = parts[pl.ds((1 + side) * n_ax, n_ax)]
        while terms.shape[0] % 2 == 0:
            terms = terms[: terms.shape[0] // 2] + terms[terms.shape[0] // 2 :]
        return jnp.sum(terms, axis=0)

    def spread_row(x):
        return jnp.broadcast_to(x, (Z, LANES))

    pl.when(has_lo)(lambda: drain(EDGE, 3 * Z * SUB))
    pl.when(has_hi)(lambda: drain(EDGE + 1, 3 * Z * SUB))
    for c in range(3):
        for r in (0, R + 1):
            lay(slot_of(2, c, r), hx[c, r])
    sums_in(0, n_ax - 1)
    pl.when(has_lo)(lambda: sums_in(-1, n_ax))
    pl.when(has_hi)(lambda: sums_in(1, n_ax))
    lower, coef, higher = [coefficients(total_of(side)) for side in (-1, 0, 1)]
    by_row = [spread_row(jnp.where(rad == 0, coef[0:1], lower[R - 1 : R]))]
    by_row = by_row + [spread_row(coef[r : r + 1]) for r in range(R)]
    by_row = by_row + [spread_row(jnp.where(rad == n_rad - 1, 0.0, higher[0:1]))]
    for c in range(3):
        for r in range(1, R + 1):
            for k in range(K):
                lanes = slice(k * LANES, (k + 1) * LANES)
                base, turn, outer, inner = [
                    flat[slot_of(*at), :, lanes] for at in ((0, c, r), (1, c, r), (2, c, r + 1), (2, c, r - 1))]
                out_ref[c, r - 1, :, lanes] = base + by_row[r] * turn + (by_row[r + 1] * outer - by_row[r - 1] * inner)

    line, total = 3 * K, n_ax - 1
    pl.when(ax < n_ax - 2)(lambda: drain(SEND, 4 * block + total))
    pl.when(last)(lambda: drain(SEND, (4 + near) * block + total))
    pl.when(second)(lambda: drain(SEND, (4 + far) * block + total))

    def sent(group):
        usual = line * (Z + 2) + 3 * Z * SUB + n_ax
        pl.when(ax < n_ax - 1)(lambda: drain(SEND + group, usual))
        pl.when(last)(lambda: drain(SEND + group, usual + 2 * line))

    pl.when(has_hi)(lambda: sent(1))
    pl.when(has_lo)(lambda: sent(2))


def shards(n_ax, n_rad, velocity, cycle_map):
    _, R, Z, T = velocity.shape
    assert n_ax >= 8 and R >= NRING and Z >= 3

    def vmem(*shape):
        return pltpu.VMEM(shape, jnp.float32)

    return pl.pallas_call(
        functools.partial(kernel, n_ax, n_rad),
        out_shape=jax.ShapeDtypeStruct(velocity.shape, velocity.dtype),
        in_specs=[pl.BlockSpec(memory_space=pltpu.HBM)] * 2,
        out_specs=pl.BlockSpec(memory_space=pltpu.VMEM),
        scratch_shapes=[
            vmem(*velocity.shape),
            pltpu.VMEM(cycle_map.shape, jnp.int32),
            vmem(NRING * SUB, LANES),
            vmem(NRING, 2 * (MOSTSEG - 1).bit_length() + 1, SUB, LANES),
            vmem(3 * R * (Z + 10) * SUB, LANES),
            vmem(3 * 2 * (Z + 4) * SUB, LANES),
            vmem(2, 3, 2 * R, T),
            vmem(3, 2 * R, T),
            vmem(2, 3, Z + 4, T),
            vmem(3, 2 * R, T),
            vmem(2, 3, 1, T),
            vmem(2, 3, R + 2, Z + 2, SUB, LANES),
            vmem(2, 6, R, Z, SUB, LANES),
            vmem(3, R, Z + 6, SUB, LANES),
            vmem(3, R, Z + 6, SUB, LANES),
            vmem(6, R, Z + 6, SUB, LANES),
            vmem(2, 6, R, Z + 2, SUB, LANES),
            vmem(3, R + 2, Z, SUB, LANES),
            vmem(9 * (R + 2) * Z * SUB, LANES),
            vmem(9 * (R + 2), Z, T),
            vmem(2, R, SUB, LANES),
            vmem(1, LANES),
            vmem(3 * n_ax, 1, LANES),
            vmem(3 * (R * 6 + Z) * SUB * (T // LANES) + 2 * n_ax, LANES),
            pltpu.SemaphoreType.REGULAR((len(stages(n_ax)),)),
            pltpu.SemaphoreType.DMA((SEMS,)),
        ],
        compiler_params=pltpu.CompilerParams(collective_id=0, has_side_effects=True, vmem_limit_bytes=8 << 20),
    )(*(pltpu.with_memory_space_constraint(x, pltpu.HBM) for x in (velocity, cycle_map)))


def solution(mesh):
    n_ax, n_rad = mesh.shape["ax"], mesh.shape["rad"]
    spec = P(None, "rad", "ax", None)
    body = functools.partial(shards, n_ax, n_rad)
    return jax.shard_map(body, mesh=mesh, in_specs=(spec, P()), out_specs=spec, check_vma=False)
```
